256 devices in a mesh: sec: 2 (over core), grp: 128 (over y, z, x).
Axes of the slice: x: 4, y: 4, z: 8, core: 2. Of those that a mesh axis runs over, the one named last changes fastest.
Arguments:
- stratum_warmth_anomaly: float32 [90, 65536], P('sec', 'grp'), may hold values from 0.7 to 1.3
- pressure_depth: float32 [90, 65536], P('sec', 'grp'), may hold values from 0.5 to 2
- absorber_amounts: float32 [4, 90, 65536], P(None, 'sec', 'grp'), may hold values from 0.1 to 1
- ground_warmth_anomaly: float32 [65536], P('grp'), may hold values from 0.9 to 1.3
- sun_elevation_factor: float32 [65536], P('grp'), may hold values from 0.2 to 1
- daytime_mask: int32 [65536], P('grp'), may hold values 0 or 1
- dispatch_position: int32 [128, 512], P('grp'), may hold values from 0 to 511, each once within a row
- arrival_membership: int32 [128, 512], P('grp'), may hold values from 0 to 511, each once within a row
- adjacency_table: int32 [6, 65536], P(None, 'grp'), may hold values from 0 to 639, as said below
- blending_coefficient: float32 [6, 65536], P(None, 'grp'), may hold values from 0.02 to 0.15
- opacity_table: float32 [4, 112, 90], P(None, 'sec'), may hold values from 0.001 to 0.3
- emission_share: float32 [112], P('sec'), may hold values from 0.05 to 0.5
- sunshine_share: float32 [112], P('sec'), may hold values from 0.05 to 0.5
Outputs:
- heating: float32 [90, 65536], P('sec', 'grp')
- mixed: float32 [4, 90, 65536], P(None, 'sec', 'grp')
The draws below stay inside these ranges and needn't reach their ends.
Inputs may be any that keep to these rules, and one draw needn't show every extreme that they name: `dispatch_position`: each row is a permutation of 0 to 511. `arrival_membership`: each row is a permutation of 0 to 511, so every radiation column has exactly four members. adjacency_table[k, c] - (c mod 512) lies in 0 to 128.
All inputs are finite; a program needn't handle non-finite values. No bound on the sum of `daytime_mask` on one device may be relied on, other than what follows from the above.
Results may differ from the reference program's by a relative error of at most 0.0003.
Values sent between devices are 32-bit elements; how exact they have to be, the bound alone decides.
No kernel may reach another device: no remote copies, remote signals or barrier semaphores. Data moves between devices by JAX's collectives and lax.ppermute only.
A program may use at most 64 MiB of HBM per device.

```python
import math
import jax
import jax.numpy as jnp
from jax import lax

COL_DEV = 512
LAYER_TALLY = 90
GPTS = 112
SPECIES = 4
NEAR_COUNT = 6
STEPS = 4
LEVEL_BLOCK = 9
HALO = 64
GRID_CELL_TALLY = 65536
N_GRP = 128


def draw_adjacency_table(key, part):
    local_ids = jnp.arange(GRID_CELL_TALLY, dtype=jnp.int32) % COL_DEV
    offsets = jax.random.randint(key, (NEAR_COUNT, GRID_CELL_TALLY), -HALO, HALO + 1, dtype=jnp.int32)
    row_ids = jnp.arange(NEAR_COUNT, dtype=jnp.int32)[:, None]
    offsets = jnp.where((row_ids == 0) & (local_ids[None, :] == COL_DEV - 1), HALO, offsets)
    offsets = jnp.where((row_ids == 1) & (local_ids[None, :] == 0), -HALO, offsets)
    return local_ids[None, :] + HALO + offsets


def with_ends(result, own_key, low, high):
    shape = result.shape
    spot = [jax.random.randint(jax.random.fold_in(own_key, axis), (), 0, shape[axis]) for axis in range(len(shape))]
    result = result.at[tuple(spot)].set(low)
    longest = shape.index(max(shape))
    spot[longest] = (spot[longest] + 1) % shape[longest]
    return result.at[tuple(spot)].set(high)


def shard_levels(own_key, shape, cuts, least, largest):
    level, own = 1.0, jax.random.fold_in(own_key, 6)
    for dim, parts in cuts:
        steps = jnp.exp(jax.random.uniform(jax.random.fold_in(own, dim), (parts,), jnp.float32, least / len(cuts), largest / len(cuts)))
        level = level * jnp.repeat(steps, shape[dim] // parts).reshape([-1 if axis == dim else 1 for axis in range(len(shape))])
    return level


def setup_inputs(seed: int = 0) -> dict:
    key_list = jax.random.split(jax.random.key(seed), 14)
    stratum_warmth_anomaly = jnp.clip(0.7 + 0.59999996 * jax.random.uniform(key_list[0], (LAYER_TALLY, GRID_CELL_TALLY), jnp.float32) ** shard_levels(key_list[0], (LAYER_TALLY, GRID_CELL_TALLY), ((0, 2), (1, 128)), -0.2, 0.2), 0.7, 1.3)
    pressure_depth = jnp.clip(0.5 + 1.5 * jax.random.uniform(key_list[1], (LAYER_TALLY, GRID_CELL_TALLY), jnp.float32) ** shard_levels(key_list[1], (LAYER_TALLY, GRID_CELL_TALLY), ((0, 2), (1, 128)), -0.2, 0.2), 0.5, 2.0)
    absorber_amounts = jnp.clip(jnp.exp(math.log(1.0) - 2.3025851 * jax.random.uniform(key_list[2], (SPECIES, LAYER_TALLY, GRID_CELL_TALLY), jnp.float32) ** shard_levels(key_list[2], (SPECIES, LAYER_TALLY, GRID_CELL_TALLY), ((1, 2), (2, 128)), -0.2, 0.2)), 0.1, 1.0)
    ground_warmth_anomaly = jnp.clip(0.9 + 0.39999998 * jax.random.uniform(key_list[3], (GRID_CELL_TALLY,), jnp.float32) ** shard_levels(key_list[3], (GRID_CELL_TALLY,), ((0, 128),), -0.2, 0.2), 0.9, 1.3)
    sun_elevation_factor = jnp.clip(0.2 + 0.8 * jax.random.uniform(key_list[4], (GRID_CELL_TALLY,), jnp.float32) ** shard_levels(key_list[4], (GRID_CELL_TALLY,), ((0, 128),), -0.2, 0.2), 0.2, 1.0)
    daytime_mask = with_ends((jax.random.randint(key_list[5], (GRID_CELL_TALLY,), 0, 2) < 1).astype(jnp.int32), jax.random.fold_in(key_list[5], 1), 0, 1)
    dispatch_position = jax.vmap(lambda own: jax.random.permutation(own, COL_DEV))(jax.random.split(key_list[6], N_GRP)).reshape((N_GRP, COL_DEV)).astype(jnp.int32)
    arrival_membership = jax.vmap(lambda own: jax.random.permutation(own, COL_DEV))(jax.random.split(key_list[7], N_GRP)).reshape((N_GRP, COL_DEV)).astype(jnp.int32)
    adjacency_table = draw_adjacency_table(jax.random.fold_in(key_list[13], 71), 0)
    blending_coefficient = jnp.clip(jnp.exp(math.log(0.15) - 2.014903 * jax.random.uniform(key_list[9], (NEAR_COUNT, GRID_CELL_TALLY), jnp.float32) ** shard_levels(key_list[9], (NEAR_COUNT, GRID_CELL_TALLY), ((1, 128),), -0.2, 0.2)), 0.02, 0.15)
    opacity_table = jnp.clip(jnp.exp(math.log(0.3) - 5.7037825 * jax.random.uniform(key_list[10], (SPECIES, GPTS, LAYER_TALLY), jnp.float32) ** shard_levels(key_list[10], (SPECIES, GPTS, LAYER_TALLY), ((1, 2),), -0.2, 0.2)), 0.001, 0.3)
    emission_share = jnp.clip(jnp.exp(math.log(0.5) - 2.3025851 * jax.random.uniform(key_list[11], (GPTS,), jnp.float32) ** shard_levels(key_list[11], (GPTS,), ((0, 2),), -0.2, 0.2)), 0.05, 0.5)
    sunshine_share = jnp.clip(jnp.exp(math.log(0.5) - 2.3025851 * jax.random.uniform(key_list[12], (GPTS,), jnp.float32) ** shard_levels(key_list[12], (GPTS,), ((0, 2),), -0.2, 0.2)), 0.05, 0.5)
    return {"stratum_warmth_anomaly": stratum_warmth_anomaly, "pressure_depth": pressure_depth, "absorber_amounts": absorber_amounts, "ground_warmth_anomaly": ground_warmth_anomaly, "sun_elevation_factor": sun_elevation_factor, "daytime_mask": daytime_mask, "dispatch_position": dispatch_position, "arrival_membership": arrival_membership, "adjacency_table": adjacency_table, "blending_coefficient": blending_coefficient, "opacity_table": opacity_table, "emission_share": emission_share, "sunshine_share": sunshine_share}


DIFFUSE = 1.66


def optical(opacity_table, radiant_species, stratum_index):
    coeffs = lax.dynamic_index_in_dim(opacity_table, stratum_index, 2, keepdims=False)
    amounts = lax.dynamic_index_in_dim(radiant_species, stratum_index, 1, keepdims=False)
    optical_depth = coeffs[0][:, None] * amounts[0][None, :]
    for species in range(1, coeffs.shape[0]):
        optical_depth = optical_depth + coeffs[species][:, None] * amounts[species][None, :]
    return optical_depth


def compute_flux_heating(radiant_warmth, radiant_depth, radiant_species, radiant_ground, sunlight_incline, incoming_sunshine, opacity_table, emission_share, sunshine_share):
    strata_range, radiant_span = radiant_warmth.shape
    blocks = strata_range // LEVEL_BLOCK
    gpoints = emission_share.shape[0]
    block_ids = jnp.arange(blocks, dtype=jnp.int32)

    def layer_terms(stratum_index):
        optical_depth = optical(opacity_table, radiant_species, stratum_index)
        stratum_warmth = lax.dynamic_index_in_dim(radiant_warmth, stratum_index, 0, keepdims=False)
        source = emission_share[:, None] * (stratum_warmth ** 4)[None, :]
        return optical_depth, jnp.exp(-DIFFUSE * optical_depth), source

    def down_block(fluxes, block_id):
        thermal, direct = fluxes
        thermal_rows = []
        direct_rows = []
        for inner_id in range(LEVEL_BLOCK):
            optical_depth, transmit, source = layer_terms(block_id * LEVEL_BLOCK + inner_id)
            thermal = transmit * thermal + (1.0 - transmit) * source
            direct = direct * jnp.exp(-optical_depth / sunlight_incline[None, :])
            thermal_rows.append(jnp.sum(thermal, axis=0))
            direct_rows.append(jnp.sum(direct, axis=0))
        return (thermal, direct), (jnp.stack(thermal_rows), jnp.stack(direct_rows))

    down_init = (jnp.zeros((gpoints, radiant_span), jnp.float32), sunshine_share[:, None] * incoming_sunshine[None, :])
    final_down, (down_rows, direct_rows) = lax.scan(down_block, down_init, block_ids)
    thermal_down = jnp.concatenate([jnp.zeros((1, radiant_span), jnp.float32), down_rows.reshape(strata_range, radiant_span)], axis=0)
    direct_down = jnp.concatenate([jnp.sum(down_init[1], axis=0)[None], direct_rows.reshape(strata_range, radiant_span)], axis=0)

    def up_block(upward, block_id):
        upward_rows = []
        for inner_id in range(LEVEL_BLOCK - 1, -1, -1):
            optical_depth, transmit, source = layer_terms(block_id * LEVEL_BLOCK + inner_id)
            upward = transmit * upward + (1.0 - transmit) * source
            upward_rows.append(jnp.sum(upward, axis=0))
        return upward, jnp.stack(upward_rows[::-1])

    up_init = emission_share[:, None] * (radiant_ground ** 4)[None, :]
    final_up, up_rows = lax.scan(up_block, up_init, block_ids, reverse=True)
    upward_flux = jnp.concatenate([up_rows.reshape(strata_range, radiant_span), jnp.sum(up_init, axis=0)[None]], axis=0)
    net_flux = thermal_down - upward_flux + direct_down
    return (net_flux[:-1] - net_flux[1:]) / radiant_depth


def reference(stratum_warmth_anomaly, pressure_depth, absorber_amounts, ground_warmth_anomaly, sun_elevation_factor, daytime_mask, dispatch_position, arrival_membership, adjacency_table, blending_coefficient, opacity_table, emission_share, sunshine_share):
    overall_summation = stratum_warmth_anomaly.shape[1]
    cell_sequence = dispatch_position.shape[1]
    per_peer = cell_sequence // dispatch_position.shape[0]
    groups_dev = cell_sequence // 4
    rad_total = overall_summation // 4
    column_ids = jnp.arange(overall_summation, dtype=jnp.int32)
    source_dev = column_ids // cell_sequence
    position = dispatch_position.reshape(-1).astype(jnp.int32)
    target = position // per_peer
    received = source_dev * per_peer + position % per_peer
    rad_ids = (target * groups_dev + arrival_membership[target, received] // 4).astype(jnp.int32)

    def average_quantity(quantity):
        moved = jnp.moveaxis(quantity, -1, 0)
        summed = jax.ops.segment_sum(moved, rad_ids, num_segments=rad_total)
        return jnp.moveaxis(summed, 0, -1) * 0.25

    radiant_warmth = average_quantity(stratum_warmth_anomaly)
    radiant_depth = average_quantity(pressure_depth)
    radiant_species = average_quantity(absorber_amounts)
    radiant_ground = average_quantity(ground_warmth_anomaly)
    sunlight_incline = average_quantity(sun_elevation_factor)
    incoming_sunshine = average_quantity(daytime_mask.astype(jnp.float32) * sun_elevation_factor)
    radiant_heating = compute_flux_heating(radiant_warmth, radiant_depth, radiant_species, radiant_ground, sunlight_incline, incoming_sunshine, opacity_table, emission_share, sunshine_share)
    heating = jnp.take(radiant_heating, rad_ids, axis=1)

    base_ids = source_dev * cell_sequence - HALO
    mixed = absorber_amounts
    for step_id in range(STEPS):
        update = jnp.zeros_like(mixed)
        for near_id in range(adjacency_table.shape[0]):
            source_ids = ((base_ids + adjacency_table[near_id]) % overall_summation).astype(jnp.int32)
            update = update + blending_coefficient[near_id] * (jnp.take(mixed, source_ids, axis=2) - mixed)
        mixed = mixed + update
    return heating, mixed
```

```python
import functools
import math

import jax
import jax.numpy as jnp
from jax import lax
from jax.experimental import pallas as pl
from jax.experimental.pallas import tpu as pltpu
from jax.sharding import PartitionSpec as P

STEPS = 4
HALO = 64
DIFFUSE = 1.66
LOG2E = math.log2(math.e)
BF = jnp.bfloat16
F32 = jnp.float32

PEERS = 128
SLOTS = 4
COLS = 512
LEV = 45
ROW = 48
FIELDS = 6
FEAT = ROW * FIELDS
CHUNK = SLOTS * FEAT // 128
RAD = 128
GH = 56
REACH = STEPS * HALO
WIDE = COLS + 2 * REACH
SPECIES = 4
NEAR = 6
UNROLL = 9
NT = (((1,), (1,)), ((), ()))
NN = (((1,), (0,)), ((), ()))


def split(x):
    hi = x.astype(BF)
    return hi, (x - hi.astype(F32)).astype(BF)


def dot(a, b, dims):
    return lax.dot_general(a, b, dims, preferred_element_type=F32)


def slot_matrix(position):
    rows = lax.broadcasted_iota(jnp.int32, (COLS, COLS), 0)
    slot = (rows & (PEERS - 1)) * SLOTS + (rows >> 7)
    return jnp.where(slot == position, 1.0, 0.0).astype(BF)


def pack_kernel(temp, thick, tracers, ground, sun, day, pos, adj, coef, send, right, left, table, bundle):
    fields = [temp[...], thick[...]] + [tracers[s] for s in range(SPECIES)]
    for k, field in enumerate(fields):
        bundle[k * ROW : k * ROW + LEV, :] = field
        if k:
            bundle[k * ROW + LEV : (k + 1) * ROW, :] = jnp.zeros((ROW - LEV, COLS), F32)
    sunny = sun[...]
    bundle[LEV : LEV + 1, :] = ground[...]
    bundle[LEV + 1 : LEV + 2, :] = sunny
    bundle[LEV + 2 : LEV + 3, :] = day[...].astype(F32) * sunny
    tail = bundle[256:288, :]
    for k in range(1, 4):
        bundle[256 + 32 * k : 288 + 32 * k, :] = tail
    placing = slot_matrix(pos[...])
    hi, lo = split(bundle[...])
    packed = dot(placing, hi, NT) + dot(placing, lo, NT)
    lane = lax.broadcasted_iota(jnp.int32, (PEERS, 128), 1) >> 5
    last = jnp.zeros((PEERS, 128), F32)
    for m in range(SLOTS):
        block = packed[m * PEERS : (m + 1) * PEERS, :]
        send[pl.ds(2 * m, PEERS, CHUNK), :] = block[:, 0:128]
        send[pl.ds(2 * m + 1, PEERS, CHUNK), :] = block[:, 128:256]
        last = jnp.where(lane == m, block[:, 256:384], last)
    send[pl.ds(CHUNK - 1, PEERS, CHUNK), :] = last
    body = SPECIES * ROW
    right[0:body, :] = bundle[2 * ROW : FEAT, COLS - REACH :]
    left[0:body, :] = bundle[2 * ROW : FEAT, :REACH]
    column = lax.broadcasted_iota(jnp.int32, (NEAR, COLS), 1)
    reach = (adj[...] - column).astype(F32)
    pad = jnp.zeros((2, COLS), F32)
    both = jnp.concatenate([reach, pad, coef[...], pad], axis=0)
    table[...] = both
    right[body : body + 16, :] = both[:, COLS - REACH :]
    left[body : body + 16, :] = both[:, :REACH]


def pool_kernel(arrived, member, pooled, stage):
    ids = member[...] >> 2
    rows = lax.broadcasted_iota(jnp.int32, (RAD, 128), 0)
    lane = lax.broadcasted_iota(jnp.int32, (PEERS, 128), 1) >> 5
    last = arrived[pl.ds(CHUNK - 1, PEERS, CHUNK), :]
    chosen = []
    for m in range(SLOTS):
        chosen.append(jnp.where(rows == ids[m : m + 1, :], 0.25, 0.0).astype(BF))
        span = slice(m * PEERS, (m + 1) * PEERS)
        stage[span, 0:128] = arrived[pl.ds(2 * m, PEERS, CHUNK), :]
        stage[span, 128:256] = arrived[pl.ds(2 * m + 1, PEERS, CHUNK), :]
        stage[span, 256:384] = jnp.where(lane == m, last, 0.0)
    selector = jnp.concatenate(chosen, axis=1)
    hi, lo = split(stage[...])
    total = dot(selector, hi, NN) + dot(selector, lo, NN)
    pooled[0:128, :] = total[:, 0:128].T
    pooled[128:256, :] = total[:, 128:256].T
    tail = total[:, 256:384].T
    pooled[256:288, :] = tail[0:32] + tail[32:64] + tail[64:96] + tail[96:128]


def flux_kernel(side, own, other, opacity, emission, sunshine, mine, theirs, fields, warm, kept, sums, net):
    me = side[0]
    fields[pl.ds(me, 1)] = own[...][None]
    fields[pl.ds(1 - me, 1)] = other[...][None]
    for h in range(2):
        warm[h] = jnp.square(jnp.square(fields[h, 0:ROW, :]))
        fields[h, 2 * ROW : FEAT, :] = fields[h, 2 * ROW : FEAT, :] * (-DIFFUSE * LOG2E)
    surface = own[40:48, :]
    ground4 = jnp.square(jnp.square(surface[5:6, :]))
    slant = 1.0 / (DIFFUSE * surface[6:7, :])
    slant = jnp.broadcast_to(slant, (GH, RAD))
    insolation = surface[7:8, :]
    emit = jnp.broadcast_to(emission[...], (GH, RAD))

    def fold(x):
        return jnp.sum(x.reshape(GH // 8, 8, RAD), axis=0)

    def down(h, block, carry):
        thermal, direct = carry
        start = h * LEV + block * UNROLL
        shift = lax.rem(128 - start, 128)
        coeffs = [pltpu.roll(opacity[s], shift, 1) for s in range(SPECIES)]
        for i in range(UNROLL):
            inner = block * UNROLL + i
            tau = None
            for s in range(SPECIES):
                amount = fields[h, pl.ds((2 + s) * ROW + inner, 1), :]
                term = jnp.broadcast_to(coeffs[s][:, i : i + 1], (GH, RAD)) * amount
                tau = term if tau is None else tau + term
            opaque = 1.0 - jnp.exp2(tau)
            kept[start + i] = opaque
            source = emit * warm[h, pl.ds(inner, 1), :]
            gain = opaque * (thermal - source)
            thermal = thermal - gain
            passed = direct * jnp.exp2(tau * slant)
            sums[pl.ds(8 * (start + i), 8), :] = fold(gain + (direct - passed))
            direct = passed
        return thermal, direct

    def up(h, block, upward):
        start = h * LEV + block * UNROLL
        for i in range(UNROLL - 1, -1, -1):
            source = emit * warm[h, pl.ds(block * UNROLL + i, 1), :]
            gain = kept[start + i] * (upward - source)
            upward = upward - gain
            rows = pl.ds(8 * (start + i), 8)
            sums[rows, :] = sums[rows, :] + fold(gain)
        return upward

    blocks = LEV // UNROLL
    carry = (jnp.zeros((GH, RAD), F32), sunshine[...] * insolation)
    for h in range(2):
        carry = lax.fori_loop(0, blocks, functools.partial(down, h), carry)
    upward = emit * ground4
    for h in (1, 0):
        upward = lax.fori_loop(0, blocks, lambda b, u, h=h: up(h, blocks - 1 - b, u), upward)
    for h in range(2):
        total = None
        for k in range(8):
            part = sums[pl.ds(8 * LEV * h + k, LEV, 8), :]
            total = part if total is None else total + part
        net[h, 0:LEV, :] = total
        net[h, LEV:ROW, :] = jnp.zeros((ROW - LEV, RAD), F32)
    mine[...] = net[pl.ds(me, 1)][0]
    theirs[...] = net[pl.ds(1 - me, 1)][0]


def spread_kernel(mine, gotten, own, member, send):
    heat = (mine[...] + gotten[...]) / own[ROW : 2 * ROW, :]
    rows = lax.broadcasted_iota(jnp.int32, (ROW, RAD), 0)
    heat = jnp.where(rows < LEV, heat, 0.0)
    gap = jnp.zeros((16, RAD), F32)
    hi, lo = split(jnp.concatenate([heat, gap, heat, gap], axis=0))
    ids = member[...] >> 2
    lanes = lax.broadcasted_iota(jnp.int32, (PEERS, RAD), 1)
    for h in range(2):
        parts = []
        for m in (2 * h, 2 * h + 1):
            selector = jnp.where(lanes == ids[:, m : m + 1], 1.0, 0.0).astype(BF)
            parts.append(dot(selector, hi, NT) + dot(selector, lo, NT))
        send[pl.ds(h, PEERS, 2), :] = jnp.where(lanes < 64, parts[0], parts[1])


def unplace_kernel(returned, pos, heating):
    parts = []
    for h in range(2):
        turned = returned[pl.ds(h, PEERS, 2), :].T
        parts += [turned[0:ROW, :], turned[64 : 64 + ROW, :]]
    hi, lo = split(jnp.concatenate(parts, axis=1))
    placing = slot_matrix(pos[...])
    heating[...] = (dot(hi, placing, NN) + dot(lo, placing, NN))[0:LEV, :]


def mix_kernel(tracers, table, from_left, from_right, mixed, high, low, band):
    body = SPECIES * ROW
    hi, lo = split(from_left[0:body, :])
    high[0, :, 0:REACH] = hi
    low[0, :, 0:REACH] = lo
    hi, lo = split(from_right[0:body, :])
    high[0, :, REACH + COLS :] = hi
    low[0, :, REACH + COLS :] = lo
    for s in range(SPECIES):
        fill = jnp.concatenate([tracers[s], jnp.zeros((ROW - LEV, COLS), F32)], axis=0)
        hi, lo = split(fill)
        high[0, s * ROW : (s + 1) * ROW, REACH : REACH + COLS] = hi
        low[0, s * ROW : (s + 1) * ROW, REACH : REACH + COLS] = lo
    tables = jnp.concatenate([from_left[body:, :], table[...], from_right[body:, :]], axis=1)
    shifted = pltpu.roll(tables, WIDE - HALO, 1)
    rows = lax.broadcasted_iota(jnp.int32, (256, 128), 0).astype(F32)
    lanes = lax.broadcasted_iota(jnp.int32, (1, 128), 1).astype(F32)

    def build(source, k):
        part = source[:, k * 128 : (k + 1) * 128]
        blend = jnp.where(rows == lanes + HALO, 1.0 - jnp.sum(part[8:14, :], axis=0, keepdims=True), 0.0)
        for n in range(NEAR):
            blend = blend + jnp.where(rows == lanes + part[n : n + 1, :], part[8 + n : 9 + n, :], 0.0)
        return split(blend)

    for k in range(7):
        hi, lo = build(shifted, k)
        band[0, 0, k] = hi
        band[0, 1, k] = lo
    for k in range(6):
        hi, lo = build(tables, k + 1)
        band[1, 0, k] = hi
        band[1, 1, k] = lo
    for step in range(STEPS):
        now, later = step % 2, (step + 1) % 2
        tiles = 7 - step
        first = step // 2
        for k in range(tiles):
            window = slice(k * 128, k * 128 + 256)
            bh, bl = band[now, 0, k + first], band[now, 1, k + first]
            xh, xl = high[now, :, window], low[now, :, window]
            new = dot(xh, bh, NN) + (dot(xh, bl, NN) + dot(xl, bh, NN))
            if step < STEPS - 1:
                hi, lo = split(new)
                high[later, :, k * 128 : (k + 1) * 128] = hi
                low[later, :, k * 128 : (k + 1) * 128] = lo
            else:
                for s in range(SPECIES):
                    mixed[s, :, k * 128 : (k + 1) * 128] = new[s * ROW : s * ROW + LEV, :]


def shape(*dims):
    return jax.ShapeDtypeStruct(dims, F32)


def per_device(
    stratum_warmth_anomaly,
    pressure_depth,
    absorber_amounts,
    ground_warmth_anomaly,
    sun_elevation_factor,
    daytime_mask,
    dispatch_position,
    arrival_membership,
    adjacency_table,
    blending_coefficient,
    opacity_table,
    emission_share,
    sunshine_share,
):
    n = lax.axis_size("grp")
    up = [(i, (i + 1) % n) for i in range(n)]
    down = [(j, i) for i, j in up]
    swap = [(0, 1), (1, 0)]
    halo_rows = SPECIES * ROW + 16

    send, right, left, table = pl.pallas_call(
        pack_kernel,
        out_shape=(shape(PEERS * CHUNK, 128), shape(halo_rows, REACH), shape(halo_rows, REACH), shape(16, COLS)),
        scratch_shapes=[pltpu.VMEM((384, COLS), F32)],
        name="pack",
    )(
        stratum_warmth_anomaly,
        pressure_depth,
        absorber_amounts,
        ground_warmth_anomaly[None],
        sun_elevation_factor[None],
        daytime_mask[None],
        dispatch_position,
        adjacency_table,
        blending_coefficient,
    )
    from_left = lax.ppermute(right, "grp", up)
    from_right = lax.ppermute(left, "grp", down)
    arrived = lax.all_to_all(
        send.reshape(PEERS * CHUNK, 1, 128), "grp", split_axis=0, concat_axis=0, tiled=True
    ).reshape(PEERS * CHUNK, 128)

    mixed = pl.pallas_call(
        mix_kernel,
        out_shape=shape(SPECIES, LEV, COLS),
        scratch_shapes=[
            pltpu.VMEM((2, SPECIES * ROW, WIDE), BF),
            pltpu.VMEM((2, SPECIES * ROW, WIDE), BF),
            pltpu.VMEM((2, 2, 7, 256, 128), BF),
        ],
        name="mix",
    )(absorber_amounts, table, from_left, from_right)

    members = arrival_membership.reshape(PEERS, SLOTS)
    pooled = pl.pallas_call(
        pool_kernel,
        out_shape=shape(FEAT, RAD),
        scratch_shapes=[pltpu.VMEM((COLS, 384), F32)],
        name="pool",
    )(arrived, members.T)
    other = lax.ppermute(pooled, "sec", swap)
    side = lax.axis_index("sec").astype(jnp.int32)[None]
    opacity = jnp.pad(opacity_table, ((0, 0), (0, 0), (0, 128 - 2 * LEV)))
    mine, theirs = pl.pallas_call(
        flux_kernel,
        out_shape=(shape(ROW, RAD), shape(ROW, RAD)),
        in_specs=[pl.BlockSpec(memory_space=pltpu.SMEM)] + [pl.BlockSpec(memory_space=pltpu.VMEM)] * 5,
        scratch_shapes=[
            pltpu.VMEM((2, FEAT, RAD), F32),
            pltpu.VMEM((2, ROW, RAD), F32),
            pltpu.VMEM((2 * LEV, GH, RAD), F32),
            pltpu.VMEM((2 * LEV * 8, RAD), F32),
            pltpu.VMEM((2, ROW, RAD), F32),
        ],
        name="flux",
    )(side, pooled, other, opacity, emission_share[:, None], sunshine_share[:, None])
    gotten = lax.ppermute(theirs, "sec", swap)
    back = pl.pallas_call(spread_kernel, out_shape=shape(PEERS * 2, 128), name="spread")(
        mine, gotten, pooled, members
    )
    returned = lax.all_to_all(
        back.reshape(PEERS * 2, 1, 128), "grp", split_axis=0, concat_axis=0, tiled=True
    ).reshape(PEERS * 2, 128)
    heating = pl.pallas_call(unplace_kernel, out_shape=shape(LEV, COLS), name="unplace")(
        returned, dispatch_position
    )
    return (heating, mixed)


def solution(mesh):
    in_specs = (
        P("sec", "grp"),
        P("sec", "grp"),
        P(None, "sec", "grp"),
        P("grp"),
        P("grp"),
        P("grp"),
        P("grp", None),
        P("grp", None),
        P(None, "grp"),
        P(None, "grp"),
        P(None, "sec", None),
        P("sec"),
        P("sec"),
    )
    out_specs = (P("sec", "grp"), P(None, "sec", "grp"))
    return jax.shard_map(
        per_device, mesh=mesh, in_specs=in_specs, out_specs=out_specs, check_vma=False
    )
```

```python
import functools
import math

import jax
import jax.numpy as jnp
from jax import lax
from jax.experimental import pallas as pl
from jax.experimental.pallas import tpu as pltpu
from jax.sharding import PartitionSpec as P

STEPS = 4
HALO = 64
DIFFUSE = 1.66
LOG2E = math.log2(math.e)
BF = jnp.bfloat16
F32 = jnp.float32

PEERS = 128
SLOTS = 4
COLS = 512
LEV = 45
ROW = 48
BASE = 2 * ROW
BODY = 192
FEAT = BASE + BODY
CHUNK = SLOTS * FEAT // 128
RAD = 128
GH = 56
REACH = STEPS * HALO
WIDE = COLS + 2 * REACH
SPECIES = 4
NEAR = 6
UNROLL = 9
NT = (((1,), (1,)), ((), ()))
NN = (((1,), (0,)), ((), ()))


def split(x):
    hi = x.astype(BF)
    return hi, (x - hi.astype(F32)).astype(BF)


def dot(a, b, dims):
    return lax.dot_general(a, b, dims, preferred_element_type=F32)


def slot_matrix(position):
    rows = lax.broadcasted_iota(jnp.int32, (COLS, COLS), 0)
    slot = (rows & (PEERS - 1)) * SLOTS + (rows >> 7)
    return jnp.where(slot == position, 1.0, 0.0).astype(BF)


def pack_kernel(temp, thick, tracers, ground, sun, day, pos, adj, coef, send, right, left, table, bundle):
    bundle[0:LEV, :] = temp[...]
    bundle[ROW : ROW + LEV, :] = thick[...]
    bundle[ROW + LEV : BASE, :] = jnp.zeros((ROW - LEV, COLS), F32)
    spare = BASE + LEV * SPECIES
    bundle[spare:FEAT, :] = jnp.zeros((FEAT - spare, COLS), F32)
    for l in range(LEV):
        bundle[BASE + SPECIES * l : BASE + SPECIES * (l + 1), :] = tracers[l]
    sunny = sun[...]
    bundle[LEV : LEV + 1, :] = ground[...]
    bundle[LEV + 1 : LEV + 2, :] = sunny
    bundle[LEV + 2 : LEV + 3, :] = day[...].astype(F32) * sunny
    tail = bundle[256:288, :]
    for k in range(1, 4):
        bundle[256 + 32 * k : 288 + 32 * k, :] = tail
    placing = slot_matrix(pos[...])
    hi, lo = split(bundle[...])
    packed = dot(placing, hi, NT) + dot(placing, lo, NT)
    lane = lax.broadcasted_iota(jnp.int32, (PEERS, 128), 1) >> 5
    last = jnp.zeros((PEERS, 128), F32)
    for m in range(SLOTS):
        block = packed[m * PEERS : (m + 1) * PEERS, :]
        send[pl.ds(2 * m, PEERS, CHUNK), :] = block[:, 0:128]
        send[pl.ds(2 * m + 1, PEERS, CHUNK), :] = block[:, 128:256]
        last = jnp.where(lane == m, block[:, 256:384], last)
    send[pl.ds(CHUNK - 1, PEERS, CHUNK), :] = last
    right[0:BODY, :] = bundle[BASE:FEAT, COLS - REACH :]
    left[0:BODY, :] = bundle[BASE:FEAT, :REACH]
    column = lax.broadcasted_iota(jnp.int32, (NEAR, COLS), 1)
    reach = (adj[...] - column).astype(F32)
    pad = jnp.zeros((2, COLS), F32)
    both = jnp.concatenate([reach, pad, coef[...], pad], axis=0)
    table[...] = both
    right[BODY : BODY + 16, :] = both[:, COLS - REACH :]
    left[BODY : BODY + 16, :] = both[:, :REACH]


def pool_kernel(arrived, member, pooled, stage):
    ids = member[...] >> 2
    rows = lax.broadcasted_iota(jnp.int32, (RAD, 128), 0)
    lane = lax.broadcasted_iota(jnp.int32, (PEERS, 128), 1) >> 5
    last = arrived[pl.ds(CHUNK - 1, PEERS, CHUNK), :]
    chosen = []
    for m in range(SLOTS):
        chosen.append(jnp.where(rows == ids[m : m + 1, :], 0.25, 0.0).astype(BF))
        span = slice(m * PEERS, (m + 1) * PEERS)
        stage[span, 0:128] = arrived[pl.ds(2 * m, PEERS, CHUNK), :]
        stage[span, 128:256] = arrived[pl.ds(2 * m + 1, PEERS, CHUNK), :]
        stage[span, 256:384] = jnp.where(lane == m, last, 0.0)
    selector = jnp.concatenate(chosen, axis=1)
    hi, lo = split(stage[...])
    total = dot(selector, hi, NN) + dot(selector, lo, NN)
    pooled[0:128, :] = total[:, 0:128].T
    pooled[128:256, :] = total[:, 128:256].T
    tail = total[:, 256:384].T
    pooled[256:288, :] = tail[0:32] + tail[32:64] + tail[64:96] + tail[96:128]


def flux_kernel(side, own, other, opacity, emission, sunshine, mine, theirs, fields, warm, kept, sums, net):
    me = side[0]
    fields[pl.ds(me, 1)] = own[...][None]
    fields[pl.ds(1 - me, 1)] = other[...][None]
    for h in range(2):
        warm[h] = jnp.square(jnp.square(fields[h, 0:ROW, :]))
        fields[h, BASE:FEAT, :] = fields[h, BASE:FEAT, :] * (-DIFFUSE * LOG2E)
    surface = own[40:48, :]
    ground4 = jnp.square(jnp.square(surface[5:6, :]))
    slant = 1.0 / (DIFFUSE * surface[6:7, :])
    slant = jnp.broadcast_to(slant, (GH, RAD))
    insolation = surface[7:8, :]
    emit = jnp.broadcast_to(emission[...], (GH, RAD))

    def fold(x):
        return jnp.sum(x.reshape(GH // 8, 8, RAD), axis=0)

    def down(h, block, carry):
        thermal, direct = carry
        start = h * LEV + block * UNROLL
        shift = lax.rem(128 - start, 128)
        coeffs = [pltpu.roll(opacity[s], shift, 1) for s in range(SPECIES)]
        for i in range(UNROLL):
            inner = block * UNROLL + i
            tau = None
            for s in range(SPECIES):
                amount = fields[h, pl.ds(BASE + SPECIES * inner + s, 1), :]
                term = jnp.broadcast_to(coeffs[s][:, i : i + 1], (GH, RAD)) * amount
                tau = term if tau is None else tau + term
            opaque = 1.0 - jnp.exp2(tau)
            kept[start + i] = opaque
            source = emit * warm[h, pl.ds(inner, 1), :]
            gain = opaque * (thermal - source)
            thermal = thermal - gain
            passed = direct * jnp.exp2(tau * slant)
            sums[pl.ds(8 * (start + i), 8), :] = fold(gain + (direct - passed))
            direct = passed
        return thermal, direct

    def up(h, block, upward):
        start = h * LEV + block * UNROLL
        for i in range(UNROLL - 1, -1, -1):
            source = emit * warm[h, pl.ds(block * UNROLL + i, 1), :]
            gain = kept[start + i] * (upward - source)
            upward = upward - gain
            rows = pl.ds(8 * (start + i), 8)
            sums[rows, :] = sums[rows, :] + fold(gain)
        return upward

    blocks = LEV // UNROLL
    carry = (jnp.zeros((GH, RAD), F32), sunshine[...] * insolation)
    for h in range(2):
        carry = lax.fori_loop(0, blocks, functools.partial(down, h), carry)
    upward = emit * ground4
    for h in (1, 0):
        upward = lax.fori_loop(0, blocks, lambda b, u, h=h: up(h, blocks - 1 - b, u), upward)
    for h in range(2):
        total = None
        for k in range(8):
            part = sums[pl.ds(8 * LEV * h + k, LEV, 8), :]
            total = part if total is None else total + part
        net[h, 0:LEV, :] = total
        net[h, LEV:ROW, :] = jnp.zeros((ROW - LEV, RAD), F32)
    mine[...] = net[pl.ds(me, 1)][0]
    theirs[...] = net[pl.ds(1 - me, 1)][0]


def spread_kernel(mine, gotten, own, member, send):
    heat = (mine[...] + gotten[...]) / own[ROW:BASE, :]
    rows = lax.broadcasted_iota(jnp.int32, (ROW, RAD), 0)
    heat = jnp.where(rows < LEV, heat, 0.0)
    gap = jnp.zeros((16, RAD), F32)
    hi, lo = split(jnp.concatenate([heat, gap, heat, gap], axis=0))
    ids = member[...] >> 2
    lanes = lax.broadcasted_iota(jnp.int32, (PEERS, RAD), 1)
    for h in range(2):
        parts = []
        for m in (2 * h, 2 * h + 1):
            selector = jnp.where(lanes == ids[:, m : m + 1], 1.0, 0.0).astype(BF)
            parts.append(dot(selector, hi, NT) + dot(selector, lo, NT))
        send[pl.ds(h, PEERS, 2), :] = jnp.where(lanes < 64, parts[0], parts[1])


def unplace_kernel(returned, pos, heating):
    parts = []
    for h in range(2):
        turned = returned[pl.ds(h, PEERS, 2), :].T
        parts += [turned[0:ROW, :], turned[64 : 64 + ROW, :]]
    hi, lo = split(jnp.concatenate(parts, axis=1))
    placing = slot_matrix(pos[...])
    heating[...] = (dot(hi, placing, NN) + dot(lo, placing, NN))[0:LEV, :]


def mix_kernel(tracers, table, from_left, from_right, mixed, high, low, band, stage):
    spare = LEV * SPECIES
    stage[spare:BODY, :] = jnp.zeros((BODY - spare, COLS), F32)
    for l in range(LEV):
        stage[SPECIES * l : SPECIES * (l + 1), :] = tracers[l]
    parts = (from_left[0:BODY, :], stage[...], from_right[0:BODY, :])
    for part, start in zip(parts, (0, REACH, REACH + COLS)):
        hi, lo = split(part)
        high[0, :, start : start + part.shape[1]] = hi
        low[0, :, start : start + part.shape[1]] = lo
    tables = jnp.concatenate([from_left[BODY:, :], table[...], from_right[BODY:, :]], axis=1)
    shifted = pltpu.roll(tables, WIDE - HALO, 1)
    rows = lax.broadcasted_iota(jnp.int32, (256, 128), 0).astype(F32)
    lanes = lax.broadcasted_iota(jnp.int32, (1, 128), 1).astype(F32)

    def build(source, k):
        part = source[:, k * 128 : (k + 1) * 128]
        blend = jnp.where(rows == lanes + HALO, 1.0 - jnp.sum(part[8:14, :], axis=0, keepdims=True), 0.0)
        for n in range(NEAR):
            blend = blend + jnp.where(rows == lanes + part[n : n + 1, :], part[8 + n : 9 + n, :], 0.0)
        return split(blend)

    for k in range(7):
        hi, lo = build(shifted, k)
        band[0, 0, k] = hi
        band[0, 1, k] = lo
    for k in range(6):
        hi, lo = build(tables, k + 1)
        band[1, 0, k] = hi
        band[1, 1, k] = lo
    for step in range(STEPS):
        now, later = step % 2, (step + 1) % 2
        tiles = 7 - step
        first = step // 2
        for k in range(tiles):
            window = slice(k * 128, k * 128 + 256)
            bh, bl = band[now, 0, k + first], band[now, 1, k + first]
            xh, xl = high[now, :, window], low[now, :, window]
            new = dot(xh, bh, NN) + (dot(xh, bl, NN) + dot(xl, bh, NN))
            if step < STEPS - 1:
                hi, lo = split(new)
                high[later, :, k * 128 : (k + 1) * 128] = hi
                low[later, :, k * 128 : (k + 1) * 128] = lo
            else:
                for l in range(LEV):
                    mixed[l, :, k * 128 : (k + 1) * 128] = new[SPECIES * l : SPECIES * (l + 1), :]


def shape(*dims):
    return jax.ShapeDtypeStruct(dims, F32)


def call(kernel, name, out_shape, scratch, in_specs=None, grant=16):
    specs = {} if in_specs is None else {"in_specs": in_specs}
    return pl.pallas_call(
        kernel,
        out_shape=out_shape,
        scratch_shapes=scratch,
        name=name,
        compiler_params=pltpu.CompilerParams(vmem_limit_bytes=grant << 20),
        **specs,
    )


def per_device(
    stratum_warmth_anomaly,
    pressure_depth,
    absorber_amounts,
    ground_warmth_anomaly,
    sun_elevation_factor,
    daytime_mask,
    dispatch_position,
    arrival_membership,
    adjacency_table,
    blending_coefficient,
    opacity_table,
    emission_share,
    sunshine_share,
):
    n = lax.axis_size("grp")
    up = [(i, (i + 1) % n) for i in range(n)]
    down = [(j, i) for i, j in up]
    swap = [(0, 1), (1, 0)]
    halo_rows = BODY + 16
    tracers = jnp.transpose(absorber_amounts, (1, 0, 2))

    send, right, left, table = call(
        pack_kernel,
        "pack",
        (shape(PEERS * CHUNK, 128), shape(halo_rows, REACH), shape(halo_rows, REACH), shape(16, COLS)),
        [pltpu.VMEM((384, COLS), F32)],
        grant=60,
    )(
        stratum_warmth_anomaly,
        pressure_depth,
        tracers,
        ground_warmth_anomaly[None],
        sun_elevation_factor[None],
        daytime_mask[None],
        dispatch_position,
        adjacency_table,
        blending_coefficient,
    )
    from_left = lax.ppermute(right, "grp", up)
    from_right = lax.ppermute(left, "grp", down)
    arrived = lax.all_to_all(
        send.reshape(PEERS * CHUNK, 1, 128), "grp", split_axis=0, concat_axis=0, tiled=True
    )
    mixed = call(
        mix_kernel,
        "mix",
        shape(LEV, SPECIES, COLS),
        [
            pltpu.VMEM((2, BODY, WIDE), BF),
            pltpu.VMEM((2, BODY, WIDE), BF),
            pltpu.VMEM((2, 2, 7, 256, 128), BF),
            pltpu.VMEM((BODY, COLS), F32),
        ],
    )(tracers, table, from_left, from_right)
    members = arrival_membership.reshape(PEERS, SLOTS)
    opacity = jnp.pad(opacity_table, ((0, 0), (0, 0), (0, 128 - 2 * LEV)))
    side = lax.axis_index("sec").astype(jnp.int32)[None]
    arrived, mixed, members, members_t, opacity, emission, sunshine, side = lax.optimization_barrier(
        (arrived, mixed, members, members.T, opacity, emission_share[:, None], sunshine_share[:, None], side)
    )

    pooled = call(pool_kernel, "pool", shape(FEAT, RAD), [pltpu.VMEM((COLS, 384), F32)])(
        arrived.reshape(PEERS * CHUNK, 128), members_t
    )
    other = lax.ppermute(pooled, "sec", swap)
    mine, theirs = call(
        flux_kernel,
        "flux",
        (shape(ROW, RAD), shape(ROW, RAD)),
        [
            pltpu.VMEM((2, FEAT, RAD), F32),
            pltpu.VMEM((2, ROW, RAD), F32),
            pltpu.VMEM((2 * LEV, GH, RAD), F32),
            pltpu.VMEM((2 * LEV * 8, RAD), F32),
            pltpu.VMEM((2, ROW, RAD), F32),
        ],
        [pl.BlockSpec(memory_space=pltpu.SMEM)] + [pl.BlockSpec(memory_space=pltpu.VMEM)] * 5,
    )(side, pooled, other, opacity, emission, sunshine)
    gotten = lax.ppermute(theirs, "sec", swap)
    back = call(spread_kernel, "spread", shape(PEERS * 2, 128), [])(mine, gotten, pooled, members)
    returned = lax.all_to_all(
        back.reshape(PEERS * 2, 1, 128), "grp", split_axis=0, concat_axis=0, tiled=True
    ).reshape(PEERS * 2, 128)
    heating = call(unplace_kernel, "unplace", shape(LEV, COLS), [])(returned, dispatch_position)
    return (heating, jnp.transpose(mixed, (1, 0, 2)))


def solution(mesh):
    in_specs = (
        P("sec", "grp"),
        P("sec", "grp"),
        P(None, "sec", "grp"),
        P("grp"),
        P("grp"),
        P("grp"),
        P("grp", None),
        P("grp", None),
        P(None, "grp"),
        P(None, "grp"),
        P(None, "sec", None),
        P("sec"),
        P("sec"),
    )
    out_specs = (P("sec", "grp"), P(None, "sec", "grp"))
    return jax.shard_map(
        per_device, mesh=mesh, in_specs=in_specs, out_specs=out_specs, check_vma=False
    )
```

```python
import functools
import math

import jax
import jax.numpy as jnp
from jax import lax
from jax.experimental import pallas as pl
from jax.experimental.pallas import tpu as pltpu
from jax.sharding import PartitionSpec as P


STEPS = 4
HALO = 64
DIFFUSE = 1.66
LOG2E = math.log2(math.e)
BF = jnp.bfloat16
F32 = jnp.float32

PEERS = 128
SLOTS = 4
COLS = 512
LEV = 45
ROW = 48
BASE = 2 * ROW
BODY = 192
FEAT = BASE + BODY
CHUNK = SLOTS * FEAT // 128
RAD = 128
GH = 56
REACH = STEPS * HALO
WIDE = COLS + 2 * REACH
SPECIES = 4
NEAR = 6
UNROLL = 9
NT = (((1,), (1,)), ((), ()))
NN = (((1,), (0,)), ((), ()))


def split(x):
    hi = x.astype(BF)
    return hi, (x - hi.astype(F32)).astype(BF)


def dot(a, b, dims):
    return lax.dot_general(a, b, dims, preferred_element_type=F32)


def slot_matrix(position):
    rows = lax.broadcasted_iota(jnp.int32, (COLS, COLS), 0)
    slot = (rows & (PEERS - 1)) * SLOTS + (rows >> 7)
    return jnp.where(slot == position, 1.0, 0.0).astype(BF)


def pack_kernel(temp, thick, tracers, ground, sun, day, pos, adj, coef, send, right, left, table, bundle):
    bundle[0:LEV, :] = temp[...]
    bundle[ROW : ROW + LEV, :] = thick[...]
    bundle[ROW + LEV : BASE, :] = jnp.zeros((ROW - LEV, COLS), F32)
    spare = BASE + LEV * SPECIES
    bundle[spare:FEAT, :] = jnp.zeros((FEAT - spare, COLS), F32)
    for l in range(LEV):
        bundle[BASE + SPECIES * l : BASE + SPECIES * (l + 1), :] = tracers[l]
    sunny = sun[...]
    bundle[LEV : LEV + 1, :] = ground[...]
    bundle[LEV + 1 : LEV + 2, :] = sunny
    bundle[LEV + 2 : LEV + 3, :] = day[...].astype(F32) * sunny
    tail = bundle[256:288, :]
    for k in range(1, 4):
        bundle[256 + 32 * k : 288 + 32 * k, :] = tail
    placing = slot_matrix(pos[...])
    hi, lo = split(bundle[...])
    packed = dot(placing, hi, NT) + dot(placing, lo, NT)
    lane = lax.broadcasted_iota(jnp.int32, (PEERS, 128), 1) >> 5
    last = jnp.zeros((PEERS, 128), F32)
    for m in range(SLOTS):
        block = packed[m * PEERS : (m + 1) * PEERS, :]
        send[pl.ds(2 * m, PEERS, CHUNK), :] = block[:, 0:128]
        send[pl.ds(2 * m + 1, PEERS, CHUNK), :] = block[:, 128:256]
        last = jnp.where(lane == m, block[:, 256:384], last)
    send[pl.ds(CHUNK - 1, PEERS, CHUNK), :] = last
    right[0:BODY, :] = bundle[BASE:FEAT, COLS - REACH :]
    left[0:BODY, :] = bundle[BASE:FEAT, :REACH]
    column = lax.broadcasted_iota(jnp.int32, (NEAR, COLS), 1)
    reach = (adj[...] - column).astype(F32)
    pad = jnp.zeros((2, COLS), F32)
    both = jnp.concatenate([reach, pad, coef[...], pad], axis=0)
    table[...] = both
    right[BODY : BODY + 16, :] = both[:, COLS - REACH :]
    left[BODY : BODY + 16, :] = both[:, :REACH]


def pool_kernel(arrived, member, pooled, stage):
    ids = member[...] >> 2
    rows = lax.broadcasted_iota(jnp.int32, (RAD, 128), 0)
    lane = lax.broadcasted_iota(jnp.int32, (PEERS, 128), 1) >> 5
    last = arrived[pl.ds(CHUNK - 1, PEERS, CHUNK), :]
    chosen = []
    for m in range(SLOTS):
        chosen.append(jnp.where(rows == ids[m : m + 1, :], 0.25, 0.0).astype(BF))
        span = slice(m * PEERS, (m + 1) * PEERS)
        stage[span, 0:128] = arrived[pl.ds(2 * m, PEERS, CHUNK), :]
        stage[span, 128:256] = arrived[pl.ds(2 * m + 1, PEERS, CHUNK), :]
        stage[span, 256:384] = jnp.where(lane == m, last, 0.0)
    selector = jnp.concatenate(chosen, axis=1)
    hi, lo = split(stage[...])
    total = dot(selector, hi, NN) + dot(selector, lo, NN)
    pooled[0:128, :] = total[:, 0:128].T
    pooled[128:256, :] = total[:, 128:256].T
    tail = total[:, 256:384].T
    pooled[256:288, :] = tail[0:32] + tail[32:64] + tail[64:96] + tail[96:128]


def flux_kernel(side, own, other, opacity, emission, sunshine, mine, theirs, fields, warm, kept, sums, net):
    me = side[0]
    fields[pl.ds(me, 1)] = own[...][None]
    fields[pl.ds(1 - me, 1)] = other[...][None]
    for h in range(2):
        warm[h] = jnp.square(jnp.square(fields[h, 0:ROW, :]))
        fields[h, BASE:FEAT, :] = fields[h, BASE:FEAT, :] * (-DIFFUSE * LOG2E)
    surface = own[40:48, :]
    ground4 = jnp.square(jnp.square(surface[5:6, :]))
    slant = 1.0 / (DIFFUSE * surface[6:7, :])
    slant = jnp.broadcast_to(slant, (GH, RAD))
    insolation = surface[7:8, :]
    emit = jnp.broadcast_to(emission[...], (GH, RAD))

    def fold(x):
        return jnp.sum(x.reshape(GH // 8, 8, RAD), axis=0)

    def down(h, block, carry):
        thermal, direct = carry
        start = h * LEV + block * UNROLL
        shift = lax.rem(128 - start, 128)
        coeffs = [pltpu.roll(opacity[s], shift, 1) for s in range(SPECIES)]
        for i in range(UNROLL):
            inner = block * UNROLL + i
            tau = None
            for s in range(SPECIES):
                amount = fields[h, pl.ds(BASE + SPECIES * inner + s, 1), :]
                term = jnp.broadcast_to(coeffs[s][:, i : i + 1], (GH, RAD)) * amount
                tau = term if tau is None else tau + term
            opaque = 1.0 - jnp.exp2(tau)
            kept[start + i] = opaque
            source = emit * warm[h, pl.ds(inner, 1), :]
            gain = opaque * (thermal - source)
            thermal = thermal - gain
            passed = direct * jnp.exp2(tau * slant)
            sums[pl.ds(8 * (start + i), 8), :] = fold(gain + (direct - passed))
            direct = passed
        return thermal, direct

    def up(h, block, upward):
        start = h * LEV + block * UNROLL
        for i in range(UNROLL - 1, -1, -1):
            source = emit * warm[h, pl.ds(block * UNROLL + i, 1), :]
            gain = kept[start + i] * (upward - source)
            upward = upward - gain
            rows = pl.ds(8 * (start + i), 8)
            sums[rows, :] = sums[rows, :] + fold(gain)
        return upward

    blocks = LEV // UNROLL
    carry = (jnp.zeros((GH, RAD), F32), sunshine[...] * insolation)
    for h in range(2):
        carry = lax.fori_loop(0, blocks, functools.partial(down, h), carry)
    upward = emit * ground4
    for h in (1, 0):
        upward = lax.fori_loop(0, blocks, lambda b, u, h=h: up(h, blocks - 1 - b, u), upward)
    for h in range(2):
        total = None
        for k in range(8):
            part = sums[pl.ds(8 * LEV * h + k, LEV, 8), :]
            total = part if total is None else total + part
        net[h, 0:LEV, :] = total
        net[h, LEV:ROW, :] = jnp.zeros((ROW - LEV, RAD), F32)
    mine[...] = net[pl.ds(me, 1)][0]
    theirs[...] = net[pl.ds(1 - me, 1)][0]


def spread_kernel(mine, gotten, own, member, send):
    heat = (mine[...] + gotten[...]) / own[ROW:BASE, :]
    rows = lax.broadcasted_iota(jnp.int32, (ROW, RAD), 0)
    heat = jnp.where(rows < LEV, heat, 0.0)
    gap = jnp.zeros((16, RAD), F32)
    hi, lo = split(jnp.concatenate([heat, gap, heat, gap], axis=0))
    ids = member[...] >> 2
    lanes = lax.broadcasted_iota(jnp.int32, (PEERS, RAD), 1)
    for h in range(2):
        parts = []
        for m in (2 * h, 2 * h + 1):
            selector = jnp.where(lanes == ids[:, m : m + 1], 1.0, 0.0).astype(BF)
            parts.append(dot(selector, hi, NT) + dot(selector, lo, NT))
        send[pl.ds(h, PEERS, 2), :] = jnp.where(lanes < 64, parts[0], parts[1])


def unplace_kernel(returned, pos, heating):
    parts = []
    for h in range(2):
        turned = returned[pl.ds(h, PEERS, 2), :].T
        parts += [turned[0:ROW, :], turned[64 : 64 + ROW, :]]
    hi, lo = split(jnp.concatenate(parts, axis=1))
    placing = slot_matrix(pos[...])
    heating[...] = (dot(hi, placing, NN) + dot(lo, placing, NN))[0:LEV, :]


def mix_kernel(tracers, table, from_left, from_right, mixed, high, low, band, stage):
    spare = LEV * SPECIES
    stage[spare:BODY, :] = jnp.zeros((BODY - spare, COLS), F32)
    for l in range(LEV):
        stage[SPECIES * l : SPECIES * (l + 1), :] = tracers[l]
    parts = (from_left[0:BODY, :], stage[...], from_right[0:BODY, :])
    for part, start in zip(parts, (0, REACH, REACH + COLS)):
        hi, lo = split(part)
        high[0, :, start : start + part.shape[1]] = hi
        low[0, :, start : start + part.shape[1]] = lo
    tables = jnp.concatenate([from_left[BODY:, :], table[...], from_right[BODY:, :]], axis=1)
    shifted = pltpu.roll(tables, WIDE - HALO, 1)
    rows = lax.broadcasted_iota(jnp.int32, (256, 128), 0).astype(F32)
    lanes = lax.broadcasted_iota(jnp.int32, (1, 128), 1).astype(F32)

    def build(source, k):
        part = source[:, k * 128 : (k + 1) * 128]
        blend = jnp.where(rows == lanes + HALO, 1.0 - jnp.sum(part[8:14, :], axis=0, keepdims=True), 0.0)
        for n in range(NEAR):
            blend = blend + jnp.where(rows == lanes + part[n : n + 1, :], part[8 + n : 9 + n, :], 0.0)
        return split(blend)

    for k in range(7):
        hi, lo = build(shifted, k)
        band[0, 0, k] = hi
        band[0, 1, k] = lo
    for k in range(6):
        hi, lo = build(tables, k + 1)
        band[1, 0, k] = hi
        band[1, 1, k] = lo
    for step in range(STEPS):
        now, later = step % 2, (step + 1) % 2
        tiles = 7 - step
        first = step // 2
        for k in range(tiles):
            window = slice(k * 128, k * 128 + 256)
            bh, bl = band[now, 0, k + first], band[now, 1, k + first]
            xh, xl = high[now, :, window], low[now, :, window]
            new = dot(xh, bh, NN) + (dot(xh, bl, NN) + dot(xl, bh, NN))
            if step < STEPS - 1:
                hi, lo = split(new)
                high[later, :, k * 128 : (k + 1) * 128] = hi
                low[later, :, k * 128 : (k + 1) * 128] = lo
            else:
                for l in range(LEV):
                    mixed[l, :, k * 128 : (k + 1) * 128] = new[SPECIES * l : SPECIES * (l + 1), :]


def shape(*dims):
    return jax.ShapeDtypeStruct(dims, F32)


def call(kernel, out_shape, scratch, in_specs=None, grant=16):
    specs = {} if in_specs is None else {"in_specs": in_specs}
    return pl.pallas_call(
        kernel,
        out_shape=out_shape,
        scratch_shapes=scratch,
        compiler_params=pltpu.CompilerParams(vmem_limit_bytes=grant << 20),
        **specs,
    )


def per_device(
    stratum_warmth_anomaly,
    pressure_depth,
    absorber_amounts,
    ground_warmth_anomaly,
    sun_elevation_factor,
    daytime_mask,
    dispatch_position,
    arrival_membership,
    adjacency_table,
    blending_coefficient,
    opacity_table,
    emission_share,
    sunshine_share,
):
    n = lax.axis_size("grp")
    up = [(i, (i + 1) % n) for i in range(n)]
    down = [(j, i) for i, j in up]
    swap = [(0, 1), (1, 0)]
    halo_rows = BODY + 16
    tracers = jnp.transpose(absorber_amounts, (1, 0, 2))

    send, right, left, table = call(
        pack_kernel,
        (shape(PEERS * CHUNK, 128), shape(halo_rows, REACH), shape(halo_rows, REACH), shape(16, COLS)),
        [pltpu.VMEM((384, COLS), F32)],
        grant=60,
    )(
        stratum_warmth_anomaly,
        pressure_depth,
        tracers,
        ground_warmth_anomaly[None],
        sun_elevation_factor[None],
        daytime_mask[None],
        dispatch_position,
        adjacency_table,
        blending_coefficient,
    )
    from_left = lax.ppermute(right, "grp", up)
    from_right = lax.ppermute(left, "grp", down)
    arrived = lax.all_to_all(send.reshape(PEERS * CHUNK, 1, 128), "grp", split_axis=0, concat_axis=0, tiled=True)
    mixed = call(
        mix_kernel,
        shape(LEV, SPECIES, COLS),
        [
            pltpu.VMEM((2, BODY, WIDE), BF),
            pltpu.VMEM((2, BODY, WIDE), BF),
            pltpu.VMEM((2, 2, 7, 256, 128), BF),
            pltpu.VMEM((BODY, COLS), F32),
        ],
    )(tracers, table, from_left, from_right)
    members = arrival_membership.reshape(PEERS, SLOTS)
    opacity = jnp.pad(opacity_table, ((0, 0), (0, 0), (0, 128 - 2 * LEV)))
    side = lax.axis_index("sec").astype(jnp.int32)[None]
    arrived, mixed, members, members_t, opacity, emission, sunshine, side = lax.optimization_barrier(
        (arrived, mixed, members, members.T, opacity, emission_share[:, None], sunshine_share[:, None], side)
    )

    pooled = call(pool_kernel, shape(FEAT, RAD), [pltpu.VMEM((COLS, 384), F32)])(
        arrived.reshape(PEERS * CHUNK, 128), members_t
    )
    other = lax.ppermute(pooled, "sec", swap)
    mine, theirs = call(
        flux_kernel,
        (shape(ROW, RAD), shape(ROW, RAD)),
        [
            pltpu.VMEM((2, FEAT, RAD), F32),
            pltpu.VMEM((2, ROW, RAD), F32),
            pltpu.VMEM((2 * LEV, GH, RAD), F32),
            pltpu.VMEM((2 * LEV * 8, RAD), F32),
            pltpu.VMEM((2, ROW, RAD), F32),
        ],
        [pl.BlockSpec(memory_space=pltpu.SMEM)] + [pl.BlockSpec(memory_space=pltpu.VMEM)] * 5,
    )(side, pooled, other, opacity, emission, sunshine)
    gotten = lax.ppermute(theirs, "sec", swap)
    back = call(spread_kernel, shape(PEERS * 2, 128), [])(mine, gotten, pooled, members)
    returned = lax.all_to_all(
        back.reshape(PEERS * 2, 1, 128), "grp", split_axis=0, concat_axis=0, tiled=True
    ).reshape(PEERS * 2, 128)
    heating = call(unplace_kernel, shape(LEV, COLS), [])(returned, dispatch_position)
    return (heating, jnp.transpose(mixed, (1, 0, 2)))


def solution(mesh):
    in_specs = (
        P("sec", "grp"),
        P("sec", "grp"),
        P(None, "sec", "grp"),
        P("grp"),
        P("grp"),
        P("grp"),
        P("grp", None),
        P("grp", None),
        P(None, "grp"),
        P(None, "grp"),
        P(None, "sec", None),
        P("sec"),
        P("sec"),
    )
    out_specs = (P("sec", "grp"), P(None, "sec", "grp"))
    return jax.shard_map(
        per_device, mesh=mesh, in_specs=in_specs, out_specs=out_specs, check_vma=False
    )
```

```python
import math

import jax
import jax.numpy as jnp
from jax import lax
from jax.experimental import pallas as pl
from jax.experimental.pallas import tpu as pltpu
from jax.sharding import PartitionSpec as P


STEPS = 4
HALO = 64
DIFFUSE = 1.66
LOG2E = math.log2(math.e)
BF = jnp.bfloat16
F32 = jnp.float32

PEERS = 128
SLOTS = 4
COLS = 512
LEV = 45
ROW = 48
BASE = 2 * ROW
BODY = 192
FEAT = BASE + BODY
CHUNK = SLOTS * FEAT // 128
RAD = 128
GH = 56
REACH = STEPS * HALO
WIDE = COLS + 2 * REACH
SPECIES = 4
NEAR = 6
BLOCK = 9
BLOCKS = 2 * LEV // BLOCK
TALL = 64
PART = 40
NT = (((1,), (1,)), ((), ()))
NN = (((1,), (0,)), ((), ()))


def split(x):
    hi = x.astype(BF)
    return hi, (x - hi.astype(F32)).astype(BF)


def dot(a, b, dims):
    return lax.dot_general(a, b, dims, preferred_element_type=F32)


def slot_matrix(position):
    rows = lax.broadcasted_iota(jnp.int32, (COLS, COLS), 0)
    slot = (rows & (PEERS - 1)) * SLOTS + (rows >> 7)
    return jnp.where(slot == position, 1.0, 0.0).astype(BF)


def pack_kernel(*refs):
    sources, outs, scratch = refs[:9], refs[9:13], refs[13:]
    temp, thick, tracers, ground, sun, day, pos, adj, coef = scratch[:9]
    send, right, left, table, bundle, sems, done = scratch[9:]
    copies = [pltpu.make_async_copy(a, b, sems.at[i]) for i, (a, b) in enumerate(zip(sources, scratch))]
    for i in (6, 7, 8, 2, 0, 1, 3, 4, 5):
        copies[i].start()
    stores = [pltpu.make_async_copy(a, b, done.at[i]) for i, (a, b) in enumerate(zip((send, right, left, table), outs))]
    bundle[ROW + LEV : BASE, :] = jnp.zeros((ROW - LEV, COLS), F32)
    spare = BASE + LEV * SPECIES
    bundle[spare:FEAT, :] = jnp.zeros((FEAT - spare, COLS), F32)
    for i in (6, 7, 8):
        copies[i].wait()
    placing = slot_matrix(pos[...])
    column = lax.broadcasted_iota(jnp.int32, (NEAR, COLS), 1)
    reach = (adj[...] - column).astype(F32)
    pad = jnp.zeros((2, COLS), F32)
    both = jnp.concatenate([reach, pad, coef[...], pad], axis=0)
    table[...] = both
    right[BODY : BODY + 16, :] = both[:, COLS - REACH :]
    left[BODY : BODY + 16, :] = both[:, :REACH]
    copies[2].wait()
    for l in range(LEV):
        bundle[BASE + SPECIES * l : BASE + SPECIES * (l + 1), :] = tracers[l]
    right[0:BODY, :] = bundle[BASE:FEAT, COLS - REACH :]
    left[0:BODY, :] = bundle[BASE:FEAT, :REACH]
    for i in (1, 2, 3):
        stores[i].start()
    for i in (0, 1, 3, 4, 5):
        copies[i].wait()
    bundle[0:LEV, :] = temp[...]
    bundle[ROW : ROW + LEV, :] = thick[...]
    sunny = sun[...]
    bundle[LEV : LEV + 1, :] = ground[...]
    bundle[LEV + 1 : LEV + 2, :] = sunny
    bundle[LEV + 2 : LEV + 3, :] = day[...].astype(F32) * sunny
    tail = bundle[256:288, :]
    for k in range(1, 4):
        bundle[256 + 32 * k : 288 + 32 * k, :] = tail
    hi, lo = split(bundle[...])
    packed = dot(placing, hi, NT) + dot(placing, lo, NT)
    lane = lax.broadcasted_iota(jnp.int32, (PEERS, 128), 1) >> 5
    last = jnp.zeros((PEERS, 128), F32)
    for m in range(SLOTS):
        block = packed[m * PEERS : (m + 1) * PEERS, :]
        send[pl.ds(2 * m, PEERS, CHUNK), :] = block[:, 0:128]
        send[pl.ds(2 * m + 1, PEERS, CHUNK), :] = block[:, 128:256]
        last = jnp.where(lane == m, block[:, 256:384], last)
    send[pl.ds(CHUNK - 1, PEERS, CHUNK), :] = last
    stores[0].start()
    for store in stores:
        store.wait()


def pool_kernel(arrived, member, pooled, stage):
    ids = member[...] >> 2
    rows = lax.broadcasted_iota(jnp.int32, (RAD, 128), 0)
    lane = lax.broadcasted_iota(jnp.int32, (PEERS, 128), 1) >> 5
    last = arrived[pl.ds(CHUNK - 1, PEERS, CHUNK), :]
    chosen = []
    for m in range(SLOTS):
        chosen.append(jnp.where(rows == ids[m : m + 1, :], 0.25, 0.0).astype(BF))
        span = slice(m * PEERS, (m + 1) * PEERS)
        stage[span, 0:128] = arrived[pl.ds(2 * m, PEERS, CHUNK), :]
        stage[span, 128:256] = arrived[pl.ds(2 * m + 1, PEERS, CHUNK), :]
        stage[span, 256:384] = jnp.where(lane == m, last, 0.0)
    selector = jnp.concatenate(chosen, axis=1)
    hi, lo = split(stage[...])
    total = dot(selector, hi, NN) + dot(selector, lo, NN)
    pooled[0:128, :] = total[:, 0:128].T
    pooled[128:256, :] = total[:, 128:256].T
    tail = total[:, 256:384].T
    pooled[256:288, :] = tail[0:32] + tail[32:64] + tail[64:96] + tail[96:128]


def weight_kernel(opacity, weights):
    rows = lax.broadcasted_iota(jnp.int32, (128, 128), 0)
    lanes = lax.broadcasted_iota(jnp.int32, (128, 128), 1)
    picks = []
    for s in range(SPECIES):
        lane = jnp.where(rows < BLOCK, SPECIES * rows + s, -1)
        picks.append((lanes == lane) | (lanes == jnp.where(lane < 0, -1, lane + 2 * PART)))
    for s in range(SPECIES):
        lane = jnp.where(rows < BLOCK, SPECIES * rows + s + PART, -1)
        picks.append(lanes == lane)
    picker = jnp.concatenate([jnp.where(p, 1.0, 0.0).astype(BF) for p in picks], axis=0)
    group = lax.broadcasted_iota(jnp.int32, (TALL, 128), 1)
    group = jnp.where(group >= 2 * PART, group - 2 * PART, jnp.where(group >= PART, group - PART, group)) >> 2
    pad = jnp.zeros((TALL - GH, 128), F32)
    for b in range(BLOCKS):
        his, los = [], []
        for s in range(SPECIES):
            level = opacity[s]
            if b:
                level = pltpu.roll(level, 128 - b * BLOCK, 1)
            hi, lo = split(jnp.concatenate([level, pad], axis=0))
            his.append(hi)
            los.append(lo)
        wide = dot(jnp.concatenate(his + los, axis=1), picker, NN)
        for i in range(BLOCK):
            start = (b * BLOCK + i) * TALL
            weights[start : start + TALL, :] = jnp.where(group == i, wide, 0.0).astype(BF)


def flux_kernel(side, own, other, weights, emission, sunshine, mine, theirs, fields, warm, taus, sums, net):
    me = side[0]
    fields[pl.ds(me, 1)] = own[...][None]
    fields[pl.ds(1 - me, 1)] = other[...][None]
    for h in range(2):
        warm[h] = jnp.square(jnp.square(fields[h, 0:ROW, :]))
        fields[h, BASE:FEAT, :] = fields[h, BASE:FEAT, :] * (-DIFFUSE * LOG2E)
    surface = own[40:48, :]
    ground4 = jnp.square(jnp.square(surface[5:6, :]))
    slant = 1.0 / (DIFFUSE * surface[6:7, :])
    slant = jnp.broadcast_to(slant, (GH, RAD))
    insolation = surface[7:8, :]
    emit = jnp.broadcast_to(emission[...], (GH, RAD))
    pad = jnp.zeros((128 - 3 * PART, RAD), F32)
    tall = BLOCK * TALL
    for b in range(BLOCKS):
        h, inner = divmod(b * BLOCK, LEV)
        start = BASE + SPECIES * inner
        part = fields[h, start : start + PART, :]
        hi = part.astype(BF).astype(F32)
        amounts = jnp.concatenate([hi, hi, part - hi, pad], axis=0).astype(BF)
        taus[b * tall : (b + 1) * tall, :] = dot(weights[b * tall : (b + 1) * tall, :], amounts, NN)

    def fold(x):
        return jnp.sum(x.reshape(GH // 8, 8, RAD), axis=0)

    thermal = jnp.zeros((GH, RAD), F32)
    direct = sunshine[...] * insolation
    beam = fold(direct)
    for l in range(2 * LEV):
        h, inner = divmod(l, LEV)
        rows = slice(l * TALL, l * TALL + GH)
        tau = taus[rows, :]
        opaque = 1.0 - jnp.exp2(tau)
        taus[rows, :] = opaque
        source = emit * warm[h, inner : inner + 1, :]
        gain = opaque * (thermal - source)
        thermal = thermal - gain
        direct = direct * jnp.exp2(tau * slant)
        below = fold(direct)
        sums[8 * l : 8 * l + 8, :] = fold(gain) + (beam - below)
        beam = below
    upward = emit * ground4
    for l in range(2 * LEV - 1, -1, -1):
        h, inner = divmod(l, LEV)
        source = emit * warm[h, inner : inner + 1, :]
        gain = taus[l * TALL : l * TALL + GH, :] * (upward - source)
        upward = upward - gain
        sums[8 * l : 8 * l + 8, :] = sums[8 * l : 8 * l + 8, :] + fold(gain)
    for h in range(2):
        total = None
        for k in range(8):
            part = sums[pl.ds(8 * LEV * h + k, LEV, 8), :]
            total = part if total is None else total + part
        net[h, 0:LEV, :] = total
        net[h, LEV:ROW, :] = jnp.zeros((ROW - LEV, RAD), F32)
    mine[...] = net[pl.ds(me, 1)][0]
    theirs[...] = net[pl.ds(1 - me, 1)][0]


def spread_kernel(mine, gotten, own, member, send):
    heat = (mine[...] + gotten[...]) / own[ROW:BASE, :]
    rows = lax.broadcasted_iota(jnp.int32, (ROW, RAD), 0)
    heat = jnp.where(rows < LEV, heat, 0.0)
    gap = jnp.zeros((16, RAD), F32)
    hi, lo = split(jnp.concatenate([heat, gap, heat, gap], axis=0))
    ids = member[...] >> 2
    lanes = lax.broadcasted_iota(jnp.int32, (PEERS, RAD), 1)
    for h in range(2):
        parts = []
        for m in (2 * h, 2 * h + 1):
            selector = jnp.where(lanes == ids[:, m : m + 1], 1.0, 0.0).astype(BF)
            parts.append(dot(selector, hi, NT) + dot(selector, lo, NT))
        send[pl.ds(h, PEERS, 2), :] = jnp.where(lanes < 64, parts[0], parts[1])


def unplace_kernel(returned, pos, heating):
    parts = []
    for h in range(2):
        turned = returned[pl.ds(h, PEERS, 2), :].T
        parts += [turned[0:ROW, :], turned[64 : 64 + ROW, :]]
    hi, lo = split(jnp.concatenate(parts, axis=1))
    placing = slot_matrix(pos[...])
    heating[...] = (dot(hi, placing, NN) + dot(lo, placing, NN))[0:LEV, :]


def mix_kernel(tracers, table, from_left, from_right, mixed, high, low, band, stage):
    spare = LEV * SPECIES
    stage[spare:BODY, :] = jnp.zeros((BODY - spare, COLS), F32)
    for l in range(LEV):
        stage[SPECIES * l : SPECIES * (l + 1), :] = tracers[l]
    parts = (from_left[0:BODY, :], stage[...], from_right[0:BODY, :])
    for part, start in zip(parts, (0, REACH, REACH + COLS)):
        hi, lo = split(part)
        high[0, :, start : start + part.shape[1]] = hi
        low[0, :, start : start + part.shape[1]] = lo
    tables = jnp.concatenate([from_left[BODY:, :], table[...], from_right[BODY:, :]], axis=1)
    shifted = pltpu.roll(tables, WIDE - HALO, 1)
    rows = lax.broadcasted_iota(jnp.int32, (256, 128), 0).astype(F32)
    lanes = lax.broadcasted_iota(jnp.int32, (1, 128), 1).astype(F32)

    def build(source, k):
        part = source[:, k * 128 : (k + 1) * 128]
        blend = jnp.where(rows == lanes + HALO, 1.0 - jnp.sum(part[8:14, :], axis=0, keepdims=True), 0.0)
        for n in range(NEAR):
            blend = blend + jnp.where(rows == lanes + part[n : n + 1, :], part[8 + n : 9 + n, :], 0.0)
        return split(blend)

    for k in range(7):
        hi, lo = build(shifted, k)
        band[0, 0, k] = hi
        band[0, 1, k] = lo
    for k in range(6):
        hi, lo = build(tables, k + 1)
        band[1, 0, k] = hi
        band[1, 1, k] = lo
    for step in range(STEPS):
        now, later = step % 2, (step + 1) % 2
        tiles = 7 - step
        first = step // 2
        for k in range(tiles):
            window = slice(k * 128, k * 128 + 256)
            bh, bl = band[now, 0, k + first], band[now, 1, k + first]
            xh, xl = high[now, :, window], low[now, :, window]
            new = dot(xh, bh, NN) + (dot(xh, bl, NN) + dot(xl, bh, NN))
            if step < STEPS - 1:
                hi, lo = split(new)
                high[later, :, k * 128 : (k + 1) * 128] = hi
                low[later, :, k * 128 : (k + 1) * 128] = lo
            else:
                for l in range(LEV):
                    mixed[l, :, k * 128 : (k + 1) * 128] = new[SPECIES * l : SPECIES * (l + 1), :]


def shape(*dims):
    return jax.ShapeDtypeStruct(dims, F32)


def call(kernel, out_shape, scratch, vmem_limit_bytes=16 << 20, **specs):
    return pl.pallas_call(
        kernel,
        out_shape=out_shape,
        scratch_shapes=scratch,
        compiler_params=pltpu.CompilerParams(vmem_limit_bytes=vmem_limit_bytes),
        **specs,
    )


def per_device(
    stratum_warmth_anomaly,
    pressure_depth,
    absorber_amounts,
    ground_warmth_anomaly,
    sun_elevation_factor,
    daytime_mask,
    dispatch_position,
    arrival_membership,
    adjacency_table,
    blending_coefficient,
    opacity_table,
    emission_share,
    sunshine_share,
):
    n = lax.axis_size("grp")
    up = [(i, (i + 1) % n) for i in range(n)]
    down = [(j, i) for i, j in up]
    swap = [(0, 1), (1, 0)]
    halo_rows = BODY + 16
    tracers = jnp.transpose(absorber_amounts, (1, 0, 2))

    hbm = pl.BlockSpec(memory_space=pltpu.HBM)
    packed = (shape(PEERS * CHUNK, 128), shape(halo_rows, REACH), shape(halo_rows, REACH), shape(16, COLS))
    given = ((LEV, COLS), (LEV, COLS), (LEV, SPECIES, COLS), (1, COLS), (1, COLS))
    send, right, left, table = call(
        pack_kernel,
        packed,
        [pltpu.VMEM(dims, F32) for dims in given]
        + [pltpu.VMEM((rows, COLS), jnp.int32) for rows in (1, 1, NEAR)]
        + [pltpu.VMEM((NEAR, COLS), F32)]
        + [pltpu.VMEM(out.shape, F32) for out in packed]
        + [pltpu.VMEM((384, COLS), F32), pltpu.SemaphoreType.DMA((9,)), pltpu.SemaphoreType.DMA((4,))],
        in_specs=[hbm] * 9,
        out_specs=[hbm] * 4,
        vmem_limit_bytes=60 << 20,
    )(
        stratum_warmth_anomaly,
        pressure_depth,
        tracers,
        ground_warmth_anomaly[None],
        sun_elevation_factor[None],
        daytime_mask[None],
        dispatch_position,
        adjacency_table,
        blending_coefficient,
    )
    from_left = lax.ppermute(right, "grp", up)
    from_right = lax.ppermute(left, "grp", down)
    arrived = lax.all_to_all(send.reshape(PEERS * CHUNK, 1, 128), "grp", split_axis=0, concat_axis=0, tiled=True)
    mixed = call(
        mix_kernel,
        shape(LEV, SPECIES, COLS),
        [
            pltpu.VMEM((2, BODY, WIDE), BF),
            pltpu.VMEM((2, BODY, WIDE), BF),
            pltpu.VMEM((2, 2, 7, 256, 128), BF),
            pltpu.VMEM((BODY, COLS), F32),
        ],
    )(tracers, table, from_left, from_right)
    members = arrival_membership.reshape(PEERS, SLOTS)
    opacity = jnp.pad(opacity_table, ((0, 0), (0, 0), (0, 128 - 2 * LEV)))
    weights = call(weight_kernel, jax.ShapeDtypeStruct((2 * LEV * TALL, 128), BF), [])(opacity)
    side = lax.axis_index("sec").astype(jnp.int32)[None]
    arrived, mixed, members, members_t, weights, emission, sunshine, side = lax.optimization_barrier(
        (arrived, mixed, members, members.T, weights, emission_share[:, None], sunshine_share[:, None], side)
    )

    pooled = call(pool_kernel, shape(FEAT, RAD), [pltpu.VMEM((COLS, 384), F32)])(
        arrived.reshape(PEERS * CHUNK, 128), members_t
    )
    other = lax.ppermute(pooled, "sec", swap)
    mine, theirs = call(
        flux_kernel,
        (shape(ROW, RAD), shape(ROW, RAD)),
        [
            pltpu.VMEM((2, FEAT, RAD), F32),
            pltpu.VMEM((2, ROW, RAD), F32),
            pltpu.VMEM((2 * LEV * TALL, RAD), F32),
            pltpu.VMEM((2 * LEV * 8, RAD), F32),
            pltpu.VMEM((2, ROW, RAD), F32),
        ],
        in_specs=[pl.BlockSpec(memory_space=pltpu.SMEM)] + [pl.BlockSpec(memory_space=pltpu.VMEM)] * 5,
    )(side, pooled, other, weights, emission, sunshine)
    gotten = lax.ppermute(theirs, "sec", swap)
    back = call(spread_kernel, shape(PEERS * 2, 128), [])(mine, gotten, pooled, members)
    returned = lax.all_to_all(
        back.reshape(PEERS * 2, 1, 128), "grp", split_axis=0, concat_axis=0, tiled=True
    ).reshape(PEERS * 2, 128)
    heating = call(unplace_kernel, shape(LEV, COLS), [])(returned, dispatch_position)
    return (heating, jnp.transpose(mixed, (1, 0, 2)))


def solution(mesh):
    in_specs = (
        P("sec", "grp"),
        P("sec", "grp"),
        P(None, "sec", "grp"),
        P("grp"),
        P("grp"),
        P("grp"),
        P("grp", None),
        P("grp", None),
        P(None, "grp"),
        P(None, "grp"),
        P(None, "sec", None),
        P("sec"),
        P("sec"),
    )
    out_specs = (P("sec", "grp"), P(None, "sec", "grp"))
    return jax.shard_map(
        per_device, mesh=mesh, in_specs=in_specs, out_specs=out_specs, check_vma=False
    )
```

```python
import math

import jax
import jax.numpy as jnp
from jax import lax
from jax.experimental import pallas as pl
from jax.experimental.pallas import tpu as pltpu
from jax.sharding import PartitionSpec as P


STEPS = 4
HALO = 64
DIFFUSE = 1.66
LOG2E = math.log2(math.e)
BF = jnp.bfloat16
F32 = jnp.float32

PEERS = 128
SLOTS = 4
COLS = 512
LEV = 45
ROW = 48
BASE = 2 * ROW
BODY = 192
FEAT = BASE + BODY
CHUNK = SLOTS * FEAT // 128
RAD = 128
GH = 56
REACH = STEPS * HALO
WIDE = COLS + 2 * REACH
SPECIES = 4
NEAR = 6
BLOCK = 9
BLOCKS = 2 * LEV // BLOCK
TALL = 64
PART = 40
NT = (((1,), (1,)), ((), ()))
NN = (((1,), (0,)), ((), ()))


def split(x):
    hi = x.astype(BF)
    return hi, (x - hi.astype(F32)).astype(BF)


def dot(a, b, dims):
    return lax.dot_general(a, b, dims, preferred_element_type=F32)


def slot_matrix(position):
    rows = lax.broadcasted_iota(jnp.int32, (COLS, COLS), 0)
    slot = (rows & (PEERS - 1)) * SLOTS + (rows >> 7)
    return jnp.where(slot == position, 1.0, 0.0).astype(BF)


def pack_kernel(*refs):
    sources, outs, scratch = refs[:9], refs[9:13], refs[13:]
    temp, thick, tracers, ground, sun, day, pos, adj, coef = scratch[:9]
    send, right, left, table, bundle, sems, done = scratch[9:]
    copies = [pltpu.make_async_copy(a, b, sems.at[i]) for i, (a, b) in enumerate(zip(sources, scratch))]
    for i in (6, 7, 8, 2, 0, 1, 3, 4, 5):
        copies[i].start()
    stores = [pltpu.make_async_copy(a, b, done.at[i]) for i, (a, b) in enumerate(zip((send, right, left, table), outs))]
    bundle[ROW + LEV : BASE, :] = jnp.zeros((ROW - LEV, COLS), F32)
    spare = BASE + LEV * SPECIES
    bundle[spare:FEAT, :] = jnp.zeros((FEAT - spare, COLS), F32)
    for i in (6, 7, 8):
        copies[i].wait()
    placing = slot_matrix(pos[...])
    column = lax.broadcasted_iota(jnp.int32, (NEAR, COLS), 1)
    reach = (adj[...] - column).astype(F32)
    pad = jnp.zeros((2, COLS), F32)
    both = jnp.concatenate([reach, pad, coef[...], pad], axis=0)
    table[...] = both
    right[BODY : BODY + 16, :] = both[:, COLS - REACH :]
    left[BODY : BODY + 16, :] = both[:, :REACH]
    copies[2].wait()
    for l in range(LEV):
        bundle[BASE + SPECIES * l : BASE + SPECIES * (l + 1), :] = tracers[l]
    right[0:BODY, :] = bundle[BASE:FEAT, COLS - REACH :]
    left[0:BODY, :] = bundle[BASE:FEAT, :REACH]
    for i in (1, 2, 3):
        stores[i].start()
    for i in (0, 1, 3, 4, 5):
        copies[i].wait()
    bundle[0:LEV, :] = temp[...]
    bundle[ROW : ROW + LEV, :] = thick[...]
    sunny = sun[...]
    bundle[LEV : LEV + 1, :] = ground[...]
    bundle[LEV + 1 : LEV + 2, :] = sunny
    bundle[LEV + 2 : LEV + 3, :] = day[...].astype(F32) * sunny
    tail = bundle[256:288, :]
    for k in range(1, 4):
        bundle[256 + 32 * k : 288 + 32 * k, :] = tail
    hi, lo = split(bundle[...])
    packed = dot(placing, hi, NT) + dot(placing, lo, NT)
    lane = lax.broadcasted_iota(jnp.int32, (PEERS, 128), 1) >> 5
    last = jnp.zeros((PEERS, 128), F32)
    for m in range(SLOTS):
        block = packed[m * PEERS : (m + 1) * PEERS, :]
        send[pl.ds(2 * m, PEERS, CHUNK), :] = block[:, 0:128]
        send[pl.ds(2 * m + 1, PEERS, CHUNK), :] = block[:, 128:256]
        last = jnp.where(lane == m, block[:, 256:384], last)
    send[pl.ds(CHUNK - 1, PEERS, CHUNK), :] = last
    stores[0].start()
    for store in stores:
        store.wait()


def pool_kernel(arrived, member, pooled, stage):
    ids = member[...] >> 2
    rows = lax.broadcasted_iota(jnp.int32, (RAD, 128), 0)
    lane = lax.broadcasted_iota(jnp.int32, (PEERS, 128), 1) >> 5
    last = arrived[pl.ds(CHUNK - 1, PEERS, CHUNK), :]
    chosen = []
    for m in range(SLOTS):
        chosen.append(jnp.where(rows == ids[m : m + 1, :], 0.25, 0.0).astype(BF))
        span = slice(m * PEERS, (m + 1) * PEERS)
        stage[span, 0:128] = arrived[pl.ds(2 * m, PEERS, CHUNK), :]
        stage[span, 128:256] = arrived[pl.ds(2 * m + 1, PEERS, CHUNK), :]
        stage[span, 256:384] = jnp.where(lane == m, last, 0.0)
    selector = jnp.concatenate(chosen, axis=1)
    hi, lo = split(stage[...])
    total = dot(selector, hi, NN) + dot(selector, lo, NN)
    pooled[0:128, :] = total[:, 0:128].T
    pooled[128:256, :] = total[:, 128:256].T
    tail = total[:, 256:384].T
    pooled[256:288, :] = tail[0:32] + tail[32:64] + tail[64:96] + tail[96:128]


def weight_kernel(opacity, weights):
    rows = lax.broadcasted_iota(jnp.int32, (128, 128), 0)
    lanes = lax.broadcasted_iota(jnp.int32, (128, 128), 1)
    picks = []
    for s in range(SPECIES):
        lane = jnp.where(rows < BLOCK, SPECIES * rows + s, -1)
        picks.append((lanes == lane) | (lanes == jnp.where(lane < 0, -1, lane + 2 * PART)))
    for s in range(SPECIES):
        lane = jnp.where(rows < BLOCK, SPECIES * rows + s + PART, -1)
        picks.append(lanes == lane)
    picker = jnp.concatenate([jnp.where(p, 1.0, 0.0).astype(BF) for p in picks], axis=0)
    group = lax.broadcasted_iota(jnp.int32, (TALL, 128), 1)
    group = jnp.where(group >= 2 * PART, group - 2 * PART, jnp.where(group >= PART, group - PART, group)) >> 2
    pad = jnp.zeros((TALL - GH, 128), F32)
    for b in range(BLOCKS):
        his, los = [], []
        for s in range(SPECIES):
            level = opacity[s]
            if b:
                level = pltpu.roll(level, 128 - b * BLOCK, 1)
            hi, lo = split(jnp.concatenate([level, pad], axis=0))
            his.append(hi)
            los.append(lo)
        wide = dot(jnp.concatenate(his + los, axis=1), picker, NN)
        for i in range(BLOCK):
            start = (b * BLOCK + i) * TALL
            weights[start : start + TALL, :] = jnp.where(group == i, wide, 0.0).astype(BF)


def flux_kernel(side, own, other, weights, emission, sunshine, mine, theirs, fields, warm, taus, sums, net):
    me = side[0]
    fields[pl.ds(me, 1)] = own[...][None]
    fields[pl.ds(1 - me, 1)] = other[...][None]
    for h in range(2):
        warm[h] = jnp.square(jnp.square(fields[h, 0:ROW, :]))
        fields[h, BASE:FEAT, :] = fields[h, BASE:FEAT, :] * (-DIFFUSE * LOG2E)
    surface = own[40:48, :]
    ground4 = jnp.square(jnp.square(surface[5:6, :]))
    slant = 1.0 / (DIFFUSE * surface[6:7, :])
    slant = jnp.broadcast_to(slant, (GH, RAD))
    insolation = surface[7:8, :]
    emit = jnp.broadcast_to(emission[...], (GH, RAD))
    pad = jnp.zeros((128 - 3 * PART, RAD), F32)
    tall = BLOCK * TALL
    for b in range(BLOCKS):
        h, inner = divmod(b * BLOCK, LEV)
        start = BASE + SPECIES * inner
        part = fields[h, start : start + PART, :]
        hi = part.astype(BF).astype(F32)
        amounts = jnp.concatenate([hi, hi, part - hi, pad], axis=0).astype(BF)
        taus[b * tall : (b + 1) * tall, :] = dot(weights[b * tall : (b + 1) * tall, :], amounts, NN)

    def fold(x):
        return jnp.sum(x.reshape(GH // 8, 8, RAD), axis=0)

    thermal = jnp.zeros((GH, RAD), F32)
    direct = sunshine[...] * insolation
    beam = fold(direct)
    for l in range(2 * LEV):
        h, inner = divmod(l, LEV)
        rows = slice(l * TALL, l * TALL + GH)
        tau = taus[rows, :]
        opaque = 1.0 - jnp.exp2(tau)
        taus[rows, :] = opaque
        source = emit * warm[h, inner : inner + 1, :]
        gain = opaque * (thermal - source)
        thermal = thermal - gain
        direct = direct * jnp.exp2(tau * slant)
        below = fold(direct)
        sums[8 * l : 8 * l + 8, :] = fold(gain) + (beam - below)
        beam = below
    upward = emit * ground4
    for l in range(2 * LEV - 1, -1, -1):
        h, inner = divmod(l, LEV)
        source = emit * warm[h, inner : inner + 1, :]
        gain = taus[l * TALL : l * TALL + GH, :] * (upward - source)
        upward = upward - gain
        sums[8 * l : 8 * l + 8, :] = sums[8 * l : 8 * l + 8, :] + fold(gain)
    for h in range(2):
        total = None
        for k in range(8):
            part = sums[pl.ds(8 * LEV * h + k, LEV, 8), :]
            total = part if total is None else total + part
        net[h, 0:LEV, :] = total
        net[h, LEV:ROW, :] = jnp.zeros((ROW - LEV, RAD), F32)
    mine[...] = net[pl.ds(me, 1)][0]
    theirs[...] = net[pl.ds(1 - me, 1)][0]


def spread_kernel(mine, gotten, own, member, send):
    heat = (mine[...] + gotten[...]) / own[ROW:BASE, :]
    rows = lax.broadcasted_iota(jnp.int32, (ROW, RAD), 0)
    heat = jnp.where(rows < LEV, heat, 0.0)
    gap = jnp.zeros((16, RAD), F32)
    hi, lo = split(jnp.concatenate([heat, gap, heat, gap], axis=0))
    ids = member[...] >> 2
    lanes = lax.broadcasted_iota(jnp.int32, (PEERS, RAD), 1)
    for h in range(2):
        parts = []
        for m in (2 * h, 2 * h + 1):
            selector = jnp.where(lanes == ids[:, m : m + 1], 1.0, 0.0).astype(BF)
            parts.append(dot(selector, hi, NT) + dot(selector, lo, NT))
        send[pl.ds(h, PEERS, 2), :] = jnp.where(lanes < 64, parts[0], parts[1])


def unplace_kernel(returned, pos, heating):
    parts = []
    for h in range(2):
        turned = returned[pl.ds(h, PEERS, 2), :].T
        parts += [turned[0:ROW, :], turned[64 : 64 + ROW, :]]
    hi, lo = split(jnp.concatenate(parts, axis=1))
    placing = slot_matrix(pos[...])
    heating[...] = (dot(hi, placing, NN) + dot(lo, placing, NN))[0:LEV, :]


def mix_kernel(tracers, table, from_left, from_right, mixed, high, low, band, stage):
    spare = LEV * SPECIES
    stage[spare:BODY, :] = jnp.zeros((BODY - spare, COLS), F32)
    for l in range(LEV):
        stage[SPECIES * l : SPECIES * (l + 1), :] = tracers[l]
    parts = (from_left[0:BODY, :], stage[...], from_right[0:BODY, :])
    for part, start in zip(parts, (0, REACH, REACH + COLS)):
        hi, lo = split(part)
        high[0, :, start : start + part.shape[1]] = hi
        low[0, :, start : start + part.shape[1]] = lo
    tables = jnp.concatenate([from_left[BODY:, :], table[...], from_right[BODY:, :]], axis=1)
    shifted = pltpu.roll(tables, WIDE - HALO, 1)
    rows = lax.broadcasted_iota(jnp.int32, (256, 128), 0).astype(F32)
    lanes = lax.broadcasted_iota(jnp.int32, (1, 128), 1).astype(F32)

    def build(source, k):
        part = source[:, k * 128 : (k + 1) * 128]
        blend = jnp.where(rows == lanes + HALO, 1.0 - jnp.sum(part[8:14, :], axis=0, keepdims=True), 0.0)
        for n in range(NEAR):
            blend = blend + jnp.where(rows == lanes + part[n : n + 1, :], part[8 + n : 9 + n, :], 0.0)
        return split(blend)

    for k in range(7):
        hi, lo = build(shifted, k)
        band[0, 0, k] = hi
        band[0, 1, k] = lo
    for k in range(6):
        hi, lo = build(tables, k + 1)
        band[1, 0, k] = hi
        band[1, 1, k] = lo
    for step in range(STEPS):
        now, later = step % 2, (step + 1) % 2
        tiles = 7 - step
        first = step // 2
        for k in range(tiles):
            window = slice(k * 128, k * 128 + 256)
            bh, bl = band[now, 0, k + first], band[now, 1, k + first]
            xh, xl = high[now, :, window], low[now, :, window]
            new = dot(xh, bh, NN) + (dot(xh, bl, NN) + dot(xl, bh, NN))
            if step < STEPS - 1:
                hi, lo = split(new)
                high[later, :, k * 128 : (k + 1) * 128] = hi
                low[later, :, k * 128 : (k + 1) * 128] = lo
            else:
                for l in range(LEV):
                    mixed[l, :, k * 128 : (k + 1) * 128] = new[SPECIES * l : SPECIES * (l + 1), :]


def shape(*dims):
    return jax.ShapeDtypeStruct(dims, F32)


def call(kernel, out_shape, scratch, vmem_limit_bytes=16 << 20, **specs):
    return pl.pallas_call(
        kernel,
        out_shape=out_shape,
        scratch_shapes=scratch,
        compiler_params=pltpu.CompilerParams(vmem_limit_bytes=vmem_limit_bytes),
        **specs,
    )


def per_device(
    stratum_warmth_anomaly,
    pressure_depth,
    absorber_amounts,
    ground_warmth_anomaly,
    sun_elevation_factor,
    daytime_mask,
    dispatch_position,
    arrival_membership,
    adjacency_table,
    blending_coefficient,
    opacity_table,
    emission_share,
    sunshine_share,
):
    n = lax.axis_size("grp")
    up = [(i, (i + 1) % n) for i in range(n)]
    down = [(j, i) for i, j in up]
    swap = [(0, 1), (1, 0)]
    halo_rows = BODY + 16
    tracers = jnp.transpose(absorber_amounts, (1, 0, 2))

    hbm = pl.BlockSpec(memory_space=pltpu.HBM)
    packed = (shape(PEERS * CHUNK, 128), shape(halo_rows, REACH), shape(halo_rows, REACH), shape(16, COLS))
    given = ((LEV, COLS), (LEV, COLS), (LEV, SPECIES, COLS), (1, COLS), (1, COLS))
    send, right, left, table = call(
        pack_kernel,
        packed,
        [pltpu.VMEM(dims, F32) for dims in given]
        + [pltpu.VMEM((rows, COLS), jnp.int32) for rows in (1, 1, NEAR)]
        + [pltpu.VMEM((NEAR, COLS), F32)]
        + [pltpu.VMEM(out.shape, F32) for out in packed]
        + [pltpu.VMEM((384, COLS), F32), pltpu.SemaphoreType.DMA((9,)), pltpu.SemaphoreType.DMA((4,))],
        in_specs=[hbm] * 9,
        out_specs=[hbm] * 4,
        vmem_limit_bytes=60 << 20,
    )(
        stratum_warmth_anomaly,
        pressure_depth,
        tracers,
        ground_warmth_anomaly[None],
        sun_elevation_factor[None],
        daytime_mask[None],
        dispatch_position,
        adjacency_table,
        blending_coefficient,
    )
    arrived = lax.all_to_all(
        send.reshape(PEERS * CHUNK, 1, 128), "grp", split_axis=0, concat_axis=0, tiled=True
    )
    members = arrival_membership.reshape(PEERS, SLOTS)
    opacity = jnp.pad(opacity_table, ((0, 0), (0, 0), (0, 128 - 2 * LEV)))
    weights = call(weight_kernel, jax.ShapeDtypeStruct((2 * LEV * TALL, 128), BF), [])(opacity)
    side = lax.axis_index("sec").astype(jnp.int32)[None]
    arrived, members, members_t, weights, emission, sunshine, side = lax.optimization_barrier(
        (arrived, members, members.T, weights, emission_share[:, None], sunshine_share[:, None], side)
    )

    pooled = call(pool_kernel, shape(FEAT, RAD), [pltpu.VMEM((COLS, 384), F32)])(
        arrived.reshape(PEERS * CHUNK, 128), members_t
    )
    other = lax.ppermute(pooled, "sec", swap)
    mine, theirs = call(
        flux_kernel,
        (shape(ROW, RAD), shape(ROW, RAD)),
        [
            pltpu.VMEM((2, FEAT, RAD), F32),
            pltpu.VMEM((2, ROW, RAD), F32),
            pltpu.VMEM((2 * LEV * TALL, RAD), F32),
            pltpu.VMEM((2 * LEV * 8, RAD), F32),
            pltpu.VMEM((2, ROW, RAD), F32),
        ],
        in_specs=[pl.BlockSpec(memory_space=pltpu.SMEM)] + [pl.BlockSpec(memory_space=pltpu.VMEM)] * 5,
    )(side, pooled, other, weights, emission, sunshine)
    mine, theirs, right, left = lax.optimization_barrier((mine, theirs, right, left))
    gotten = lax.ppermute(theirs, "sec", swap)
    from_left = lax.ppermute(right, "grp", up)
    from_right = lax.ppermute(left, "grp", down)
    back = call(spread_kernel, shape(PEERS * 2, 128), [])(mine, gotten, pooled, members)
    returned = lax.all_to_all(
        back.reshape(PEERS * 2, 1, 128), "grp", split_axis=0, concat_axis=0, tiled=True
    ).reshape(PEERS * 2, 128)
    mixed = call(
        mix_kernel,
        shape(LEV, SPECIES, COLS),
        [
            pltpu.VMEM((2, BODY, WIDE), BF),
            pltpu.VMEM((2, BODY, WIDE), BF),
            pltpu.VMEM((2, 2, 7, 256, 128), BF),
            pltpu.VMEM((BODY, COLS), F32),
        ],
    )(tracers, table, from_left, from_right)
    returned, mixed = lax.optimization_barrier((returned, mixed))
    heating = call(unplace_kernel, shape(LEV, COLS), [])(returned, dispatch_position)
    return (heating, jnp.transpose(mixed, (1, 0, 2)))


def solution(mesh):
    in_specs = (
        P("sec", "grp"),
        P("sec", "grp"),
        P(None, "sec", "grp"),
        P("grp"),
        P("grp"),
        P("grp"),
        P("grp", None),
        P("grp", None),
        P(None, "grp"),
        P(None, "grp"),
        P(None, "sec", None),
        P("sec"),
        P("sec"),
    )
    out_specs = (P("sec", "grp"), P(None, "sec", "grp"))
    return jax.shard_map(
        per_device, mesh=mesh, in_specs=in_specs, out_specs=out_specs, check_vma=False
    )
```

```python
import math

import jax
import jax.numpy as jnp
from jax import lax
from jax.experimental import pallas as pl
from jax.experimental.pallas import tpu as pltpu
from jax.sharding import PartitionSpec as P


STEPS = 4
HALO = 64
DIFFUSE = 1.66
LOG2E = math.log2(math.e)
BF = jnp.bfloat16
F32 = jnp.float32

PEERS = 128
SLOTS = 4
COLS = 512
LEV = 45
ROW = 48
BASE = 2 * ROW
BODY = 192
FEAT = BASE + BODY
CHUNK = SLOTS * FEAT // 128
RAD = 128
GH = 56
REACH = STEPS * HALO
WIDE = COLS + 2 * REACH
SPECIES = 4
NEAR = 6
BLOCK = 9
BLOCKS = LEV // BLOCK
GALL = 2 * GH
PART = 40
NT = (((1,), (1,)), ((), ()))
NN = (((1,), (0,)), ((), ()))


def split(x):
    hi = x.astype(BF)
    return hi, (x - hi.astype(F32)).astype(BF)


def dot(a, b, dims):
    return lax.dot_general(a, b, dims, preferred_element_type=F32)


def slot_matrix(position):
    rows = lax.broadcasted_iota(jnp.int32, (COLS, COLS), 0)
    slot = (rows & (PEERS - 1)) * SLOTS + (rows >> 7)
    return jnp.where(slot == position, 1.0, 0.0).astype(BF)


def pack_kernel(*refs):
    sources, outs, scratch = refs[:9], refs[9:13], refs[13:]
    temp, thick, tracers, ground, sun, day, pos, adj, coef = scratch[:9]
    send, right, left, table, bundle, sems, done = scratch[9:]
    copies = [pltpu.make_async_copy(a, b, sems.at[i]) for i, (a, b) in enumerate(zip(sources, scratch))]
    for i in (6, 7, 8, 2, 0, 1, 3, 4, 5):
        copies[i].start()
    stores = [pltpu.make_async_copy(a, b, done.at[i]) for i, (a, b) in enumerate(zip((send, right, left, table), outs))]
    bundle[ROW + LEV : BASE, :] = jnp.zeros((ROW - LEV, COLS), F32)
    spare = BASE + LEV * SPECIES
    bundle[spare:FEAT, :] = jnp.zeros((FEAT - spare, COLS), F32)
    for i in (6, 7, 8):
        copies[i].wait()
    placing = slot_matrix(pos[...])
    column = lax.broadcasted_iota(jnp.int32, (NEAR, COLS), 1)
    reach = (adj[...] - column).astype(F32)
    pad = jnp.zeros((2, COLS), F32)
    both = jnp.concatenate([reach, pad, coef[...], pad], axis=0)
    table[...] = both
    right[BODY : BODY + 16, :] = both[:, COLS - REACH :]
    left[BODY : BODY + 16, :] = both[:, :REACH]
    copies[2].wait()
    for l in range(LEV):
        bundle[BASE + SPECIES * l : BASE + SPECIES * (l + 1), :] = tracers[l]
    right[0:BODY, :] = bundle[BASE:FEAT, COLS - REACH :]
    left[0:BODY, :] = bundle[BASE:FEAT, :REACH]
    for i in (1, 2, 3):
        stores[i].start()
    for i in (0, 1, 3, 4, 5):
        copies[i].wait()
    bundle[0:LEV, :] = temp[...]
    bundle[ROW : ROW + LEV, :] = thick[...]
    sunny = sun[...]
    bundle[LEV : LEV + 1, :] = ground[...]
    bundle[LEV + 1 : LEV + 2, :] = sunny
    bundle[LEV + 2 : LEV + 3, :] = day[...].astype(F32) * sunny
    hi, lo = split(bundle[0:256, :])
    packed = dot(placing, hi, NT) + dot(placing, lo, NT)
    tail = bundle[256:288, :]
    hi = tail.astype(BF).astype(F32)
    tails = dot(placing, jnp.concatenate([hi] * SLOTS + [tail - hi] * SLOTS, axis=0).astype(BF), NT)
    tails = tails[:, 0:128] + tails[:, 128:256]
    lane = lax.broadcasted_iota(jnp.int32, (PEERS, 128), 1) >> 5
    last = jnp.zeros((PEERS, 128), F32)
    for m in range(SLOTS):
        block = packed[m * PEERS : (m + 1) * PEERS, :]
        send[pl.ds(2 * m, PEERS, CHUNK), :] = block[:, 0:128]
        send[pl.ds(2 * m + 1, PEERS, CHUNK), :] = block[:, 128:256]
        last = jnp.where(lane == m, tails[m * PEERS : (m + 1) * PEERS, :], last)
    send[pl.ds(CHUNK - 1, PEERS, CHUNK), :] = last
    stores[0].start()
    for store in stores:
        store.wait()


def weight_kernel(side, own, other, weights, emit, shine, full):
    me = side[0]
    full[pl.ds(me, 1)] = own[...][None]
    full[pl.ds(1 - me, 1)] = other[...][None]
    shift = lax.rem(128 - LEV * me, 128)
    tables = [jnp.concatenate([full[0, s], full[1, s]], axis=0) for s in range(SPECIES)]
    emit[...] = jnp.broadcast_to(tables[0][:, 2 * LEV : 2 * LEV + 1], (GALL, RAD))
    shine[...] = jnp.broadcast_to(tables[0][:, 2 * LEV + 1 : 2 * LEV + 2], (GALL, RAD))
    tables = [pltpu.roll(table, shift, 1) for table in tables]
    rows = lax.broadcasted_iota(jnp.int32, (128, 128), 0)
    lanes = lax.broadcasted_iota(jnp.int32, (128, 128), 1)
    picks = []
    for s in range(SPECIES):
        lane = jnp.where(rows < BLOCK, SPECIES * rows + s, -1)
        picks.append((lanes == lane) | (lanes == jnp.where(lane < 0, -1, lane + 2 * PART)))
    for s in range(SPECIES):
        lane = jnp.where(rows < BLOCK, SPECIES * rows + s + PART, -1)
        picks.append(lanes == lane)
    picker = jnp.concatenate([jnp.where(p, 1.0, 0.0).astype(BF) for p in picks], axis=0)
    group = lax.broadcasted_iota(jnp.int32, (GALL, 128), 1)
    group = jnp.where(group >= 2 * PART, group - 2 * PART, jnp.where(group >= PART, group - PART, group)) >> 2
    for b in range(BLOCKS):
        his, los = [], []
        for table in tables:
            hi, lo = split(pltpu.roll(table, 128 - b * BLOCK, 1) if b else table)
            his.append(hi)
            los.append(lo)
        wide = dot(jnp.concatenate(his + los, axis=1), picker, NN)
        for i in range(BLOCK):
            start = (b * BLOCK + i) * GALL
            weights[start : start + GALL, :] = jnp.where(group == i, wide, 0.0).astype(BF)


def fold(x):
    return jnp.sum(x.reshape(GH // 8, 8, RAD), axis=0)


def span(level, half):
    return slice(level * GALL + half * GH, level * GALL + (half + 1) * GH)


def first_kernel(side, arrived, member, weights, emit, shine, opaque, passing, warm, thick, sums, edge, stage, pooled):
    ids = member[...] >> 2
    rows = lax.broadcasted_iota(jnp.int32, (RAD, 128), 0)
    lane = lax.broadcasted_iota(jnp.int32, (PEERS, 128), 1) >> 5
    last = arrived[pl.ds(CHUNK - 1, PEERS, CHUNK), :]
    chosen = []
    for m in range(SLOTS):
        chosen.append(jnp.where(rows == ids[m : m + 1, :], 0.25, 0.0).astype(BF))
        part = slice(m * PEERS, (m + 1) * PEERS)
        stage[part, 0:128] = arrived[pl.ds(2 * m, PEERS, CHUNK), :]
        stage[part, 128:256] = arrived[pl.ds(2 * m + 1, PEERS, CHUNK), :]
        stage[part, 256:384] = jnp.where(lane == m, last, 0.0)
    selector = jnp.concatenate(chosen, axis=1)
    hi, lo = split(stage[...])
    total = dot(selector, hi, NN) + dot(selector, lo, NN)
    pooled[0:128, :] = total[:, 0:128].T
    pooled[128:256, :] = total[:, 128:256].T
    tail = total[:, 256:384].T
    pooled[256:288, :] = tail[0:32] + tail[32:64] + tail[64:96] + tail[96:128]
    surface = pooled[40:48, :]
    slant = jnp.broadcast_to(1.0 / (DIFFUSE * surface[6:7, :]), (GH, RAD))
    warm[...] = jnp.square(jnp.square(pooled[0:ROW, :]))
    thick[...] = pooled[ROW:BASE, :]
    pooled[BASE:FEAT, :] = pooled[BASE:FEAT, :] * (-DIFFUSE * LOG2E)
    pad = jnp.zeros((128 - 3 * PART, RAD), F32)
    tall = BLOCK * GALL
    for b in range(BLOCKS):
        start = BASE + SPECIES * BLOCK * b
        part = pooled[start : start + PART, :]
        hi = part.astype(BF).astype(F32)
        amounts = jnp.concatenate([hi, hi, part - hi, pad], axis=0).astype(BF)
        passing[b * tall : (b + 1) * tall, :] = dot(weights[b * tall : (b + 1) * tall, :], amounts, NN)
    me = side[0]

    @pl.when(me == 0)
    def _():
        for half in range(2):
            part = slice(half * GH, (half + 1) * GH)
            thermal = jnp.zeros((GH, RAD), F32)
            direct = shine[part, :] * surface[7:8, :]
            beam = fold(direct)
            for l in range(LEV):
                tau = passing[span(l, half), :]
                kept = 1.0 - jnp.exp2(tau)
                opaque[span(l, half), :] = kept
                gain = kept * (thermal - emit[part, :] * warm[l : l + 1, :])
                thermal = thermal - gain
                direct = direct * jnp.exp2(tau * slant)
                below = fold(direct)
                change = fold(gain) + (beam - below)
                beam = below
                row = slice(8 * l, 8 * l + 8)
                sums[row, :] = sums[row, :] + change if half else change
            edge[part, :] = thermal
            edge[GALL + half * GH : GALL + (half + 1) * GH, :] = direct

    @pl.when(me == 1)
    def _():
        ground = jnp.square(jnp.square(surface[5:6, :]))
        for half in range(2):
            part = slice(half * GH, (half + 1) * GH)
            upward = emit[part, :] * ground
            for l in range(LEV - 1, -1, -1):
                tau = passing[span(l, half), :]
                kept = 1.0 - jnp.exp2(tau)
                opaque[span(l, half), :] = kept
                passing[span(l, half), :] = jnp.exp2(tau * slant)
                gain = kept * (upward - emit[part, :] * warm[l : l + 1, :])
                upward = upward - gain
                row = slice(8 * l, 8 * l + 8)
                sums[row, :] = sums[row, :] + fold(gain) if half else fold(gain)
            edge[part, :] = upward
        edge[GALL:, :] = jnp.zeros((GALL, RAD), F32)


def second_kernel(side, gotten, opaque, passing, warm, thick, sums, emit, member, send, net):
    me = side[0]

    @pl.when(me == 0)
    def _():
        for half in range(2):
            part = slice(half * GH, (half + 1) * GH)
            upward = gotten[part, :]
            for l in range(LEV - 1, -1, -1):
                gain = opaque[span(l, half), :] * (upward - emit[part, :] * warm[l : l + 1, :])
                upward = upward - gain
                row = slice(8 * l, 8 * l + 8)
                net[row, :] = (net if half else sums)[row, :] + fold(gain)

    @pl.when(me == 1)
    def _():
        for half in range(2):
            part = slice(half * GH, (half + 1) * GH)
            thermal = gotten[part, :]
            direct = gotten[GALL + half * GH : GALL + (half + 1) * GH, :]
            beam = fold(direct)
            for l in range(LEV):
                gain = opaque[span(l, half), :] * (thermal - emit[part, :] * warm[l : l + 1, :])
                thermal = thermal - gain
                direct = direct * passing[span(l, half), :]
                below = fold(direct)
                row = slice(8 * l, 8 * l + 8)
                net[row, :] = (net if half else sums)[row, :] + fold(gain) + (beam - below)
                beam = below

    total = None
    for k in range(8):
        part = net[pl.ds(k, LEV, 8), :]
        total = part if total is None else total + part
    heat = jnp.concatenate([total / thick[0:LEV, :], jnp.zeros((ROW - LEV, RAD), F32)], axis=0)
    gap = jnp.zeros((16, RAD), F32)
    hi, lo = split(jnp.concatenate([heat, gap, heat, gap], axis=0))
    ids = member[...] >> 2
    lanes = lax.broadcasted_iota(jnp.int32, (PEERS, RAD), 1)
    for h in range(2):
        parts = []
        for m in (2 * h, 2 * h + 1):
            selector = jnp.where(lanes == ids[:, m : m + 1], 1.0, 0.0).astype(BF)
            parts.append(dot(selector, hi, NT) + dot(selector, lo, NT))
        send[pl.ds(h, PEERS, 2), :] = jnp.where(lanes < 64, parts[0], parts[1])


def unplace_kernel(returned, pos, heating):
    parts = []
    for h in range(2):
        turned = returned[pl.ds(h, PEERS, 2), :].T
        parts += [turned[0:ROW, :], turned[64 : 64 + ROW, :]]
    hi, lo = split(jnp.concatenate(parts, axis=1))
    placing = slot_matrix(pos[...])
    heating[...] = (dot(hi, placing, NN) + dot(lo, placing, NN))[0:LEV, :]


def mix_kernel(tracers, table, from_left, from_right, mixed, high, low, band, stage):
    spare = LEV * SPECIES
    stage[spare:BODY, :] = jnp.zeros((BODY - spare, COLS), F32)
    for l in range(LEV):
        stage[SPECIES * l : SPECIES * (l + 1), :] = tracers[l]
    parts = (from_left[0:BODY, :], stage[...], from_right[0:BODY, :])
    for part, start in zip(parts, (0, REACH, REACH + COLS)):
        hi, lo = split(part)
        high[0, :, start : start + part.shape[1]] = hi
        low[0, :, start : start + part.shape[1]] = lo
    tables = jnp.concatenate([from_left[BODY:, :], table[...], from_right[BODY:, :]], axis=1)
    shifted = pltpu.roll(tables, WIDE - HALO, 1)
    rows = lax.broadcasted_iota(jnp.int32, (256, 128), 0).astype(F32)
    lanes = lax.broadcasted_iota(jnp.int32, (1, 128), 1).astype(F32)

    def build(source, k):
        part = source[:, k * 128 : (k + 1) * 128]
        blend = jnp.where(rows == lanes + HALO, 1.0 - jnp.sum(part[8:14, :], axis=0, keepdims=True), 0.0)
        for n in range(NEAR):
            blend = blend + jnp.where(rows == lanes + part[n : n + 1, :], part[8 + n : 9 + n, :], 0.0)
        return split(blend)

    for k in range(7):
        hi, lo = build(shifted, k)
        band[0, 0, k] = hi
        band[0, 1, k] = lo
    for k in range(6):
        hi, lo = build(tables, k + 1)
        band[1, 0, k] = hi
        band[1, 1, k] = lo
    for step in range(STEPS):
        now, later = step % 2, (step + 1) % 2
        tiles = 7 - step
        first = step // 2
        for k in range(tiles):
            window = slice(k * 128, k * 128 + 256)
            bh, bl = band[now, 0, k + first], band[now, 1, k + first]
            xh, xl = high[now, :, window], low[now, :, window]
            new = dot(xh, bh, NN) + (dot(xh, bl, NN) + dot(xl, bh, NN))
            if step < STEPS - 1:
                hi, lo = split(new)
                high[later, :, k * 128 : (k + 1) * 128] = hi
                low[later, :, k * 128 : (k + 1) * 128] = lo
            else:
                for l in range(LEV):
                    mixed[l, :, k * 128 : (k + 1) * 128] = new[SPECIES * l : SPECIES * (l + 1), :]


def shape(*dims):
    return jax.ShapeDtypeStruct(dims, F32)


def call(kernel, out_shape, scratch, vmem_limit_bytes=16 << 20, **specs):
    return pl.pallas_call(
        kernel,
        out_shape=out_shape,
        scratch_shapes=scratch,
        compiler_params=pltpu.CompilerParams(vmem_limit_bytes=vmem_limit_bytes),
        **specs,
    )


def per_device(
    stratum_warmth_anomaly,
    pressure_depth,
    absorber_amounts,
    ground_warmth_anomaly,
    sun_elevation_factor,
    daytime_mask,
    dispatch_position,
    arrival_membership,
    adjacency_table,
    blending_coefficient,
    opacity_table,
    emission_share,
    sunshine_share,
):
    n = lax.axis_size("grp")
    up = [(i, (i + 1) % n) for i in range(n)]
    down = [(j, i) for i, j in up]
    swap = [(0, 1), (1, 0)]
    halo_rows = BODY + 16
    tracers = jnp.transpose(absorber_amounts, (1, 0, 2))

    hbm = pl.BlockSpec(memory_space=pltpu.HBM)
    packed = (shape(PEERS * CHUNK, 128), shape(halo_rows, REACH), shape(halo_rows, REACH), shape(16, COLS))
    given = ((LEV, COLS), (LEV, COLS), (LEV, SPECIES, COLS), (1, COLS), (1, COLS))
    send, right, left, table = call(
        pack_kernel,
        packed,
        [pltpu.VMEM(dims, F32) for dims in given]
        + [pltpu.VMEM((rows, COLS), jnp.int32) for rows in (1, 1, NEAR)]
        + [pltpu.VMEM((NEAR, COLS), F32)]
        + [pltpu.VMEM(out.shape, F32) for out in packed]
        + [pltpu.VMEM((FEAT, COLS), F32), pltpu.SemaphoreType.DMA((9,)), pltpu.SemaphoreType.DMA((4,))],
        in_specs=[hbm] * 9,
        out_specs=[hbm] * 4,
        vmem_limit_bytes=60 << 20,
    )(
        stratum_warmth_anomaly,
        pressure_depth,
        tracers,
        ground_warmth_anomaly[None],
        sun_elevation_factor[None],
        daytime_mask[None],
        dispatch_position,
        adjacency_table,
        blending_coefficient,
    )
    from_left = lax.ppermute(right, "grp", up)
    from_right = lax.ppermute(left, "grp", down)
    arrived = lax.all_to_all(send.reshape(PEERS * CHUNK, 1, 128), "grp", split_axis=0, concat_axis=0, tiled=True)
    mixed = call(
        mix_kernel,
        shape(LEV, SPECIES, COLS),
        [
            pltpu.VMEM((2, BODY, WIDE), BF),
            pltpu.VMEM((2, BODY, WIDE), BF),
            pltpu.VMEM((2, 2, 7, 256, 128), BF),
            pltpu.VMEM((BODY, COLS), F32),
        ],
    )(tracers, table, from_left, from_right)
    members = arrival_membership.reshape(PEERS, SLOTS)
    side = lax.axis_index("sec").astype(jnp.int32)[None]
    shares = jnp.stack([emission_share, sunshine_share], axis=-1)[None]
    spare = 128 - 2 * LEV
    opacity = jnp.concatenate([opacity_table, jnp.pad(shares, ((0, SPECIES - 1), (0, 0), (0, spare - 2)))], axis=2)
    whole = pl.BlockSpec(memory_space=pltpu.VMEM)
    scalar = pl.BlockSpec(memory_space=pltpu.SMEM)
    rows = LEV * GALL
    weights, emit, shine = call(
        weight_kernel,
        (jax.ShapeDtypeStruct((rows, 128), BF), shape(GALL, RAD), shape(GALL, RAD)),
        [pltpu.VMEM((2, SPECIES, GH, 128), F32)],
        in_specs=[scalar] + [whole] * 2,
    )(side, opacity, lax.ppermute(opacity, "sec", swap))
    arrived, mixed, members, members_t, weights, emit, shine, side = lax.optimization_barrier(
        (arrived, mixed, members, members.T, weights, emit, shine, side)
    )
    opaque, passing, warm, thick, sums, edge = call(
        first_kernel,
        (
            shape(rows, RAD),
            shape(rows, RAD),
            shape(ROW, RAD),
            shape(ROW, RAD),
            shape(8 * LEV, RAD),
            shape(2 * GALL, RAD),
        ),
        [pltpu.VMEM((COLS, 384), F32), pltpu.VMEM((FEAT, RAD), F32)],
        in_specs=[scalar] + [whole] * 5,
    )(side, arrived.reshape(PEERS * CHUNK, 128), members_t, weights, emit, shine)
    gotten = lax.ppermute(edge, "sec", swap)
    back = call(
        second_kernel, shape(PEERS * 2, 128), [pltpu.VMEM((8 * LEV, RAD), F32)], in_specs=[scalar] + [whole] * 8
    )(side, gotten, opaque, passing, warm, thick, sums, emit, members)
    returned = lax.all_to_all(
        back.reshape(PEERS * 2, 1, 128), "grp", split_axis=0, concat_axis=0, tiled=True
    ).reshape(PEERS * 2, 128)
    heating = call(unplace_kernel, shape(LEV, COLS), [])(returned, dispatch_position)
    return (heating, jnp.transpose(mixed, (1, 0, 2)))


def solution(mesh):
    in_specs = (
        P("sec", "grp"),
        P("sec", "grp"),
        P(None, "sec", "grp"),
        P("grp"),
        P("grp"),
        P("grp"),
        P("grp", None),
        P("grp", None),
        P(None, "grp"),
        P(None, "grp"),
        P(None, "sec", None),
        P("sec"),
        P("sec"),
    )
    out_specs = (P("sec", "grp"), P(None, "sec", "grp"))
    return jax.shard_map(
        per_device, mesh=mesh, in_specs=in_specs, out_specs=out_specs, check_vma=False
    )
```

```python
import math

import jax
import jax.numpy as jnp
from jax import lax
from jax.experimental import pallas as pl
from jax.experimental.pallas import tpu as pltpu
from jax.sharding import PartitionSpec as P


STEPS = 4
HALO = 64
DIFFUSE = 1.66
LOG2E = math.log2(math.e)
BF = jnp.bfloat16
F32 = jnp.float32

PEERS = 128
SLOTS = 4
COLS = 512
LEV = 45
ROW = 48
BASE = 2 * ROW
BODY = 192
FEAT = BASE + BODY
CHUNK = SLOTS * FEAT // 128
RAD = 128
GH = 56
REACH = STEPS * HALO
WIDE = COLS + 2 * REACH
SPECIES = 4
NEAR = 6
BLOCK = 9
BLOCKS = LEV // BLOCK
GALL = 2 * GH
PART = 40
NT = (((1,), (1,)), ((), ()))
NN = (((1,), (0,)), ((), ()))


def split(x):
    hi = x.astype(BF)
    return hi, (x - hi.astype(F32)).astype(BF)


def dot(a, b, dims):
    return lax.dot_general(a, b, dims, preferred_element_type=F32)


def slot_matrix(position):
    rows = lax.broadcasted_iota(jnp.int32, (COLS, COLS), 0)
    slot = (rows & (PEERS - 1)) * SLOTS + (rows >> 7)
    return jnp.where(slot == position, 1.0, 0.0).astype(BF)


def mixing_table(adj, coef):
    column = lax.broadcasted_iota(jnp.int32, (NEAR, COLS), 1)
    pad = jnp.zeros((2, COLS), F32)
    return jnp.concatenate([(adj[...] - column).astype(F32), pad, coef[...], pad], axis=0)


def pack_kernel(*refs):
    sources, outs, scratch = refs[:9], refs[9:12], refs[12:]
    temp, thick, tracers, ground, sun, day, pos, adj, coef = scratch[:9]
    send, right, left, bundle, sems, done = scratch[9:]
    copies = [pltpu.make_async_copy(a, b, sems.at[i]) for i, (a, b) in enumerate(zip(sources, scratch))]
    for i in (6, 7, 8, 2, 0, 1, 3, 4, 5):
        copies[i].start()
    stores = [pltpu.make_async_copy(a, b, done.at[i]) for i, (a, b) in enumerate(zip((send, right, left), outs))]
    bundle[ROW + LEV : BASE, :] = jnp.zeros((ROW - LEV, COLS), F32)
    spare = BASE + LEV * SPECIES
    bundle[spare:FEAT, :] = jnp.zeros((FEAT - spare, COLS), F32)
    for i in (6, 7, 8):
        copies[i].wait()
    placing = slot_matrix(pos[...])
    both = mixing_table(adj, coef)
    right[BODY : BODY + 16, :] = both[:, COLS - REACH :]
    left[BODY : BODY + 16, :] = both[:, :REACH]
    copies[2].wait()
    for l in range(LEV):
        bundle[BASE + SPECIES * l : BASE + SPECIES * (l + 1), :] = tracers[l]
    right[0:BODY, :] = bundle[BASE:FEAT, COLS - REACH :]
    left[0:BODY, :] = bundle[BASE:FEAT, :REACH]
    for i in (1, 2):
        stores[i].start()
    for i in (0, 1, 3, 4, 5):
        copies[i].wait()
    bundle[0:LEV, :] = temp[...]
    bundle[ROW : ROW + LEV, :] = thick[...]
    sunny = sun[...]
    bundle[LEV : LEV + 1, :] = ground[...]
    bundle[LEV + 1 : LEV + 2, :] = sunny
    bundle[LEV + 2 : LEV + 3, :] = day[...].astype(F32) * sunny
    hi, lo = split(bundle[0:256, :])
    packed = dot(placing, hi, NT) + dot(placing, lo, NT)
    tail = bundle[256:288, :]
    hi = tail.astype(BF).astype(F32)
    tails = dot(placing, jnp.concatenate([hi] * SLOTS + [tail - hi] * SLOTS, axis=0).astype(BF), NT)
    tails = tails[:, 0:128] + tails[:, 128:256]
    lane = lax.broadcasted_iota(jnp.int32, (PEERS, 128), 1) >> 5
    last = jnp.zeros((PEERS, 128), F32)
    for m in range(SLOTS):
        block = packed[m * PEERS : (m + 1) * PEERS, :]
        send[pl.ds(2 * m, PEERS, CHUNK), :] = block[:, 0:128]
        send[pl.ds(2 * m + 1, PEERS, CHUNK), :] = block[:, 128:256]
        last = jnp.where(lane == m, tails[m * PEERS : (m + 1) * PEERS, :], last)
    send[pl.ds(CHUNK - 1, PEERS, CHUNK), :] = last
    stores[0].start()
    for store in stores:
        store.wait()


def join_kernel(opacity, emission, sunshine, joined):
    rows = lax.broadcasted_iota(jnp.int32, (GH, GH), 0)
    lanes = lax.broadcasted_iota(jnp.int32, (GH, GH), 1)
    for s in range(SPECIES):
        joined[s] = jnp.zeros((GH, 128), F32)
        joined[s, :, 0 : 2 * LEV] = opacity[s]
    for k, share in enumerate((emission, sunshine)):
        square = jnp.where(rows == lanes, jnp.broadcast_to(share[...], (GH, GH)), 0.0)
        joined[0, :, 2 * LEV + k : 2 * LEV + k + 1] = jnp.sum(square, axis=1, keepdims=True)


def weight_kernel(side, own, other, member, weights, emit, shine, spread, full):
    ids = (member[...] >> 2).astype(F32)
    spots = lax.broadcasted_iota(jnp.int32, (128, RAD), 1).astype(F32)
    for k in range(SLOTS):
        part = slice(k * 128, (k + 1) * 128)
        column = jnp.broadcast_to(ids[:, part], (128, 128)).T
        spread[part, :] = jnp.where(column == spots, 1.0, 0.0).astype(BF)
    me = side[0]
    full[pl.ds(me, 1)] = own[...][None]
    full[pl.ds(1 - me, 1)] = other[...][None]
    shift = lax.rem(128 - LEV * me, 128)
    tables = [jnp.concatenate([full[0, s], full[1, s]], axis=0) for s in range(SPECIES)]
    emit[...] = jnp.broadcast_to(tables[0][:, 2 * LEV : 2 * LEV + 1], (GALL, RAD))
    shine[...] = jnp.broadcast_to(tables[0][:, 2 * LEV + 1 : 2 * LEV + 2], (GALL, RAD))
    tables = [pltpu.roll(table, shift, 1) for table in tables]
    rows = lax.broadcasted_iota(jnp.int32, (128, 128), 0)
    lanes = lax.broadcasted_iota(jnp.int32, (128, 128), 1)
    picks = []
    for s in range(SPECIES):
        lane = jnp.where(rows < BLOCK, SPECIES * rows + s, -1)
        picks.append((lanes == lane) | (lanes == jnp.where(lane < 0, -1, lane + 2 * PART)))
    for s in range(SPECIES):
        lane = jnp.where(rows < BLOCK, SPECIES * rows + s + PART, -1)
        picks.append(lanes == lane)
    picker = jnp.concatenate([jnp.where(p, 1.0, 0.0).astype(BF) for p in picks], axis=0)
    group = lax.broadcasted_iota(jnp.int32, (GALL, 128), 1)
    group = jnp.where(group >= 2 * PART, group - 2 * PART, jnp.where(group >= PART, group - PART, group)) >> 2
    for b in range(BLOCKS):
        his, los = [], []
        for table in tables:
            hi, lo = split(pltpu.roll(table, 128 - b * BLOCK, 1) if b else table)
            his.append(hi)
            los.append(lo)
        wide = dot(jnp.concatenate(his + los, axis=1), picker, NN)
        for i in range(BLOCK):
            start = (b * BLOCK + i) * GALL
            weights[start : start + GALL, :] = jnp.where(group == i, wide, 0.0).astype(BF)


def fold(x):
    return jnp.sum(x.reshape(GH // 8, 8, RAD), axis=0)


def span(level, half):
    return slice(level * GALL + half * GH, level * GALL + (half + 1) * GH)


def first_kernel(side, arrived, member, weights, emit, shine, trans, glow, passing, thick, sums, edge, stage, pooled, warm):
    lane = lax.broadcasted_iota(jnp.int32, (PEERS, 128), 1) >> 5
    last = arrived[pl.ds(CHUNK - 1, PEERS, CHUNK), :]
    for m in range(SLOTS):
        part = pl.ds(m, PEERS, SLOTS)
        stage[0, part, :] = arrived[pl.ds(2 * m, PEERS, CHUNK), :]
        stage[1, part, :] = arrived[pl.ds(2 * m + 1, PEERS, CHUNK), :]
        stage[2, part, :] = jnp.where(lane == m, last, 0.0)
    rows = lax.broadcasted_iota(jnp.int32, (RAD, COLS), 0)
    selector = jnp.where(rows == member[...] >> 2, 0.25, 0.0).astype(BF)
    hi, lo = split(jnp.concatenate([stage[k] for k in range(3)], axis=1))
    total = dot(selector, hi, NN) + dot(selector, lo, NN)
    pooled[0:128, :] = total[:, 0:128].T
    pooled[128:256, :] = total[:, 128:256].T
    tail = total[:, 256:384].T
    pooled[256:288, :] = tail[0:32] + tail[32:64] + tail[64:96] + tail[96:128]
    surface = pooled[40:48, :]
    slant = jnp.broadcast_to(1.0 / (DIFFUSE * surface[6:7, :]), (GH, RAD))
    warm[...] = jnp.square(jnp.square(pooled[0:ROW, :]))
    thick[...] = pooled[ROW:BASE, :]
    pooled[BASE:FEAT, :] = pooled[BASE:FEAT, :] * (-DIFFUSE * LOG2E)
    pad = jnp.zeros((128 - 3 * PART, RAD), F32)
    tall = BLOCK * GALL
    for b in range(BLOCKS):
        start = BASE + SPECIES * BLOCK * b
        part = pooled[start : start + PART, :]
        hi = part.astype(BF).astype(F32)
        amounts = jnp.concatenate([hi, hi, part - hi, pad], axis=0).astype(BF)
        passing[b * tall : (b + 1) * tall, :] = dot(weights[b * tall : (b + 1) * tall, :], amounts, NN)
    me = side[0]

    def optics(l, half):
        tau = passing[span(l, half), :]
        kept = jnp.exp2(tau)
        source = emit[half * GH : (half + 1) * GH, :] * warm[l : l + 1, :]
        added = source - kept * source
        trans[span(l, half), :] = kept
        glow[span(l, half), :] = added
        return kept, added, jnp.exp2(tau * slant)

    def note(l, half, change):
        row = slice(8 * l, 8 * l + 8)
        sums[row, :] = sums[row, :] + change if half else change

    @pl.when(me == 0)
    def _():
        for half in range(2):
            part = slice(half * GH, (half + 1) * GH)
            thermal = jnp.zeros((GH, RAD), F32)
            direct = shine[part, :] * surface[7:8, :]
            above = fold(direct)
            for l in range(LEV):
                kept, added, passed = optics(l, half)
                thermal = kept * thermal + added
                direct = direct * passed
                below = fold(thermal + direct)
                note(l, half, above - below)
                above = below
            edge[part, :] = thermal
            edge[GALL + half * GH : GALL + (half + 1) * GH, :] = direct

    @pl.when(me == 1)
    def _():
        ground = jnp.square(jnp.square(surface[5:6, :]))
        for half in range(2):
            part = slice(half * GH, (half + 1) * GH)
            upward = emit[part, :] * ground
            below = fold(upward)
            for l in range(LEV - 1, -1, -1):
                kept, added, passed = optics(l, half)
                passing[span(l, half), :] = passed
                upward = kept * upward + added
                above = fold(upward)
                note(l, half, below - above)
                below = above
            edge[part, :] = upward
        edge[GALL:, :] = jnp.zeros((GALL, RAD), F32)


def second_kernel(side, gotten, trans, glow, passing, thick, sums, spread, send, net, slots):
    me = side[0]

    @pl.when(me == 0)
    def _():
        for half in range(2):
            upward = gotten[half * GH : (half + 1) * GH, :]
            below = fold(upward)
            for l in range(LEV - 1, -1, -1):
                upward = trans[span(l, half), :] * upward + glow[span(l, half), :]
                above = fold(upward)
                row = slice(8 * l, 8 * l + 8)
                net[row, :] = (net if half else sums)[row, :] + (below - above)
                below = above

    @pl.when(me == 1)
    def _():
        for half in range(2):
            thermal = gotten[half * GH : (half + 1) * GH, :]
            direct = gotten[GALL + half * GH : GALL + (half + 1) * GH, :]
            above = fold(thermal + direct)
            for l in range(LEV):
                thermal = trans[span(l, half), :] * thermal + glow[span(l, half), :]
                direct = direct * passing[span(l, half), :]
                below = fold(thermal + direct)
                row = slice(8 * l, 8 * l + 8)
                net[row, :] = (net if half else sums)[row, :] + (above - below)
                above = below

    total = None
    for k in range(8):
        part = net[pl.ds(k, LEV, 8), :]
        total = part if total is None else total + part
    heat = jnp.concatenate([total / thick[0:LEV, :], jnp.zeros((ROW - LEV, RAD), F32)], axis=0)
    gap = jnp.zeros((16, RAD), F32)
    hi, lo = split(jnp.concatenate([heat, gap, heat, gap], axis=0))
    slots[...] = dot(spread[...], hi, NT) + dot(spread[...], lo, NT)
    lanes = lax.broadcasted_iota(jnp.int32, (PEERS, RAD), 1)
    for h in range(2):
        even, odd = slots[pl.ds(2 * h, PEERS, SLOTS), :], slots[pl.ds(2 * h + 1, PEERS, SLOTS), :]
        send[pl.ds(h, PEERS, 2), :] = jnp.where(lanes < 64, even, odd)


def unplace_kernel(returned, pos, heating):
    parts = []
    for h in range(2):
        turned = returned[pl.ds(h, PEERS, 2), :].T
        parts += [turned[0:ROW, :], turned[64 : 64 + ROW, :]]
    hi, lo = split(jnp.concatenate(parts, axis=1))
    placing = slot_matrix(pos[...])
    heating[...] = (dot(hi, placing, NN) + dot(lo, placing, NN))[0:LEV, :]


def mix_kernel(tracers, adj, coef, from_left, from_right, mixed, high, low, band, stage):
    spare = LEV * SPECIES
    stage[spare:BODY, :] = jnp.zeros((BODY - spare, COLS), F32)
    for l in range(LEV):
        stage[SPECIES * l : SPECIES * (l + 1), :] = tracers[l]
    parts = (from_left[0:BODY, :], stage[...], from_right[0:BODY, :])
    for part, start in zip(parts, (0, REACH, REACH + COLS)):
        hi, lo = split(part)
        high[0, :, start : start + part.shape[1]] = hi
        low[0, :, start : start + part.shape[1]] = lo
    tables = jnp.concatenate([from_left[BODY:, :], mixing_table(adj, coef), from_right[BODY:, :]], axis=1)
    shifted = pltpu.roll(tables, WIDE - HALO, 1)
    rows = lax.broadcasted_iota(jnp.int32, (256, 128), 0).astype(F32)
    lanes = lax.broadcasted_iota(jnp.int32, (1, 128), 1).astype(F32)

    def build(source, k):
        part = source[:, k * 128 : (k + 1) * 128]
        blend = jnp.where(rows == lanes + HALO, 1.0 - jnp.sum(part[8:14, :], axis=0, keepdims=True), 0.0)
        for n in range(NEAR):
            blend = blend + jnp.where(rows == lanes + part[n : n + 1, :], part[8 + n : 9 + n, :], 0.0)
        return split(blend)

    for k in range(7):
        hi, lo = build(shifted, k)
        band[0, 0, k] = hi
        band[0, 1, k] = lo
    for k in range(6):
        hi, lo = build(tables, k + 1)
        band[1, 0, k] = hi
        band[1, 1, k] = lo
    for step in range(STEPS):
        now, later = step % 2, (step + 1) % 2
        tiles = 7 - step
        first = step // 2
        for k in range(tiles):
            window = slice(k * 128, k * 128 + 256)
            bh, bl = band[now, 0, k + first], band[now, 1, k + first]
            xh, xl = high[now, :, window], low[now, :, window]
            new = dot(xh, bh, NN) + (dot(xh, bl, NN) + dot(xl, bh, NN))
            if step < STEPS - 1:
                hi, lo = split(new)
                high[later, :, k * 128 : (k + 1) * 128] = hi
                low[later, :, k * 128 : (k + 1) * 128] = lo
            else:
                for l in range(LEV):
                    mixed[l, :, k * 128 : (k + 1) * 128] = new[SPECIES * l : SPECIES * (l + 1), :]


def shape(*dims):
    return jax.ShapeDtypeStruct(dims, F32)


LENGTH = {"pack": 27, "join": 5, "weight": 7, "mix": 42, "first": 20, "second": 9, "unplace": 10}


def call(kernel, name, out_shape, scratch, vmem_limit_bytes=16 << 20, **specs):
    return pl.pallas_call(
        kernel,
        out_shape=out_shape,
        scratch_shapes=scratch,
        compiler_params=pltpu.CompilerParams(vmem_limit_bytes=vmem_limit_bytes),
        cost_estimate=pl.CostEstimate(flops=LENGTH[name] * 10**8, bytes_accessed=1 << 18, transcendentals=0),
        **specs,
    )


def per_device(
    stratum_warmth_anomaly,
    pressure_depth,
    absorber_amounts,
    ground_warmth_anomaly,
    sun_elevation_factor,
    daytime_mask,
    dispatch_position,
    arrival_membership,
    adjacency_table,
    blending_coefficient,
    opacity_table,
    emission_share,
    sunshine_share,
):
    n = lax.axis_size("grp")
    up = [(i, (i + 1) % n) for i in range(n)]
    down = [(j, i) for i, j in up]
    swap = [(0, 1), (1, 0)]
    halo_rows = BODY + 16
    tracers = jnp.transpose(absorber_amounts, (1, 0, 2))

    hbm = pl.BlockSpec(memory_space=pltpu.HBM)
    packed = (shape(PEERS * CHUNK, 128), shape(halo_rows, REACH), shape(halo_rows, REACH))
    given = ((LEV, COLS), (LEV, COLS), (LEV, SPECIES, COLS), (1, COLS), (1, COLS))
    send, right, left = call(
        pack_kernel,
        "pack",
        packed,
        [pltpu.VMEM(dims, F32) for dims in given]
        + [pltpu.VMEM((rows, COLS), jnp.int32) for rows in (1, 1, NEAR)]
        + [pltpu.VMEM((NEAR, COLS), F32)]
        + [pltpu.VMEM(out.shape, F32) for out in packed]
        + [pltpu.VMEM((FEAT, COLS), F32), pltpu.SemaphoreType.DMA((9,)), pltpu.SemaphoreType.DMA((3,))],
        in_specs=[hbm] * 9,
        out_specs=[hbm] * 3,
        vmem_limit_bytes=60 << 20,
    )(
        stratum_warmth_anomaly,
        pressure_depth,
        tracers,
        ground_warmth_anomaly[None],
        sun_elevation_factor[None],
        daytime_mask[None],
        dispatch_position,
        adjacency_table,
        blending_coefficient,
    )
    from_left = lax.ppermute(right, "grp", up)
    from_right = lax.ppermute(left, "grp", down)
    arrived = lax.all_to_all(send.reshape(PEERS * CHUNK, 1, 128), "grp", split_axis=0, concat_axis=0, tiled=True)
    mixed = call(
        mix_kernel,
        "mix",
        shape(LEV, SPECIES, COLS),
        [
            pltpu.VMEM((2, BODY, WIDE), BF),
            pltpu.VMEM((2, BODY, WIDE), BF),
            pltpu.VMEM((2, 2, 7, 256, 128), BF),
            pltpu.VMEM((BODY, COLS), F32),
        ],
    )(tracers, adjacency_table, blending_coefficient, from_left, from_right)
    side = lax.axis_index("sec").astype(jnp.int32)[None]
    opacity = call(join_kernel, "join", shape(SPECIES, GH, 128), [])(
        opacity_table, emission_share[None], sunshine_share[None]
    )
    whole = pl.BlockSpec(memory_space=pltpu.VMEM)
    scalar = pl.BlockSpec(memory_space=pltpu.SMEM)
    rows = LEV * GALL
    weights, emit, shine, spread = call(
        weight_kernel,
        "weight",
        (
            jax.ShapeDtypeStruct((rows, 128), BF),
            shape(GALL, RAD),
            shape(GALL, RAD),
            jax.ShapeDtypeStruct((COLS, RAD), BF),
        ),
        [pltpu.VMEM((2, SPECIES, GH, 128), F32)],
        in_specs=[scalar] + [whole] * 3,
    )(side, opacity, lax.ppermute(opacity, "sec", swap), arrival_membership)
    arrived, mixed, weights, emit, shine, spread, side = lax.optimization_barrier(
        (arrived, mixed, weights, emit, shine, spread, side)
    )
    trans, glow, passing, thick, sums, edge = call(
        first_kernel,
        "first",
        (
            shape(rows, RAD),
            shape(rows, RAD),
            shape(rows, RAD),
            shape(ROW, RAD),
            shape(8 * LEV, RAD),
            shape(2 * GALL, RAD),
        ),
        [pltpu.VMEM((3, COLS, 128), F32), pltpu.VMEM((FEAT, RAD), F32), pltpu.VMEM((ROW, RAD), F32)],
        in_specs=[scalar] + [whole] * 5,
    )(side, arrived.reshape(PEERS * CHUNK, 128), arrival_membership, weights, emit, shine)
    gotten = lax.ppermute(edge, "sec", swap)
    back = call(
        second_kernel,
        "second",
        shape(PEERS * 2, 128),
        [pltpu.VMEM((8 * LEV, RAD), F32), pltpu.VMEM((COLS, RAD), F32)],
        in_specs=[scalar] + [whole] * 7,
    )(side, gotten, trans, glow, passing, thick, sums, spread)
    returned = lax.all_to_all(
        back.reshape(PEERS * 2, 1, 128), "grp", split_axis=0, concat_axis=0, tiled=True
    ).reshape(PEERS * 2, 128)
    heating = call(unplace_kernel, "unplace", shape(LEV, COLS), [])(returned, dispatch_position)
    return (heating, jnp.transpose(mixed, (1, 0, 2)))


def solution(mesh):
    in_specs = (
        P("sec", "grp"),
        P("sec", "grp"),
        P(None, "sec", "grp"),
        P("grp"),
        P("grp"),
        P("grp"),
        P("grp", None),
        P("grp", None),
        P(None, "grp"),
        P(None, "grp"),
        P(None, "sec", None),
        P("sec"),
        P("sec"),
    )
    out_specs = (P("sec", "grp"), P(None, "sec", "grp"))
    return jax.shard_map(
        per_device, mesh=mesh, in_specs=in_specs, out_specs=out_specs, check_vma=False
    )
```

```python
import math

import jax
import jax.numpy as jnp
from jax import lax
from jax.experimental import pallas as pl
from jax.experimental.pallas import tpu as pltpu
from jax.sharding import PartitionSpec as P


STEPS = 4
HALO = 64
DIFFUSE = 1.66
LOG2E = math.log2(math.e)
BF = jnp.bfloat16
F32 = jnp.float32

PEERS = 128
SLOTS = 4
COLS = 512
LEV = 45
ROW = 48
BASE = 2 * ROW
BODY = 192
FEAT = BASE + BODY
CHUNK = SLOTS * FEAT // 128
RAD = 128
GH = 56
REACH = STEPS * HALO
WIDE = COLS + 2 * REACH
SPECIES = 4
NEAR = 6
BLOCK = 9
BLOCKS = LEV // BLOCK
GALL = 2 * GH
TALL = 512
DEEP = 2 * BLOCKS * TALL
PART = 40
NT = (((1,), (1,)), ((), ()))
NN = (((1,), (0,)), ((), ()))


def split(x):
    hi = x.astype(BF)
    return hi, (x - hi.astype(F32)).astype(BF)


def dot(a, b, dims):
    return lax.dot_general(a, b, dims, preferred_element_type=F32)


def slot_matrix(position):
    rows = lax.broadcasted_iota(jnp.int32, (COLS, COLS), 0)
    slot = (rows & (PEERS - 1)) * SLOTS + (rows >> 7)
    return jnp.where(slot == position, 1.0, 0.0).astype(BF)


def mixing_table(adj, coef):
    column = lax.broadcasted_iota(jnp.int32, (NEAR, COLS), 1)
    pad = jnp.zeros((2, COLS), F32)
    return jnp.concatenate([(adj[...] - column).astype(F32), pad, coef[...], pad], axis=0)


def pack_kernel(*refs):
    sources, outs, scratch = refs[:9], refs[9:12], refs[12:]
    temp, thick, tracers, ground, sun, day, pos, adj, coef = scratch[:9]
    send, right, left, bundle, sems, done = scratch[9:]
    copies = [pltpu.make_async_copy(a, b, sems.at[i]) for i, (a, b) in enumerate(zip(sources, scratch))]
    for i in (6, 7, 8, 2, 0, 1, 3, 4, 5):
        copies[i].start()
    stores = [pltpu.make_async_copy(a, b, done.at[i]) for i, (a, b) in enumerate(zip((send, right, left), outs))]
    bundle[ROW + LEV : BASE, :] = jnp.zeros((ROW - LEV, COLS), F32)
    spare = BASE + LEV * SPECIES
    bundle[spare:FEAT, :] = jnp.zeros((FEAT - spare, COLS), F32)
    for i in (6, 7, 8):
        copies[i].wait()
    placing = slot_matrix(pos[...])
    both = mixing_table(adj, coef)
    right[BODY : BODY + 16, :] = both[:, COLS - REACH :]
    left[BODY : BODY + 16, :] = both[:, :REACH]
    copies[2].wait()
    for l in range(LEV):
        bundle[BASE + SPECIES * l : BASE + SPECIES * (l + 1), :] = tracers[l]
    right[0:BODY, :] = bundle[BASE:FEAT, COLS - REACH :]
    left[0:BODY, :] = bundle[BASE:FEAT, :REACH]
    for i in (1, 2):
        stores[i].start()
    for i in (0, 1, 3, 4, 5):
        copies[i].wait()
    bundle[0:LEV, :] = temp[...]
    bundle[ROW : ROW + LEV, :] = thick[...]
    sunny = sun[...]
    bundle[LEV : LEV + 1, :] = ground[...]
    bundle[LEV + 1 : LEV + 2, :] = sunny
    bundle[LEV + 2 : LEV + 3, :] = day[...].astype(F32) * sunny
    hi, lo = split(bundle[0:256, :])
    packed = dot(placing, hi, NT) + dot(placing, lo, NT)
    tail = bundle[256:288, :]
    hi = tail.astype(BF).astype(F32)
    tails = dot(placing, jnp.concatenate([hi] * SLOTS + [tail - hi] * SLOTS, axis=0).astype(BF), NT)
    tails = tails[:, 0:128] + tails[:, 128:256]
    lane = lax.broadcasted_iota(jnp.int32, (PEERS, 128), 1) >> 5
    last = jnp.zeros((PEERS, 128), F32)
    for m in range(SLOTS):
        block = packed[m * PEERS : (m + 1) * PEERS, :]
        send[pl.ds(2 * m, PEERS, CHUNK), :] = block[:, 0:128]
        send[pl.ds(2 * m + 1, PEERS, CHUNK), :] = block[:, 128:256]
        last = jnp.where(lane == m, tails[m * PEERS : (m + 1) * PEERS, :], last)
    send[pl.ds(CHUNK - 1, PEERS, CHUNK), :] = last
    stores[0].start()
    for store in stores:
        store.wait()


def join_kernel(opacity, emission, sunshine, joined):
    rows = lax.broadcasted_iota(jnp.int32, (GH, GH), 0)
    lanes = lax.broadcasted_iota(jnp.int32, (GH, GH), 1)
    for s in range(SPECIES):
        joined[s] = jnp.zeros((GH, 128), F32)
        joined[s, :, 0 : 2 * LEV] = opacity[s]
    for k, share in enumerate((emission, sunshine)):
        square = jnp.where(rows == lanes, jnp.broadcast_to(share[...], (GH, GH)), 0.0)
        joined[0, :, 2 * LEV + k : 2 * LEV + k + 1] = jnp.sum(square, axis=1, keepdims=True)


def weight_kernel(side, own, other, member, pos, weights, emit, shine, spread, placing, full):
    placing[...] = slot_matrix(pos[...])
    ids = (member[...] >> 2).astype(F32)
    spots = lax.broadcasted_iota(jnp.int32, (128, RAD), 1).astype(F32)
    for k in range(SLOTS):
        part = slice(k * 128, (k + 1) * 128)
        column = jnp.broadcast_to(ids[:, part], (128, 128)).T
        spread[part, :] = jnp.where(column == spots, 1.0, 0.0).astype(BF)
    me = side[0]
    full[pl.ds(me, 1)] = own[...][None]
    full[pl.ds(1 - me, 1)] = other[...][None]
    shift = lax.rem(128 - LEV * me, 128)
    tables = [jnp.concatenate([full[0, s], full[1, s]], axis=0) for s in range(SPECIES)]
    emit[...] = jnp.broadcast_to(tables[0][:, 2 * LEV : 2 * LEV + 1], (GALL, RAD))
    shine[...] = jnp.broadcast_to(tables[0][:, 2 * LEV + 1 : 2 * LEV + 2], (GALL, RAD))
    tables = [pltpu.roll(table, shift, 1) for table in tables]
    rows = lax.broadcasted_iota(jnp.int32, (128, 128), 0)
    lanes = lax.broadcasted_iota(jnp.int32, (128, 128), 1)
    picks = []
    for s in range(SPECIES):
        lane = jnp.where(rows < BLOCK, SPECIES * rows + s, -1)
        picks.append((lanes == lane) | (lanes == jnp.where(lane < 0, -1, lane + 2 * PART)))
    for s in range(SPECIES):
        lane = jnp.where(rows < BLOCK, SPECIES * rows + s + PART, -1)
        picks.append(lanes == lane)
    picker = jnp.concatenate([jnp.where(p, 1.0, 0.0).astype(BF) for p in picks], axis=0)
    group = lax.broadcasted_iota(jnp.int32, (GH, 128), 1)
    group = jnp.where(group >= 2 * PART, group - 2 * PART, jnp.where(group >= PART, group - PART, group)) >> 2
    pad = jnp.zeros((TALL - BLOCK * GH, 128), F32)
    for b in range(BLOCKS):
        his, los = [], []
        for table in tables:
            hi, lo = split(pltpu.roll(table, 128 - b * BLOCK, 1) if b else table)
            his.append(hi)
            los.append(lo)
        wide = dot(jnp.concatenate(his + los, axis=1), picker, NN)
        for half in range(2):
            part = wide[half * GH : (half + 1) * GH, :]
            block = jnp.concatenate([jnp.where(group == i, part, 0.0) for i in range(BLOCK)] + [pad], axis=0)
            start = (half * BLOCKS + b) * TALL
            weights[start : start + TALL, :] = block.astype(BF)


def fold(x):
    return jnp.sum(x.reshape(GH // 8, 8, RAD), axis=0)


def span(level, half):
    start = (half * BLOCKS + level // BLOCK) * TALL + level % BLOCK * GH
    return slice(start, start + GH)


def first_kernel(side, arrived, member, weights, emit, shine, trans, glow, passing, thick, sums, edge, stage, pooled, warm, amounts):
    lane = lax.broadcasted_iota(jnp.int32, (PEERS, 128), 1) >> 5
    last = arrived[pl.ds(CHUNK - 1, PEERS, CHUNK), :]
    for m in range(SLOTS):
        part = pl.ds(m, PEERS, SLOTS)
        stage[0, part, :] = arrived[pl.ds(2 * m, PEERS, CHUNK), :]
        stage[1, part, :] = arrived[pl.ds(2 * m + 1, PEERS, CHUNK), :]
        stage[2, part, :] = jnp.where(lane == m, last, 0.0)
    rows = lax.broadcasted_iota(jnp.int32, (RAD, COLS), 0)
    selector = jnp.where(rows == member[...] >> 2, 0.25, 0.0).astype(BF)
    hi, lo = split(jnp.concatenate([stage[k] for k in range(3)], axis=1))
    total = dot(selector, hi, NN) + dot(selector, lo, NN)
    pooled[0:128, :] = total[:, 0:128].T
    pooled[128:256, :] = total[:, 128:256].T
    tail = total[:, 256:384].T
    pooled[256:288, :] = tail[0:32] + tail[32:64] + tail[64:96] + tail[96:128]
    surface = pooled[40:48, :]
    slant = jnp.broadcast_to(1.0 / (DIFFUSE * surface[6:7, :]), (GH, RAD))
    warm[...] = jnp.square(jnp.square(pooled[0:ROW, :]))
    thick[...] = pooled[ROW:BASE, :]
    pooled[BASE:FEAT, :] = pooled[BASE:FEAT, :] * (-DIFFUSE * LOG2E)
    pad = jnp.zeros((128 - 3 * PART, RAD), F32)
    for b in range(BLOCKS):
        start = BASE + SPECIES * BLOCK * b
        part = pooled[start : start + PART, :]
        hi = part.astype(BF).astype(F32)
        amounts[b * 128 : (b + 1) * 128, :] = jnp.concatenate([hi, hi, part - hi, pad], axis=0).astype(BF)

    def depths(half, b):
        rows = slice((half * BLOCKS + b) * TALL, (half * BLOCKS + b + 1) * TALL)
        passing[rows, :] = dot(weights[rows, :], amounts[b * 128 : (b + 1) * 128, :], NN)

    def ahead(order, place):
        if place == 0:
            depths(*order[0])
        if place + 1 < len(order):
            depths(*order[place + 1])

    me = side[0]

    def optics(l, half):
        tau = passing[span(l, half), :]
        kept = jnp.exp2(tau)
        source = emit[half * GH : (half + 1) * GH, :] * warm[l : l + 1, :]
        added = source - kept * source
        trans[span(l, half), :] = kept
        glow[span(l, half), :] = added
        return kept, added, jnp.exp2(tau * slant)

    def note(l, half, change):
        row = slice(8 * l, 8 * l + 8)
        sums[row, :] = sums[row, :] + change if half else change

    @pl.when(me == 0)
    def _():
        order = [(half, b) for half in range(2) for b in range(BLOCKS)]
        for half in range(2):
            part = slice(half * GH, (half + 1) * GH)
            thermal = jnp.zeros((GH, RAD), F32)
            direct = shine[part, :] * surface[7:8, :]
            above = fold(direct)
            for l in range(LEV):
                if l % BLOCK == 0:
                    ahead(order, half * BLOCKS + l // BLOCK)
                kept, added, passed = optics(l, half)
                thermal = kept * thermal + added
                direct = direct * passed
                below = fold(thermal + direct)
                note(l, half, above - below)
                above = below
            edge[part, :] = thermal
            edge[GALL + half * GH : GALL + (half + 1) * GH, :] = direct

    @pl.when(me == 1)
    def _():
        ground = jnp.square(jnp.square(surface[5:6, :]))
        order = [(half, BLOCKS - 1 - b) for half in range(2) for b in range(BLOCKS)]
        for half in range(2):
            part = slice(half * GH, (half + 1) * GH)
            upward = emit[part, :] * ground
            below = fold(upward)
            for l in range(LEV - 1, -1, -1):
                if l % BLOCK == BLOCK - 1:
                    ahead(order, half * BLOCKS + BLOCKS - 1 - l // BLOCK)
                kept, added, passed = optics(l, half)
                passing[span(l, half), :] = passed
                upward = kept * upward + added
                above = fold(upward)
                note(l, half, below - above)
                below = above
            edge[part, :] = upward
        edge[GALL:, :] = jnp.zeros((GALL, RAD), F32)


def second_kernel(side, gotten, trans, glow, passing, thick, sums, spread, send, net, slots):
    me = side[0]

    @pl.when(me == 0)
    def _():
        for half in range(2):
            upward = gotten[half * GH : (half + 1) * GH, :]
            below = fold(upward)
            for l in range(LEV - 1, -1, -1):
                upward = trans[span(l, half), :] * upward + glow[span(l, half), :]
                above = fold(upward)
                row = slice(8 * l, 8 * l + 8)
                net[row, :] = (net if half else sums)[row, :] + (below - above)
                below = above

    @pl.when(me == 1)
    def _():
        for half in range(2):
            thermal = gotten[half * GH : (half + 1) * GH, :]
            direct = gotten[GALL + half * GH : GALL + (half + 1) * GH, :]
            above = fold(thermal + direct)
            for l in range(LEV):
                thermal = trans[span(l, half), :] * thermal + glow[span(l, half), :]
                direct = direct * passing[span(l, half), :]
                below = fold(thermal + direct)
                row = slice(8 * l, 8 * l + 8)
                net[row, :] = (net if half else sums)[row, :] + (above - below)
                above = below

    total = None
    for k in range(8):
        part = net[pl.ds(k, LEV, 8), :]
        total = part if total is None else total + part
    heat = jnp.concatenate([total / thick[0:LEV, :], jnp.zeros((ROW - LEV, RAD), F32)], axis=0)
    gap = jnp.zeros((16, RAD), F32)
    hi, lo = split(jnp.concatenate([heat, gap, heat, gap], axis=0))
    slots[...] = dot(spread[...], hi, NT) + dot(spread[...], lo, NT)
    lanes = lax.broadcasted_iota(jnp.int32, (PEERS, RAD), 1)
    for h in range(2):
        even, odd = slots[pl.ds(2 * h, PEERS, SLOTS), :], slots[pl.ds(2 * h + 1, PEERS, SLOTS), :]
        send[pl.ds(h, PEERS, 2), :] = jnp.where(lanes < 64, even, odd)


def unplace_kernel(returned, placing, heating):
    parts = []
    for h in range(2):
        turned = returned[pl.ds(h, PEERS, 2), :].T
        parts += [turned[0:ROW, :], turned[64 : 64 + ROW, :]]
    hi, lo = split(jnp.concatenate(parts, axis=1))
    heating[...] = (dot(hi, placing[...], NN) + dot(lo, placing[...], NN))[0:LEV, :]


def mix_kernel(tracers, adj, coef, from_left, from_right, mixed, high, low, band, stage):
    spare = LEV * SPECIES
    stage[spare:BODY, :] = jnp.zeros((BODY - spare, COLS), F32)
    for l in range(LEV):
        stage[SPECIES * l : SPECIES * (l + 1), :] = tracers[l]
    parts = (from_left[0:BODY, :], stage[...], from_right[0:BODY, :])
    for part, start in zip(parts, (0, REACH, REACH + COLS)):
        hi, lo = split(part)
        high[0, :, start : start + part.shape[1]] = hi
        low[0, :, start : start + part.shape[1]] = lo
    tables = jnp.concatenate([from_left[BODY:, :], mixing_table(adj, coef), from_right[BODY:, :]], axis=1)
    shifted = pltpu.roll(tables, WIDE - HALO, 1)
    rows = lax.broadcasted_iota(jnp.int32, (256, 128), 0).astype(F32)
    lanes = lax.broadcasted_iota(jnp.int32, (1, 128), 1).astype(F32)

    def build(source, k):
        part = source[:, k * 128 : (k + 1) * 128]
        blend = jnp.where(rows == lanes + HALO, 1.0 - jnp.sum(part[8:14, :], axis=0, keepdims=True), 0.0)
        for n in range(NEAR):
            blend = blend + jnp.where(rows == lanes + part[n : n + 1, :], part[8 + n : 9 + n, :], 0.0)
        return split(blend)

    for k in range(7):
        hi, lo = build(shifted, k)
        band[0, 0, k] = hi
        band[0, 1, k] = lo
    for k in range(6):
        hi, lo = build(tables, k + 1)
        band[1, 0, k] = hi
        band[1, 1, k] = lo
    for step in range(STEPS):
        now, later = step % 2, (step + 1) % 2
        tiles = 7 - step
        first = step // 2
        for k in range(tiles):
            window = slice(k * 128, k * 128 + 256)
            bh, bl = band[now, 0, k + first], band[now, 1, k + first]
            xh, xl = high[now, :, window], low[now, :, window]
            new = dot(xh, bh, NN) + (dot(xh, bl, NN) + dot(xl, bh, NN))
            if step < STEPS - 1:
                hi, lo = split(new)
                high[later, :, k * 128 : (k + 1) * 128] = hi
                low[later, :, k * 128 : (k + 1) * 128] = lo
            else:
                for l in range(LEV):
                    mixed[l, :, k * 128 : (k + 1) * 128] = new[SPECIES * l : SPECIES * (l + 1), :]


def shape(*dims):
    return jax.ShapeDtypeStruct(dims, F32)


LENGTH = {"pack": 27, "join": 5, "weight": 7, "mix": 42, "first": 20, "second": 9, "unplace": 10}


def call(kernel, name, out_shape, scratch, vmem_limit_bytes=16 << 20, **specs):
    return pl.pallas_call(
        kernel,
        out_shape=out_shape,
        scratch_shapes=scratch,
        compiler_params=pltpu.CompilerParams(vmem_limit_bytes=vmem_limit_bytes),
        cost_estimate=pl.CostEstimate(flops=LENGTH[name] * 10**8, bytes_accessed=1 << 18, transcendentals=0),
        **specs,
    )


def per_device(
    stratum_warmth_anomaly,
    pressure_depth,
    absorber_amounts,
    ground_warmth_anomaly,
    sun_elevation_factor,
    daytime_mask,
    dispatch_position,
    arrival_membership,
    adjacency_table,
    blending_coefficient,
    opacity_table,
    emission_share,
    sunshine_share,
):
    n = lax.axis_size("grp")
    up = [(i, (i + 1) % n) for i in range(n)]
    down = [(j, i) for i, j in up]
    swap = [(0, 1), (1, 0)]
    halo_rows = BODY + 16
    tracers = jnp.transpose(absorber_amounts, (1, 0, 2))

    hbm = pl.BlockSpec(memory_space=pltpu.HBM)
    packed = (shape(PEERS * CHUNK, 128), shape(halo_rows, REACH), shape(halo_rows, REACH))
    given = ((LEV, COLS), (LEV, COLS), (LEV, SPECIES, COLS), (1, COLS), (1, COLS))
    send, right, left = call(
        pack_kernel,
        "pack",
        packed,
        [pltpu.VMEM(dims, F32) for dims in given]
        + [pltpu.VMEM((rows, COLS), jnp.int32) for rows in (1, 1, NEAR)]
        + [pltpu.VMEM((NEAR, COLS), F32)]
        + [pltpu.VMEM(out.shape, F32) for out in packed]
        + [pltpu.VMEM((FEAT, COLS), F32), pltpu.SemaphoreType.DMA((9,)), pltpu.SemaphoreType.DMA((3,))],
        in_specs=[hbm] * 9,
        out_specs=[hbm] * 3,
        vmem_limit_bytes=60 << 20,
    )(
        stratum_warmth_anomaly,
        pressure_depth,
        tracers,
        ground_warmth_anomaly[None],
        sun_elevation_factor[None],
        daytime_mask[None],
        dispatch_position,
        adjacency_table,
        blending_coefficient,
    )
    from_left = lax.ppermute(right, "grp", up)
    from_right = lax.ppermute(left, "grp", down)
    arrived = lax.all_to_all(send.reshape(PEERS * CHUNK, 1, 128), "grp", split_axis=0, concat_axis=0, tiled=True)
    mixed = call(
        mix_kernel,
        "mix",
        shape(LEV, SPECIES, COLS),
        [
            pltpu.VMEM((2, BODY, WIDE), BF),
            pltpu.VMEM((2, BODY, WIDE), BF),
            pltpu.VMEM((2, 2, 7, 256, 128), BF),
            pltpu.VMEM((BODY, COLS), F32),
        ],
    )(tracers, adjacency_table, blending_coefficient, from_left, from_right)
    side = lax.axis_index("sec").astype(jnp.int32)[None]
    opacity = call(join_kernel, "join", shape(SPECIES, GH, 128), [])(
        opacity_table, emission_share[None], sunshine_share[None]
    )
    whole = pl.BlockSpec(memory_space=pltpu.VMEM)
    scalar = pl.BlockSpec(memory_space=pltpu.SMEM)
    weights, emit, shine, spread, placing = call(
        weight_kernel,
        "weight",
        (
            jax.ShapeDtypeStruct((DEEP, 128), BF),
            shape(GALL, RAD),
            shape(GALL, RAD),
            jax.ShapeDtypeStruct((COLS, RAD), BF),
            jax.ShapeDtypeStruct((COLS, COLS), BF),
        ),
        [pltpu.VMEM((2, SPECIES, GH, 128), F32)],
        in_specs=[scalar] + [whole] * 4,
    )(side, opacity, lax.ppermute(opacity, "sec", swap), arrival_membership, dispatch_position)
    arrived, mixed, weights, emit, shine, spread, placing, side = lax.optimization_barrier(
        (arrived, mixed, weights, emit, shine, spread, placing, side)
    )
    trans, glow, passing, thick, sums, edge = call(
        first_kernel,
        "first",
        (
            shape(DEEP, RAD),
            shape(DEEP, RAD),
            shape(DEEP, RAD),
            shape(ROW, RAD),
            shape(8 * LEV, RAD),
            shape(2 * GALL, RAD),
        ),
        [
            pltpu.VMEM((3, COLS, 128), F32),
            pltpu.VMEM((FEAT, RAD), F32),
            pltpu.VMEM((ROW, RAD), F32),
            pltpu.VMEM((BLOCKS * 128, RAD), BF),
        ],
        in_specs=[scalar] + [whole] * 5,
    )(side, arrived.reshape(PEERS * CHUNK, 128), arrival_membership, weights, emit, shine)
    gotten = lax.ppermute(edge, "sec", swap)
    back = call(
        second_kernel,
        "second",
        shape(PEERS * 2, 128),
        [pltpu.VMEM((8 * LEV, RAD), F32), pltpu.VMEM((COLS, RAD), F32)],
        in_specs=[scalar] + [whole] * 7,
    )(side, gotten, trans, glow, passing, thick, sums, spread)
    returned = lax.all_to_all(
        back.reshape(PEERS * 2, 1, 128), "grp", split_axis=0, concat_axis=0, tiled=True
    ).reshape(PEERS * 2, 128)
    heating = call(unplace_kernel, "unplace", shape(LEV, COLS), [])(returned, placing)
    return (heating, jnp.transpose(mixed, (1, 0, 2)))


def solution(mesh):
    in_specs = (
        P("sec", "grp"),
        P("sec", "grp"),
        P(None, "sec", "grp"),
        P("grp"),
        P("grp"),
        P("grp"),
        P("grp", None),
        P("grp", None),
        P(None, "grp"),
        P(None, "grp"),
        P(None, "sec", None),
        P("sec"),
        P("sec"),
    )
    out_specs = (P("sec", "grp"), P(None, "sec", "grp"))
    return jax.shard_map(
        per_device, mesh=mesh, in_specs=in_specs, out_specs=out_specs, check_vma=False
    )
```

```python
import math

import jax
import jax.numpy as jnp
from jax import lax
from jax.experimental import pallas as pl
from jax.experimental.pallas import tpu as pltpu
from jax.sharding import PartitionSpec as P


STEPS = 4
HALO = 64
DIFFUSE = 1.66
LOG2E = math.log2(math.e)
BF = jnp.bfloat16
F32 = jnp.float32

PEERS = 128
SLOTS = 4
COLS = 512
LEV = 45
ROW = 48
BASE = 2 * ROW
BODY = 192
FEAT = BASE + BODY
CHUNK = SLOTS * FEAT // 128
RAD = 128
GH = 56
REACH = STEPS * HALO
WIDE = COLS + 2 * REACH
SPECIES = 4
NEAR = 6
BLOCK = 9
BLOCKS = LEV // BLOCK
GALL = 2 * GH
TALL = 512
DEEP = 2 * BLOCKS * TALL
PART = 40
NT = (((1,), (1,)), ((), ()))
NN = (((1,), (0,)), ((), ()))


def split(x):
    hi = x.astype(BF)
    return hi, (x - hi.astype(F32)).astype(BF)


def dot(a, b, dims):
    return lax.dot_general(a, b, dims, preferred_element_type=F32)


def slot_matrix(position):
    rows = lax.broadcasted_iota(jnp.int32, (COLS, COLS), 0)
    slot = (rows & (PEERS - 1)) * SLOTS + (rows >> 7)
    return jnp.where(slot == position, 1.0, 0.0).astype(BF)


def mixing_table(adj, coef):
    column = lax.broadcasted_iota(jnp.int32, (NEAR, COLS), 1)
    pad = jnp.zeros((2, COLS), F32)
    return jnp.concatenate([(adj[...] - column).astype(F32), pad, coef[...], pad], axis=0)


def pack_kernel(*refs):
    sources, outs, scratch = refs[:9], refs[9:12], refs[12:]
    temp, thick, tracers, ground, sun, day, pos, adj, coef = scratch[:9]
    send, right, left, bundle, sems, done = scratch[9:]
    copies = [pltpu.make_async_copy(a, b, sems.at[i]) for i, (a, b) in enumerate(zip(sources, scratch))]
    for i in (6, 7, 8, 2, 0, 1, 3, 4, 5):
        copies[i].start()
    middle = PEERS * CHUNK // 2
    pairs = [(send.at[0:middle, :], outs[0].at[0:middle, :]), (right, outs[1]), (left, outs[2])]
    pairs.append((send.at[middle : 2 * middle, :], outs[0].at[middle : 2 * middle, :]))
    stores = [pltpu.make_async_copy(a, b, done.at[i]) for i, (a, b) in enumerate(pairs)]
    bundle[ROW + LEV : BASE, :] = jnp.zeros((ROW - LEV, COLS), F32)
    spare = BASE + LEV * SPECIES
    bundle[spare:FEAT, :] = jnp.zeros((FEAT - spare, COLS), F32)
    for i in (6, 7, 8):
        copies[i].wait()
    placing = slot_matrix(pos[...])
    both = mixing_table(adj, coef)
    right[BODY : BODY + 16, :] = both[:, COLS - REACH :]
    left[BODY : BODY + 16, :] = both[:, :REACH]
    copies[2].wait()
    for l in range(LEV):
        bundle[BASE + SPECIES * l : BASE + SPECIES * (l + 1), :] = tracers[l]
    right[0:BODY, :] = bundle[BASE:FEAT, COLS - REACH :]
    left[0:BODY, :] = bundle[BASE:FEAT, :REACH]
    for i in (1, 2):
        stores[i].start()
    for i in (0, 1, 3, 4, 5):
        copies[i].wait()
    bundle[0:LEV, :] = temp[...]
    bundle[ROW : ROW + LEV, :] = thick[...]
    sunny = sun[...]
    bundle[LEV : LEV + 1, :] = ground[...]
    bundle[LEV + 1 : LEV + 2, :] = sunny
    bundle[LEV + 2 : LEV + 3, :] = day[...].astype(F32) * sunny
    hi, lo = split(bundle[...])
    tails = []
    for m in range(SLOTS):
        if m % 2 == 0:
            pair = placing[m * PEERS : (m + 2) * PEERS, :]
            packed = dot(hi, pair, NT) + dot(lo, pair, NT)
        block = packed[:, m % 2 * PEERS : (m % 2 + 1) * PEERS]
        send[pl.ds(2 * m, PEERS, CHUNK), :] = block[0:128, :].T
        send[pl.ds(2 * m + 1, PEERS, CHUNK), :] = block[128:256, :].T
        tails.append(block[256:288, :])
    send[pl.ds(CHUNK - 1, PEERS, CHUNK), :] = jnp.concatenate(tails, axis=0).T
    stores[0].start()
    stores[3].start()
    for store in stores:
        store.wait()


def join_kernel(opacity, emission, sunshine, joined):
    rows = lax.broadcasted_iota(jnp.int32, (GH, GH), 0)
    lanes = lax.broadcasted_iota(jnp.int32, (GH, GH), 1)
    for s in range(SPECIES):
        joined[s] = jnp.zeros((GH, 128), F32)
        joined[s, :, 0 : 2 * LEV] = opacity[s]
    for k, share in enumerate((emission, sunshine)):
        square = jnp.where(rows == lanes, jnp.broadcast_to(share[...], (GH, GH)), 0.0)
        joined[0, :, 2 * LEV + k : 2 * LEV + k + 1] = jnp.sum(square, axis=1, keepdims=True)


def weight_kernel(side, own, other, member, pos, weights, emit, shine, spread, placing, full):
    placing[...] = slot_matrix(pos[...])
    ids = (member[...] >> 2).astype(F32)
    spots = lax.broadcasted_iota(jnp.int32, (128, RAD), 1).astype(F32)
    for k in range(SLOTS):
        part = slice(k * 128, (k + 1) * 128)
        column = jnp.broadcast_to(ids[:, part], (128, 128)).T
        spread[part, :] = jnp.where(column == spots, 1.0, 0.0).astype(BF)
    me = side[0]
    full[pl.ds(me, 1)] = own[...][None]
    full[pl.ds(1 - me, 1)] = other[...][None]
    shift = lax.rem(128 - LEV * me, 128)
    tables = [jnp.concatenate([full[0, s], full[1, s]], axis=0) for s in range(SPECIES)]
    emit[...] = jnp.broadcast_to(tables[0][:, 2 * LEV : 2 * LEV + 1], (GALL, RAD))
    shine[...] = jnp.broadcast_to(tables[0][:, 2 * LEV + 1 : 2 * LEV + 2], (GALL, RAD))
    tables = [pltpu.roll(table, shift, 1) for table in tables]
    rows = lax.broadcasted_iota(jnp.int32, (128, 128), 0)
    lanes = lax.broadcasted_iota(jnp.int32, (128, 128), 1)
    picks = []
    for s in range(SPECIES):
        lane = jnp.where(rows < BLOCK, SPECIES * rows + s, -1)
        picks.append((lanes == lane) | (lanes == jnp.where(lane < 0, -1, lane + 2 * PART)))
    for s in range(SPECIES):
        lane = jnp.where(rows < BLOCK, SPECIES * rows + s + PART, -1)
        picks.append(lanes == lane)
    picker = jnp.concatenate([jnp.where(p, 1.0, 0.0).astype(BF) for p in picks], axis=0)
    group = lax.broadcasted_iota(jnp.int32, (GH, 128), 1)
    group = jnp.where(group >= 2 * PART, group - 2 * PART, jnp.where(group >= PART, group - PART, group)) >> 2
    pad = jnp.zeros((TALL - BLOCK * GH, 128), F32)
    for b in range(BLOCKS):
        his, los = [], []
        for table in tables:
            hi, lo = split(pltpu.roll(table, 128 - b * BLOCK, 1) if b else table)
            his.append(hi)
            los.append(lo)
        wide = dot(jnp.concatenate(his + los, axis=1), picker, NN)
        for half in range(2):
            part = wide[half * GH : (half + 1) * GH, :]
            block = jnp.concatenate([jnp.where(group == i, part, 0.0) for i in range(BLOCK)] + [pad], axis=0)
            start = (half * BLOCKS + b) * TALL
            weights[start : start + TALL, :] = block.astype(BF)


def fold(x):
    return jnp.sum(x.reshape(GH // 8, 8, RAD), axis=0)


def span(level, half):
    start = (half * BLOCKS + level // BLOCK) * TALL + level % BLOCK * GH
    return slice(start, start + GH)


def first_kernel(side, arrived, member, weights, emit, shine, trans, glow, passing, thick, sums, edge, stage, pooled, warm, amounts):
    lane = lax.broadcasted_iota(jnp.int32, (PEERS, 128), 1) >> 5
    last = arrived[pl.ds(CHUNK - 1, PEERS, CHUNK), :]
    for m in range(SLOTS):
        part = pl.ds(m, PEERS, SLOTS)
        stage[0, part, :] = arrived[pl.ds(2 * m, PEERS, CHUNK), :]
        stage[1, part, :] = arrived[pl.ds(2 * m + 1, PEERS, CHUNK), :]
        stage[2, part, :] = jnp.where(lane == m, last, 0.0)
    rows = lax.broadcasted_iota(jnp.int32, (RAD, COLS), 0)
    selector = jnp.where(rows == member[...] >> 2, 0.25, 0.0).astype(BF)
    hi, lo = split(jnp.concatenate([stage[k] for k in range(3)], axis=1))
    total = dot(selector, hi, NN) + dot(selector, lo, NN)
    pooled[0:128, :] = total[:, 0:128].T
    pooled[128:256, :] = total[:, 128:256].T
    tail = total[:, 256:384].T
    pooled[256:288, :] = tail[0:32] + tail[32:64] + tail[64:96] + tail[96:128]
    surface = pooled[40:48, :]
    slant = 1.0 / (DIFFUSE * surface[6:7, :])
    warm[...] = jnp.square(jnp.square(pooled[0:ROW, :]))
    thick[...] = pooled[ROW:BASE, :]
    pooled[BASE:FEAT, :] = pooled[BASE:FEAT, :] * (-DIFFUSE * LOG2E)
    pad = jnp.zeros((128 - 3 * PART, RAD), F32)
    for b in range(BLOCKS):
        start = BASE + SPECIES * BLOCK * b
        part = pooled[start : start + PART, :]
        for k, values in enumerate((part, part * slant)):
            hi = values.astype(BF).astype(F32)
            mixture = jnp.concatenate([hi, hi, values - hi, pad], axis=0).astype(BF)
            amounts[k, b * 128 : (b + 1) * 128, :] = mixture

    def depths(half, b):
        rows = slice((half * BLOCKS + b) * TALL, (half * BLOCKS + b + 1) * TALL)
        for k, exponent in enumerate((trans, passing)):
            exponent[rows, :] = dot(weights[rows, :], amounts[k, b * 128 : (b + 1) * 128, :], NN)

    def ahead(order, place):
        if place == 0:
            depths(*order[0])
        if place + 1 < len(order):
            depths(*order[place + 1])

    me = side[0]

    def optics(l, half):
        kept = jnp.exp2(trans[span(l, half), :])
        source = emit[half * GH : (half + 1) * GH, :] * warm[l : l + 1, :]
        added = source - kept * source
        trans[span(l, half), :] = kept
        glow[span(l, half), :] = added
        return kept, added, jnp.exp2(passing[span(l, half), :])

    def note(l, half, change):
        row = slice(8 * l, 8 * l + 8)
        sums[row, :] = sums[row, :] + change if half else change

    @pl.when(me == 0)
    def _():
        order = [(half, b) for half in range(2) for b in range(BLOCKS)]
        for half in range(2):
            part = slice(half * GH, (half + 1) * GH)
            thermal = jnp.zeros((GH, RAD), F32)
            direct = shine[part, :] * surface[7:8, :]
            above = fold(direct)
            for l in range(LEV):
                if l % BLOCK == 0:
                    ahead(order, half * BLOCKS + l // BLOCK)
                kept, added, passed = optics(l, half)
                thermal = kept * thermal + added
                direct = direct * passed
                below = fold(thermal + direct)
                note(l, half, above - below)
                above = below
            edge[part, :] = thermal
            edge[GALL + half * GH : GALL + (half + 1) * GH, :] = direct

    @pl.when(me == 1)
    def _():
        ground = jnp.square(jnp.square(surface[5:6, :]))
        order = [(half, BLOCKS - 1 - b) for half in range(2) for b in range(BLOCKS)]
        for half in range(2):
            part = slice(half * GH, (half + 1) * GH)
            upward = emit[part, :] * ground
            below = fold(upward)
            for l in range(LEV - 1, -1, -1):
                if l % BLOCK == BLOCK - 1:
                    ahead(order, half * BLOCKS + BLOCKS - 1 - l // BLOCK)
                kept, added, passed = optics(l, half)
                passing[span(l, half), :] = passed
                upward = kept * upward + added
                above = fold(upward)
                note(l, half, below - above)
                below = above
            edge[part, :] = upward
        edge[GALL:, :] = jnp.zeros((GALL, RAD), F32)


def second_kernel(side, gotten, trans, glow, passing, thick, sums, spread, send, net, slots):
    me = side[0]

    @pl.when(me == 0)
    def _():
        for half in range(2):
            upward = gotten[half * GH : (half + 1) * GH, :]
            below = fold(upward)
            for l in range(LEV - 1, -1, -1):
                upward = trans[span(l, half), :] * upward + glow[span(l, half), :]
                above = fold(upward)
                row = slice(8 * l, 8 * l + 8)
                net[row, :] = (net if half else sums)[row, :] + (below - above)
                below = above

    @pl.when(me == 1)
    def _():
        for half in range(2):
            thermal = gotten[half * GH : (half + 1) * GH, :]
            direct = gotten[GALL + half * GH : GALL + (half + 1) * GH, :]
            above = fold(thermal + direct)
            for l in range(LEV):
                thermal = trans[span(l, half), :] * thermal + glow[span(l, half), :]
                direct = direct * passing[span(l, half), :]
                below = fold(thermal + direct)
                row = slice(8 * l, 8 * l + 8)
                net[row, :] = (net if half else sums)[row, :] + (above - below)
                above = below

    total = None
    for k in range(8):
        part = net[pl.ds(k, LEV, 8), :]
        total = part if total is None else total + part
    heat = jnp.concatenate([total / thick[0:LEV, :], jnp.zeros((ROW - LEV, RAD), F32)], axis=0)
    gap = jnp.zeros((16, RAD), F32)
    hi, lo = split(jnp.concatenate([heat, gap, heat, gap], axis=0))
    slots[...] = dot(spread[...], hi, NT) + dot(spread[...], lo, NT)
    lanes = lax.broadcasted_iota(jnp.int32, (PEERS, RAD), 1)
    for h in range(2):
        even, odd = slots[pl.ds(2 * h, PEERS, SLOTS), :], slots[pl.ds(2 * h + 1, PEERS, SLOTS), :]
        send[pl.ds(h, PEERS, 2), :] = jnp.where(lanes < 64, even, odd)


def unplace_kernel(returned, placing, heating):
    parts = []
    for h in range(2):
        turned = returned[pl.ds(h, PEERS, 2), :].T
        parts += [turned[0:ROW, :], turned[64 : 64 + ROW, :]]
    hi, lo = split(jnp.concatenate(parts, axis=1))
    heating[...] = (dot(hi, placing[...], NN) + dot(lo, placing[...], NN))[0:LEV, :]


def mix_kernel(tracers, adj, coef, from_left, from_right, mixed, high, low, band, stage):
    spare = LEV * SPECIES
    stage[spare:BODY, :] = jnp.zeros((BODY - spare, COLS), F32)
    for l in range(LEV):
        stage[SPECIES * l : SPECIES * (l + 1), :] = tracers[l]
    parts = (from_left[0:BODY, :], stage[...], from_right[0:BODY, :])
    for part, start in zip(parts, (0, REACH, REACH + COLS)):
        hi, lo = split(part)
        high[0, :, start : start + part.shape[1]] = hi
        low[0, :, start : start + part.shape[1]] = lo
    tables = jnp.concatenate([from_left[BODY:, :], mixing_table(adj, coef), from_right[BODY:, :]], axis=1)
    shifted = pltpu.roll(tables, WIDE - HALO, 1)
    rows = lax.broadcasted_iota(jnp.int32, (256, 128), 0).astype(F32)
    lanes = lax.broadcasted_iota(jnp.int32, (1, 128), 1).astype(F32)

    def build(source, k):
        part = source[:, k * 128 : (k + 1) * 128]
        blend = jnp.where(rows == lanes + HALO, 1.0 - jnp.sum(part[8:14, :], axis=0, keepdims=True), 0.0)
        for n in range(NEAR):
            blend = blend + jnp.where(rows == lanes + part[n : n + 1, :], part[8 + n : 9 + n, :], 0.0)
        return split(blend)

    for k in range(7):
        hi, lo = build(shifted, k)
        band[0, 0, k] = hi
        band[0, 1, k] = lo
    for k in range(6):
        hi, lo = build(tables, k + 1)
        band[1, 0, k] = hi
        band[1, 1, k] = lo
    for step in range(STEPS):
        now, later = step % 2, (step + 1) % 2
        tiles = 7 - step
        first = step // 2
        for k in range(tiles):
            window = slice(k * 128, k * 128 + 256)
            bh, bl = band[now, 0, k + first], band[now, 1, k + first]
            xh, xl = high[now, :, window], low[now, :, window]
            new = dot(xh, bh, NN) + (dot(xh, bl, NN) + dot(xl, bh, NN))
            if step < STEPS - 1:
                hi, lo = split(new)
                high[later, :, k * 128 : (k + 1) * 128] = hi
                low[later, :, k * 128 : (k + 1) * 128] = lo
            else:
                for l in range(LEV):
                    mixed[l, :, k * 128 : (k + 1) * 128] = new[SPECIES * l : SPECIES * (l + 1), :]


def shape(*dims):
    return jax.ShapeDtypeStruct(dims, F32)


LENGTH = {"pack": 27, "join": 5, "weight": 7, "mix": 42, "first": 20, "second": 9, "unplace": 10}


def call(kernel, name, out_shape, scratch, vmem_limit_bytes=16 << 20, **specs):
    return pl.pallas_call(
        kernel,
        out_shape=out_shape,
        scratch_shapes=scratch,
        compiler_params=pltpu.CompilerParams(vmem_limit_bytes=vmem_limit_bytes),
        cost_estimate=pl.CostEstimate(flops=LENGTH[name] * 10**8, bytes_accessed=1 << 18, transcendentals=0),
        **specs,
    )


def per_device(
    stratum_warmth_anomaly,
    pressure_depth,
    absorber_amounts,
    ground_warmth_anomaly,
    sun_elevation_factor,
    daytime_mask,
    dispatch_position,
    arrival_membership,
    adjacency_table,
    blending_coefficient,
    opacity_table,
    emission_share,
    sunshine_share,
):
    n = lax.axis_size("grp")
    up = [(i, (i + 1) % n) for i in range(n)]
    down = [(j, i) for i, j in up]
    swap = [(0, 1), (1, 0)]
    halo_rows = BODY + 16
    tracers = jnp.transpose(absorber_amounts, (1, 0, 2))

    hbm = pl.BlockSpec(memory_space=pltpu.HBM)
    packed = (shape(PEERS * CHUNK, 128), shape(halo_rows, REACH), shape(halo_rows, REACH))
    given = ((LEV, COLS), (LEV, COLS), (LEV, SPECIES, COLS), (1, COLS), (1, COLS))
    send, right, left = call(
        pack_kernel,
        "pack",
        packed,
        [pltpu.VMEM(dims, F32) for dims in given]
        + [pltpu.VMEM((rows, COLS), jnp.int32) for rows in (1, 1, NEAR)]
        + [pltpu.VMEM((NEAR, COLS), F32)]
        + [pltpu.VMEM(out.shape, F32) for out in packed]
        + [pltpu.VMEM((FEAT, COLS), F32), pltpu.SemaphoreType.DMA((9,)), pltpu.SemaphoreType.DMA((4,))],
        in_specs=[hbm] * 9,
        out_specs=[hbm] * 3,
        vmem_limit_bytes=60 << 20,
    )(
        stratum_warmth_anomaly,
        pressure_depth,
        tracers,
        ground_warmth_anomaly[None],
        sun_elevation_factor[None],
        daytime_mask[None],
        dispatch_position,
        adjacency_table,
        blending_coefficient,
    )
    from_left = lax.ppermute(right, "grp", up)
    from_right = lax.ppermute(left, "grp", down)
    arrived = lax.all_to_all(
        send.reshape(PEERS * CHUNK, 1, 128), "grp", split_axis=0, concat_axis=0, tiled=True
    )
    mixed = call(
        mix_kernel,
        "mix",
        shape(LEV, SPECIES, COLS),
        [
            pltpu.VMEM((2, BODY, WIDE), BF),
            pltpu.VMEM((2, BODY, WIDE), BF),
            pltpu.VMEM((2, 2, 7, 256, 128), BF),
            pltpu.VMEM((BODY, COLS), F32),
        ],
    )(tracers, adjacency_table, blending_coefficient, from_left, from_right)
    side = lax.axis_index("sec").astype(jnp.int32)[None]
    opacity = call(join_kernel, "join", shape(SPECIES, GH, 128), [])(
        opacity_table, emission_share[None], sunshine_share[None]
    )
    whole = pl.BlockSpec(memory_space=pltpu.VMEM)
    scalar = pl.BlockSpec(memory_space=pltpu.SMEM)
    weights, emit, shine, spread, placing = call(
        weight_kernel,
        "weight",
        (
            jax.ShapeDtypeStruct((DEEP, 128), BF),
            shape(GALL, RAD),
            shape(GALL, RAD),
            jax.ShapeDtypeStruct((COLS, RAD), BF),
            jax.ShapeDtypeStruct((COLS, COLS), BF),
        ),
        [pltpu.VMEM((2, SPECIES, GH, 128), F32)],
        in_specs=[scalar] + [whole] * 4,
    )(side, opacity, lax.ppermute(opacity, "sec", swap), arrival_membership, dispatch_position)
    arrived, mixed, weights, emit, shine, spread, placing, side = lax.optimization_barrier(
        (arrived, mixed, weights, emit, shine, spread, placing, side)
    )
    trans, glow, passing, thick, sums, edge = call(
        first_kernel,
        "first",
        (
            shape(DEEP, RAD),
            shape(DEEP, RAD),
            shape(DEEP, RAD),
            shape(ROW, RAD),
            shape(8 * LEV, RAD),
            shape(2 * GALL, RAD),
        ),
        [
            pltpu.VMEM((3, COLS, 128), F32),
            pltpu.VMEM((FEAT, RAD), F32),
            pltpu.VMEM((ROW, RAD), F32),
            pltpu.VMEM((2, BLOCKS * 128, RAD), BF),
        ],
        in_specs=[scalar] + [whole] * 5,
    )(side, arrived.reshape(PEERS * CHUNK, 128), arrival_membership, weights, emit, shine)
    gotten = lax.ppermute(edge, "sec", swap)
    back = call(
        second_kernel,
        "second",
        shape(PEERS * 2, 128),
        [pltpu.VMEM((8 * LEV, RAD), F32), pltpu.VMEM((COLS, RAD), F32)],
        in_specs=[scalar] + [whole] * 7,
    )(side, gotten, trans, glow, passing, thick, sums, spread)
    returned = lax.all_to_all(
        back.reshape(PEERS * 2, 1, 128), "grp", split_axis=0, concat_axis=0, tiled=True
    ).reshape(PEERS * 2, 128)
    heating = call(unplace_kernel, "unplace", shape(LEV, COLS), [])(returned, placing)
    return (heating, jnp.transpose(mixed, (1, 0, 2)))


def solution(mesh):
    in_specs = (
        P("sec", "grp"),
        P("sec", "grp"),
        P(None, "sec", "grp"),
        P("grp"),
        P("grp"),
        P("grp"),
        P("grp", None),
        P("grp", None),
        P(None, "grp"),
        P(None, "grp"),
        P(None, "sec", None),
        P("sec"),
        P("sec"),
    )
    out_specs = (P("sec", "grp"), P(None, "sec", "grp"))
    return jax.shard_map(
        per_device, mesh=mesh, in_specs=in_specs, out_specs=out_specs, check_vma=False
    )
```

```python
import math

import jax
import jax.numpy as jnp
from jax import lax
from jax.experimental import pallas as pl
from jax.experimental.pallas import tpu as pltpu
from jax.sharding import PartitionSpec as P


STEPS = 4
HALO = 64
DIFFUSE = 1.66
LOG2E = math.log2(math.e)
BF = jnp.bfloat16
F32 = jnp.float32

PEERS = 128
SLOTS = 4
COLS = 512
LEV = 45
ROW = 48
BASE = 2 * ROW
BODY = 192
FEAT = BASE + BODY
CHUNK = SLOTS * FEAT // 128
RAD = 128
GH = 56
REACH = STEPS * HALO
WIDE = COLS + 2 * REACH
SPECIES = 4
NEAR = 6
BLOCK = 9
BLOCKS = LEV // BLOCK
GALL = 2 * GH
TALL = 512
DEEP = 2 * BLOCKS * TALL
PART = 40
NT = (((1,), (1,)), ((), ()))
NN = (((1,), (0,)), ((), ()))


def split(x):
    hi = x.astype(BF)
    return hi, (x - hi.astype(F32)).astype(BF)


def dot(a, b, dims):
    return lax.dot_general(a, b, dims, preferred_element_type=F32)


def slot_matrix(position):
    rows = lax.broadcasted_iota(jnp.int32, (COLS, COLS), 0)
    slot = (rows & (PEERS - 1)) * SLOTS + (rows >> 7)
    return jnp.where(slot == position, 1.0, 0.0).astype(BF)


def mixing_table(adj, coef):
    column = lax.broadcasted_iota(jnp.int32, (NEAR, COLS), 1)
    pad = jnp.zeros((2, COLS), F32)
    return jnp.concatenate([(adj[...] - column).astype(F32), pad, coef[...], pad], axis=0)


def pack_kernel(*refs):
    sources, outs, scratch = refs[:9], refs[9:12], refs[12:]
    temp, thick, tracers, ground, sun, day, pos, adj, coef = scratch[:9]
    send, right, left, bundle, sems, done = scratch[9:]
    copies = [pltpu.make_async_copy(a, b, sems.at[i]) for i, (a, b) in enumerate(zip(sources, scratch))]
    for i in (6, 7, 8, 2, 0, 1, 3, 4, 5):
        copies[i].start()
    middle = PEERS * CHUNK // 2
    pairs = [(send.at[0:middle, :], outs[0].at[0:middle, :]), (right, outs[1]), (left, outs[2])]
    pairs.append((send.at[middle : 2 * middle, :], outs[0].at[middle : 2 * middle, :]))
    stores = [pltpu.make_async_copy(a, b, done.at[i]) for i, (a, b) in enumerate(pairs)]
    bundle[ROW + LEV : BASE, :] = jnp.zeros((ROW - LEV, COLS), F32)
    spare = BASE + LEV * SPECIES
    bundle[spare:FEAT, :] = jnp.zeros((FEAT - spare, COLS), F32)
    for i in (6, 7, 8):
        copies[i].wait()
    placing = slot_matrix(pos[...])
    both = mixing_table(adj, coef)
    right[BODY : BODY + 16, :] = both[:, COLS - REACH :]
    left[BODY : BODY + 16, :] = both[:, :REACH]
    copies[2].wait()
    for l in range(LEV):
        bundle[BASE + SPECIES * l : BASE + SPECIES * (l + 1), :] = tracers[l]
    right[0:BODY, :] = bundle[BASE:FEAT, COLS - REACH :]
    left[0:BODY, :] = bundle[BASE:FEAT, :REACH]
    for i in (1, 2):
        stores[i].start()
    for i in (0, 1, 3, 4, 5):
        copies[i].wait()
    bundle[0:LEV, :] = temp[...]
    bundle[ROW : ROW + LEV, :] = thick[...]
    sunny = sun[...]
    bundle[LEV : LEV + 1, :] = ground[...]
    bundle[LEV + 1 : LEV + 2, :] = sunny
    bundle[LEV + 2 : LEV + 3, :] = day[...].astype(F32) * sunny
    hi, lo = split(bundle[...])
    tails = []
    for m in range(SLOTS):
        if m % 2 == 0:
            pair = placing[m * PEERS : (m + 2) * PEERS, :]
            packed = dot(hi, pair, NT) + dot(lo, pair, NT)
        block = packed[:, m % 2 * PEERS : (m % 2 + 1) * PEERS]
        send[pl.ds(2 * m, PEERS, CHUNK), :] = block[0:128, :].T
        send[pl.ds(2 * m + 1, PEERS, CHUNK), :] = block[128:256, :].T
        tails.append(block[256:288, :])
    send[pl.ds(CHUNK - 1, PEERS, CHUNK), :] = jnp.concatenate(tails, axis=0).T
    stores[0].start()
    stores[3].start()
    for store in stores:
        store.wait()


def join_kernel(opacity, emission, sunshine, joined):
    rows = lax.broadcasted_iota(jnp.int32, (GH, GH), 0)
    lanes = lax.broadcasted_iota(jnp.int32, (GH, GH), 1)
    for s in range(SPECIES):
        joined[s] = jnp.zeros((GH, 128), F32)
        joined[s, :, 0 : 2 * LEV] = opacity[s]
    for k, share in enumerate((emission, sunshine)):
        square = jnp.where(rows == lanes, jnp.broadcast_to(share[...], (GH, GH)), 0.0)
        joined[0, :, 2 * LEV + k : 2 * LEV + k + 1] = jnp.sum(square, axis=1, keepdims=True)


def weight_kernel(side, own, other, member, pos, weights, emit, shine, spread, placing, full):
    placing[...] = slot_matrix(pos[...])
    ids = (member[...] >> 2).astype(F32)
    spots = lax.broadcasted_iota(jnp.int32, (128, RAD), 1).astype(F32)
    for k in range(SLOTS):
        part = slice(k * 128, (k + 1) * 128)
        column = jnp.broadcast_to(ids[:, part], (128, 128)).T
        spread[part, :] = jnp.where(column == spots, 1.0, 0.0).astype(BF)
    me = side[0]
    full[pl.ds(me, 1)] = own[...][None]
    full[pl.ds(1 - me, 1)] = other[...][None]
    shift = lax.rem(128 - LEV * me, 128)
    tables = [jnp.concatenate([full[0, s], full[1, s]], axis=0) for s in range(SPECIES)]
    emit[...] = jnp.broadcast_to(tables[0][:, 2 * LEV : 2 * LEV + 1], (GALL, RAD))
    shine[...] = jnp.broadcast_to(tables[0][:, 2 * LEV + 1 : 2 * LEV + 2], (GALL, RAD))
    tables = [pltpu.roll(table, shift, 1) for table in tables]
    rows = lax.broadcasted_iota(jnp.int32, (128, 128), 0)
    lanes = lax.broadcasted_iota(jnp.int32, (128, 128), 1)
    picks = []
    for s in range(SPECIES):
        lane = jnp.where(rows < BLOCK, SPECIES * rows + s, -1)
        picks.append((lanes == lane) | (lanes == jnp.where(lane < 0, -1, lane + 2 * PART)))
    for s in range(SPECIES):
        lane = jnp.where(rows < BLOCK, SPECIES * rows + s + PART, -1)
        picks.append(lanes == lane)
    picker = jnp.concatenate([jnp.where(p, 1.0, 0.0).astype(BF) for p in picks], axis=0)
    group = lax.broadcasted_iota(jnp.int32, (GH, 128), 1)
    group = jnp.where(group >= 2 * PART, group - 2 * PART, jnp.where(group >= PART, group - PART, group)) >> 2
    pad = jnp.zeros((TALL - BLOCK * GH, 128), F32)
    for b in range(BLOCKS):
        his, los = [], []
        for table in tables:
            hi, lo = split(pltpu.roll(table, 128 - b * BLOCK, 1) if b else table)
            his.append(hi)
            los.append(lo)
        wide = dot(jnp.concatenate(his + los, axis=1), picker, NN)
        for half in range(2):
            part = wide[half * GH : (half + 1) * GH, :]
            block = jnp.concatenate([jnp.where(group == i, part, 0.0) for i in range(BLOCK)] + [pad], axis=0)
            start = (half * BLOCKS + b) * TALL
            weights[start : start + TALL, :] = block.astype(BF)


def fold(x):
    return jnp.sum(x.reshape(GH // 8, 8, RAD), axis=0)


def span(level, half):
    start = (half * BLOCKS + level // BLOCK) * TALL + level % BLOCK * GH
    return slice(start, start + GH)


def first_kernel(side, arrived, member, weights, emit, shine, trans, glow, passing, thick, sums, edge, stage, pooled, warm, amounts):
    lane = lax.broadcasted_iota(jnp.int32, (PEERS, 128), 1) >> 5
    last = arrived[pl.ds(CHUNK - 1, PEERS, CHUNK), :]
    for m in range(SLOTS):
        part = pl.ds(m, PEERS, SLOTS)
        stage[0, part, :] = arrived[pl.ds(2 * m, PEERS, CHUNK), :]
        stage[1, part, :] = arrived[pl.ds(2 * m + 1, PEERS, CHUNK), :]
        stage[2, part, :] = jnp.where(lane == m, last, 0.0)
    rows = lax.broadcasted_iota(jnp.int32, (RAD, COLS), 0)
    selector = jnp.where(rows == member[...] >> 2, 0.25, 0.0).astype(BF)
    hi, lo = split(jnp.concatenate([stage[k] for k in range(3)], axis=1))
    total = dot(selector, hi, NN) + dot(selector, lo, NN)
    pooled[0:128, :] = total[:, 0:128].T
    pooled[128:256, :] = total[:, 128:256].T
    tail = total[:, 256:384].T
    pooled[256:288, :] = tail[0:32] + tail[32:64] + tail[64:96] + tail[96:128]
    surface = pooled[40:48, :]
    slant = 1.0 / (DIFFUSE * surface[6:7, :])
    warm[...] = jnp.square(jnp.square(pooled[0:ROW, :]))
    thick[...] = pooled[ROW:BASE, :]
    pooled[BASE:FEAT, :] = pooled[BASE:FEAT, :] * (-DIFFUSE * LOG2E)
    pad = jnp.zeros((128 - 3 * PART, RAD), F32)
    for b in range(BLOCKS):
        start = BASE + SPECIES * BLOCK * b
        part = pooled[start : start + PART, :]
        for k, values in enumerate((part, part * slant)):
            hi = values.astype(BF).astype(F32)
            mixture = jnp.concatenate([hi, hi, values - hi, pad], axis=0).astype(BF)
            amounts[k, b * 128 : (b + 1) * 128, :] = mixture

    def depths(half, b):
        rows = slice((half * BLOCKS + b) * TALL, (half * BLOCKS + b + 1) * TALL)
        for k, exponent in enumerate((trans, passing)):
            exponent[rows, :] = dot(weights[rows, :], amounts[k, b * 128 : (b + 1) * 128, :], NN)

    def ahead(order, place):
        if place == 0:
            depths(*order[0])
        if place + 1 < len(order):
            depths(*order[place + 1])

    me = side[0]

    def optics(l, half):
        kept = jnp.exp2(trans[span(l, half), :])
        source = emit[half * GH : (half + 1) * GH, :] * warm[l : l + 1, :]
        added = source - kept * source
        trans[span(l, half), :] = kept
        glow[span(l, half), :] = added
        return kept, added, jnp.exp2(passing[span(l, half), :])

    def note(l, half, change):
        row = slice(8 * l, 8 * l + 8)
        sums[row, :] = sums[row, :] + change if half else change

    @pl.when(me == 0)
    def _():
        order = [(half, b) for half in range(2) for b in range(BLOCKS)]
        for half in range(2):
            part = slice(half * GH, (half + 1) * GH)
            thermal = jnp.zeros((GH, RAD), F32)
            direct = shine[part, :] * surface[7:8, :]
            above = fold(direct)
            for l in range(LEV):
                if l % BLOCK == 0:
                    ahead(order, half * BLOCKS + l // BLOCK)
                kept, added, passed = optics(l, half)
                thermal = kept * thermal + added
                direct = direct * passed
                below = fold(thermal + direct)
                note(l, half, above - below)
                above = below
            edge[part, :] = thermal
            edge[GALL + half * GH : GALL + (half + 1) * GH, :] = direct

    @pl.when(me == 1)
    def _():
        ground = jnp.square(jnp.square(surface[5:6, :]))
        order = [(half, BLOCKS - 1 - b) for half in range(2) for b in range(BLOCKS)]
        for half in range(2):
            part = slice(half * GH, (half + 1) * GH)
            upward = emit[part, :] * ground
            below = fold(upward)
            for l in range(LEV - 1, -1, -1):
                if l % BLOCK == BLOCK - 1:
                    ahead(order, half * BLOCKS + BLOCKS - 1 - l // BLOCK)
                kept, added, passed = optics(l, half)
                passing[span(l, half), :] = passed
                upward = kept * upward + added
                above = fold(upward)
                note(l, half, below - above)
                below = above
            edge[part, :] = upward
        edge[GALL:, :] = jnp.zeros((GALL, RAD), F32)


def second_kernel(side, gotten, trans, glow, passing, thick, sums, spread, send, net, slots):
    me = side[0]

    @pl.when(me == 0)
    def _():
        for half in range(2):
            upward = gotten[half * GH : (half + 1) * GH, :]
            below = fold(upward)
            for l in range(LEV - 1, -1, -1):
                upward = trans[span(l, half), :] * upward + glow[span(l, half), :]
                above = fold(upward)
                row = slice(8 * l, 8 * l + 8)
                net[row, :] = (net if half else sums)[row, :] + (below - above)
                below = above

    @pl.when(me == 1)
    def _():
        for half in range(2):
            thermal = gotten[half * GH : (half + 1) * GH, :]
            direct = gotten[GALL + half * GH : GALL + (half + 1) * GH, :]
            above = fold(thermal + direct)
            for l in range(LEV):
                thermal = trans[span(l, half), :] * thermal + glow[span(l, half), :]
                direct = direct * passing[span(l, half), :]
                below = fold(thermal + direct)
                row = slice(8 * l, 8 * l + 8)
                net[row, :] = (net if half else sums)[row, :] + (above - below)
                above = below

    total = None
    for k in range(8):
        part = net[pl.ds(k, LEV, 8), :]
        total = part if total is None else total + part
    heat = jnp.concatenate([total / thick[0:LEV, :], jnp.zeros((ROW - LEV, RAD), F32)], axis=0)
    gap = jnp.zeros((16, RAD), F32)
    hi, lo = split(jnp.concatenate([heat, gap, heat, gap], axis=0))
    slots[...] = dot(spread[...], hi, NT) + dot(spread[...], lo, NT)
    lanes = lax.broadcasted_iota(jnp.int32, (PEERS, RAD), 1)
    for h in range(2):
        even, odd = slots[pl.ds(2 * h, PEERS, SLOTS), :], slots[pl.ds(2 * h + 1, PEERS, SLOTS), :]
        send[pl.ds(h, PEERS, 2), :] = jnp.where(lanes < 64, even, odd)


def unplace_kernel(returned, placing, heating):
    parts = []
    for h in range(2):
        turned = returned[pl.ds(h, PEERS, 2), :].T
        parts += [turned[0:ROW, :], turned[64 : 64 + ROW, :]]
    hi, lo = split(jnp.concatenate(parts, axis=1))
    heating[...] = (dot(hi, placing[...], NN) + dot(lo, placing[...], NN))[0:LEV, :]


def mix_kernel(tracers, adj, coef, from_left, from_right, mixed, high, low, band, stage):
    spare = LEV * SPECIES
    stage[spare:BODY, :] = jnp.zeros((BODY - spare, COLS), F32)
    for l in range(LEV):
        stage[SPECIES * l : SPECIES * (l + 1), :] = tracers[l]
    parts = (from_left[0:BODY, :], stage[...], from_right[0:BODY, :])
    for part, start in zip(parts, (0, REACH, REACH + COLS)):
        hi, lo = split(part)
        high[0, :, start : start + part.shape[1]] = hi
        low[0, :, start : start + part.shape[1]] = lo
    tables = jnp.concatenate([from_left[BODY:, :], mixing_table(adj, coef), from_right[BODY:, :]], axis=1)
    shifted = pltpu.roll(tables, WIDE - HALO, 1)
    rows = lax.broadcasted_iota(jnp.int32, (256, 128), 0).astype(F32)
    lanes = lax.broadcasted_iota(jnp.int32, (1, 128), 1).astype(F32)

    def build(source, k):
        part = source[:, k * 128 : (k + 1) * 128]
        blend = jnp.where(rows == lanes + HALO, 1.0 - jnp.sum(part[8:14, :], axis=0, keepdims=True), 0.0)
        for n in range(NEAR):
            blend = blend + jnp.where(rows == lanes + part[n : n + 1, :], part[8 + n : 9 + n, :], 0.0)
        return split(blend)

    for k in range(7):
        hi, lo = build(shifted, k)
        band[0, 0, k] = hi
        band[0, 1, k] = lo
    for k in range(6):
        hi, lo = build(tables, k + 1)
        band[1, 0, k] = hi
        band[1, 1, k] = lo
    for step in range(STEPS):
        now, later = step % 2, (step + 1) % 2
        tiles = 7 - step
        first = step // 2
        for k in range(tiles):
            window = slice(k * 128, k * 128 + 256)
            bh, bl = band[now, 0, k + first], band[now, 1, k + first]
            xh, xl = high[now, :, window], low[now, :, window]
            new = dot(xh, bh, NN) + (dot(xh, bl, NN) + dot(xl, bh, NN))
            if step < STEPS - 1:
                hi, lo = split(new)
                high[later, :, k * 128 : (k + 1) * 128] = hi
                low[later, :, k * 128 : (k + 1) * 128] = lo
            else:
                for l in range(LEV):
                    mixed[l, :, k * 128 : (k + 1) * 128] = new[SPECIES * l : SPECIES * (l + 1), :]


def shape(*dims):
    return jax.ShapeDtypeStruct(dims, F32)


LENGTH = {"pack": 27, "join": 5, "weight": 7, "mix": 42, "first": 20, "second": 9, "unplace": 10}


def call(kernel, name, out_shape, scratch, vmem_limit_bytes=16 << 20, **specs):
    return pl.pallas_call(
        kernel,
        out_shape=out_shape,
        scratch_shapes=scratch,
        compiler_params=pltpu.CompilerParams(vmem_limit_bytes=vmem_limit_bytes),
        cost_estimate=pl.CostEstimate(flops=LENGTH[name] * 10**8, bytes_accessed=1 << 18, transcendentals=0),
        **specs,
    )


def per_device(
    stratum_warmth_anomaly,
    pressure_depth,
    absorber_amounts,
    ground_warmth_anomaly,
    sun_elevation_factor,
    daytime_mask,
    dispatch_position,
    arrival_membership,
    adjacency_table,
    blending_coefficient,
    opacity_table,
    emission_share,
    sunshine_share,
):
    n = lax.axis_size("grp")
    up = [(i, (i + 1) % n) for i in range(n)]
    down = [(j, i) for i, j in up]
    swap = [(0, 1), (1, 0)]
    halo_rows = BODY + 16
    tracers = jnp.transpose(absorber_amounts, (1, 0, 2))

    hbm = pl.BlockSpec(memory_space=pltpu.HBM)
    packed = (shape(PEERS * CHUNK, 128), shape(halo_rows, REACH), shape(halo_rows, REACH))
    given = ((LEV, COLS), (LEV, COLS), (LEV, SPECIES, COLS), (1, COLS), (1, COLS))
    send, right, left = call(
        pack_kernel,
        "pack",
        packed,
        [pltpu.VMEM(dims, F32) for dims in given]
        + [pltpu.VMEM((rows, COLS), jnp.int32) for rows in (1, 1, NEAR)]
        + [pltpu.VMEM((NEAR, COLS), F32)]
        + [pltpu.VMEM(out.shape, F32) for out in packed]
        + [pltpu.VMEM((FEAT, COLS), F32), pltpu.SemaphoreType.DMA((9,)), pltpu.SemaphoreType.DMA((4,))],
        in_specs=[hbm] * 9,
        out_specs=[hbm] * 3,
        vmem_limit_bytes=60 << 20,
    )(
        stratum_warmth_anomaly,
        pressure_depth,
        tracers,
        ground_warmth_anomaly[None],
        sun_elevation_factor[None],
        daytime_mask[None],
        dispatch_position,
        adjacency_table,
        blending_coefficient,
    )
    from_left = lax.ppermute(right, "grp", up)
    from_right = lax.ppermute(left, "grp", down)
    arrived = lax.all_to_all(
        send.reshape(PEERS * CHUNK, 1, 128), "grp", split_axis=0, concat_axis=0, tiled=True
    )
    side = lax.axis_index("sec").astype(jnp.int32)[None]
    opacity = call(join_kernel, "join", shape(SPECIES, GH, 128), [])(
        opacity_table, emission_share[None], sunshine_share[None]
    )
    whole = pl.BlockSpec(memory_space=pltpu.VMEM)
    scalar = pl.BlockSpec(memory_space=pltpu.SMEM)
    weights, emit, shine, spread, placing = call(
        weight_kernel,
        "weight",
        (
            jax.ShapeDtypeStruct((DEEP, 128), BF),
            shape(GALL, RAD),
            shape(GALL, RAD),
            jax.ShapeDtypeStruct((COLS, RAD), BF),
            jax.ShapeDtypeStruct((COLS, COLS), BF),
        ),
        [pltpu.VMEM((2, SPECIES, GH, 128), F32)],
        in_specs=[scalar] + [whole] * 4,
    )(side, opacity, lax.ppermute(opacity, "sec", swap), arrival_membership, dispatch_position)
    arrived, weights, emit, shine, spread, placing, side = lax.optimization_barrier(
        (arrived, weights, emit, shine, spread, placing, side)
    )
    trans, glow, passing, thick, sums, edge = call(
        first_kernel,
        "first",
        (
            shape(DEEP, RAD),
            shape(DEEP, RAD),
            shape(DEEP, RAD),
            shape(ROW, RAD),
            shape(8 * LEV, RAD),
            shape(2 * GALL, RAD),
        ),
        [
            pltpu.VMEM((3, COLS, 128), F32),
            pltpu.VMEM((FEAT, RAD), F32),
            pltpu.VMEM((ROW, RAD), F32),
            pltpu.VMEM((2, BLOCKS * 128, RAD), BF),
        ],
        in_specs=[scalar] + [whole] * 5,
    )(side, arrived.reshape(PEERS * CHUNK, 128), arrival_membership, weights, emit, shine)
    gotten = lax.ppermute(edge, "sec", swap)
    back = call(
        second_kernel,
        "second",
        shape(PEERS * 2, 128),
        [pltpu.VMEM((8 * LEV, RAD), F32), pltpu.VMEM((COLS, RAD), F32)],
        in_specs=[scalar] + [whole] * 7,
    )(side, gotten, trans, glow, passing, thick, sums, spread)
    returned = lax.all_to_all(
        back.reshape(PEERS * 2, 1, 128), "grp", split_axis=0, concat_axis=0, tiled=True
    ).reshape(PEERS * 2, 128)
    mixed = call(
        mix_kernel,
        "mix",
        shape(LEV, SPECIES, COLS),
        [
            pltpu.VMEM((2, BODY, WIDE), BF),
            pltpu.VMEM((2, BODY, WIDE), BF),
            pltpu.VMEM((2, 2, 7, 256, 128), BF),
            pltpu.VMEM((BODY, COLS), F32),
        ],
    )(tracers, adjacency_table, blending_coefficient, from_left, from_right)
    returned, mixed = lax.optimization_barrier((returned, mixed))
    heating = call(unplace_kernel, "unplace", shape(LEV, COLS), [])(returned, placing)
    return (heating, jnp.transpose(mixed, (1, 0, 2)))


def solution(mesh):
    in_specs = (
        P("sec", "grp"),
        P("sec", "grp"),
        P(None, "sec", "grp"),
        P("grp"),
        P("grp"),
        P("grp"),
        P("grp", None),
        P("grp", None),
        P(None, "grp"),
        P(None, "grp"),
        P(None, "sec", None),
        P("sec"),
        P("sec"),
    )
    out_specs = (P("sec", "grp"), P(None, "sec", "grp"))
    return jax.shard_map(
        per_device, mesh=mesh, in_specs=in_specs, out_specs=out_specs, check_vma=False
    )
```

```python
import math

import jax
import jax.numpy as jnp
from jax import lax
from jax.experimental import pallas as pl
from jax.experimental.pallas import tpu as pltpu
from jax.sharding import PartitionSpec as P


STEPS = 4
HALO = 64
DIFFUSE = 1.66
LOG2E = math.log2(math.e)
BF = jnp.bfloat16
F32 = jnp.float32

PEERS = 128
SLOTS = 4
COLS = 512
LEV = 45
ROW = 48
BASE = 2 * ROW
BODY = 192
FEAT = BASE + BODY
CHUNK = SLOTS * FEAT // 128
RAD = 128
GH = 56
REACH = STEPS * HALO
WIDE = COLS + 2 * REACH
SPECIES = 4
NEAR = 6
BLOCK = 9
BLOCKS = LEV // BLOCK
GALL = 2 * GH
TALL = 512
DEEP = 2 * BLOCKS * TALL
PART = 40
NT = (((1,), (1,)), ((), ()))
NN = (((1,), (0,)), ((), ()))


def split(x):
    hi = x.astype(BF)
    return hi, (x - hi.astype(F32)).astype(BF)


def dot(a, b, dims):
    return lax.dot_general(a, b, dims, preferred_element_type=F32)


def slot_matrix(position):
    rows = lax.broadcasted_iota(jnp.int32, (COLS, COLS), 0)
    slot = (rows & (PEERS - 1)) * SLOTS + (rows >> 7)
    return jnp.where(slot == position, 1.0, 0.0).astype(BF)


def mixing_table(adj, coef):
    column = lax.broadcasted_iota(jnp.int32, (NEAR, COLS), 1)
    pad = jnp.zeros((2, COLS), F32)
    return jnp.concatenate([(adj[...] - column).astype(F32), pad, coef[...], pad], axis=0)


def pack_kernel(*refs):
    sources, out, scratch = refs[:7], refs[7], refs[8:]
    temp, thick, tracers, ground, sun, day, pos = scratch[:7]
    send, bundle, sems, done = scratch[7:]
    copies = [pltpu.make_async_copy(a, b, sems.at[i]) for i, (a, b) in enumerate(zip(sources, scratch))]
    for i in (6, 2, 0, 1, 3, 4, 5):
        copies[i].start()
    middle = PEERS * CHUNK // 2
    halves = [slice(0, middle), slice(middle, 2 * middle)]
    stores = [pltpu.make_async_copy(send.at[h, :], out.at[h, :], done.at[i]) for i, h in enumerate(halves)]
    bundle[ROW + LEV : BASE, :] = jnp.zeros((ROW - LEV, COLS), F32)
    spare = BASE + LEV * SPECIES
    bundle[spare:FEAT, :] = jnp.zeros((FEAT - spare, COLS), F32)
    copies[6].wait()
    placing = slot_matrix(pos[...])
    copies[2].wait()
    for l in range(LEV):
        bundle[BASE + SPECIES * l : BASE + SPECIES * (l + 1), :] = tracers[l]
    for i in (0, 1, 3, 4, 5):
        copies[i].wait()
    bundle[0:LEV, :] = temp[...]
    bundle[ROW : ROW + LEV, :] = thick[...]
    sunny = sun[...]
    bundle[LEV : LEV + 1, :] = ground[...]
    bundle[LEV + 1 : LEV + 2, :] = sunny
    bundle[LEV + 2 : LEV + 3, :] = day[...].astype(F32) * sunny
    hi, lo = split(bundle[...])
    tails = []
    for m in range(SLOTS):
        if m % 2 == 0:
            pair = placing[m * PEERS : (m + 2) * PEERS, :]
            packed = dot(hi, pair, NT) + dot(lo, pair, NT)
        block = packed[:, m % 2 * PEERS : (m % 2 + 1) * PEERS]
        send[pl.ds(2 * m, PEERS, CHUNK), :] = block[0:128, :].T
        send[pl.ds(2 * m + 1, PEERS, CHUNK), :] = block[128:256, :].T
        tails.append(block[256:288, :])
    send[pl.ds(CHUNK - 1, PEERS, CHUNK), :] = jnp.concatenate(tails, axis=0).T
    for store in stores:
        store.start()
    for store in stores:
        store.wait()


def edge_kernel(tracers, adj, coef, right, left):
    both = mixing_table(adj, coef)
    right[BODY : BODY + 16, :] = both[:, COLS - REACH :]
    left[BODY : BODY + 16, :] = both[:, :REACH]
    spare = LEV * SPECIES
    for side, first in ((right, COLS - REACH), (left, 0)):
        side[spare:BODY, :] = jnp.zeros((BODY - spare, REACH), F32)
        for l in range(LEV):
            side[SPECIES * l : SPECIES * (l + 1), :] = tracers[l, :, first : first + REACH]


def join_kernel(opacity, emission, sunshine, joined):
    rows = lax.broadcasted_iota(jnp.int32, (GH, GH), 0)
    lanes = lax.broadcasted_iota(jnp.int32, (GH, GH), 1)
    for s in range(SPECIES):
        joined[s] = jnp.zeros((GH, 128), F32)
        joined[s, :, 0 : 2 * LEV] = opacity[s]
    for k, share in enumerate((emission, sunshine)):
        square = jnp.where(rows == lanes, jnp.broadcast_to(share[...], (GH, GH)), 0.0)
        joined[0, :, 2 * LEV + k : 2 * LEV + k + 1] = jnp.sum(square, axis=1, keepdims=True)


def weight_kernel(side, own, other, member, pos, weights, emit, shine, spread, placing, full):
    placing[...] = slot_matrix(pos[...])
    ids = (member[...] >> 2).astype(F32)
    spots = lax.broadcasted_iota(jnp.int32, (128, RAD), 1).astype(F32)
    for k in range(SLOTS):
        part = slice(k * 128, (k + 1) * 128)
        column = jnp.broadcast_to(ids[:, part], (128, 128)).T
        spread[part, :] = jnp.where(column == spots, 1.0, 0.0).astype(BF)
    me = side[0]
    full[pl.ds(me, 1)] = own[...][None]
    full[pl.ds(1 - me, 1)] = other[...][None]
    shift = lax.rem(128 - LEV * me, 128)
    tables = [jnp.concatenate([full[0, s], full[1, s]], axis=0) for s in range(SPECIES)]
    emit[...] = jnp.broadcast_to(tables[0][:, 2 * LEV : 2 * LEV + 1], (GALL, RAD))
    shine[...] = jnp.broadcast_to(tables[0][:, 2 * LEV + 1 : 2 * LEV + 2], (GALL, RAD))
    tables = [pltpu.roll(table, shift, 1) for table in tables]
    rows = lax.broadcasted_iota(jnp.int32, (128, 128), 0)
    lanes = lax.broadcasted_iota(jnp.int32, (128, 128), 1)
    picks = []
    for s in range(SPECIES):
        lane = jnp.where(rows < BLOCK, SPECIES * rows + s, -1)
        picks.append((lanes == lane) | (lanes == jnp.where(lane < 0, -1, lane + 2 * PART)))
    for s in range(SPECIES):
        lane = jnp.where(rows < BLOCK, SPECIES * rows + s + PART, -1)
        picks.append(lanes == lane)
    picker = jnp.concatenate([jnp.where(p, 1.0, 0.0).astype(BF) for p in picks], axis=0)
    group = lax.broadcasted_iota(jnp.int32, (GH, 128), 1)
    group = jnp.where(group >= 2 * PART, group - 2 * PART, jnp.where(group >= PART, group - PART, group)) >> 2
    pad = jnp.zeros((TALL - BLOCK * GH, 128), F32)
    for b in range(BLOCKS):
        his, los = [], []
        for table in tables:
            hi, lo = split(pltpu.roll(table, 128 - b * BLOCK, 1) if b else table)
            his.append(hi)
            los.append(lo)
        wide = dot(jnp.concatenate(his + los, axis=1), picker, NN)
        for half in range(2):
            part = wide[half * GH : (half + 1) * GH, :]
            block = jnp.concatenate([jnp.where(group == i, part, 0.0) for i in range(BLOCK)] + [pad], axis=0)
            start = (half * BLOCKS + b) * TALL
            weights[start : start + TALL, :] = block.astype(BF)


def fold(x):
    return jnp.sum(x.reshape(GH // 8, 8, RAD), axis=0)


def span(level, half):
    start = (half * BLOCKS + level // BLOCK) * TALL + level % BLOCK * GH
    return slice(start, start + GH)


def first_kernel(side, arrived, member, weights, emit, shine, trans, glow, passing, thick, sums, edge, stage, pooled, warm, amounts):
    lane = lax.broadcasted_iota(jnp.int32, (PEERS, 128), 1) >> 5
    last = arrived[pl.ds(CHUNK - 1, PEERS, CHUNK), :]
    for m in range(SLOTS):
        part = pl.ds(m, PEERS, SLOTS)
        stage[0, part, :] = arrived[pl.ds(2 * m, PEERS, CHUNK), :]
        stage[1, part, :] = arrived[pl.ds(2 * m + 1, PEERS, CHUNK), :]
        stage[2, part, :] = jnp.where(lane == m, last, 0.0)
    rows = lax.broadcasted_iota(jnp.int32, (RAD, COLS), 0)
    selector = jnp.where(rows == member[...] >> 2, 0.25, 0.0).astype(BF)
    hi, lo = split(jnp.concatenate([stage[k] for k in range(3)], axis=1))
    total = dot(selector, hi, NN) + dot(selector, lo, NN)
    pooled[0:128, :] = total[:, 0:128].T
    pooled[128:256, :] = total[:, 128:256].T
    tail = total[:, 256:384].T
    pooled[256:288, :] = tail[0:32] + tail[32:64] + tail[64:96] + tail[96:128]
    surface = pooled[40:48, :]
    slant = 1.0 / (DIFFUSE * surface[6:7, :])
    warm[...] = jnp.square(jnp.square(pooled[0:ROW, :]))
    thick[...] = pooled[ROW:BASE, :]
    pooled[BASE:FEAT, :] = pooled[BASE:FEAT, :] * (-DIFFUSE * LOG2E)
    pad = jnp.zeros((128 - 3 * PART, RAD), F32)
    for b in range(BLOCKS):
        start = BASE + SPECIES * BLOCK * b
        part = pooled[start : start + PART, :]
        for k, values in enumerate((part, part * slant)):
            hi = values.astype(BF).astype(F32)
            mixture = jnp.concatenate([hi, hi, values - hi, pad], axis=0).astype(BF)
            amounts[k, b * 128 : (b + 1) * 128, :] = mixture

    def depths(half, b):
        rows = slice((half * BLOCKS + b) * TALL, (half * BLOCKS + b + 1) * TALL)
        for k, exponent in enumerate((trans, passing)):
            exponent[rows, :] = dot(weights[rows, :], amounts[k, b * 128 : (b + 1) * 128, :], NN)

    def ahead(order, place):
        if place == 0:
            depths(*order[0])
        if place + 1 < len(order):
            depths(*order[place + 1])

    me = side[0]

    def optics(l, half):
        kept = jnp.exp2(trans[span(l, half), :])
        source = emit[half * GH : (half + 1) * GH, :] * warm[l : l + 1, :]
        added = source - kept * source
        trans[span(l, half), :] = kept
        glow[span(l, half), :] = added
        return kept, added, jnp.exp2(passing[span(l, half), :])

    def note(l, half, change):
        row = slice(8 * l, 8 * l + 8)
        sums[row, :] = sums[row, :] + change if half else change

    @pl.when(me == 0)
    def _():
        order = [(half, b) for half in range(2) for b in range(BLOCKS)]
        for half in range(2):
            part = slice(half * GH, (half + 1) * GH)
            thermal = jnp.zeros((GH, RAD), F32)
            direct = shine[part, :] * surface[7:8, :]
            above = fold(direct)
            for l in range(LEV):
                if l % BLOCK == 0:
                    ahead(order, half * BLOCKS + l // BLOCK)
                kept, added, passed = optics(l, half)
                thermal = kept * thermal + added
                direct = direct * passed
                below = fold(thermal + direct)
                note(l, half, above - below)
                above = below
            edge[part, :] = thermal
            edge[GALL + half * GH : GALL + (half + 1) * GH, :] = direct

    @pl.when(me == 1)
    def _():
        ground = jnp.square(jnp.square(surface[5:6, :]))
        order = [(half, BLOCKS - 1 - b) for half in range(2) for b in range(BLOCKS)]
        for half in range(2):
            part = slice(half * GH, (half + 1) * GH)
            upward = emit[part, :] * ground
            below = fold(upward)
            for l in range(LEV - 1, -1, -1):
                if l % BLOCK == BLOCK - 1:
                    ahead(order, half * BLOCKS + BLOCKS - 1 - l // BLOCK)
                kept, added, passed = optics(l, half)
                passing[span(l, half), :] = passed
                upward = kept * upward + added
                above = fold(upward)
                note(l, half, below - above)
                below = above
            edge[part, :] = upward
        edge[GALL:, :] = jnp.zeros((GALL, RAD), F32)


def second_kernel(side, gotten, trans, glow, passing, thick, sums, spread, send, net, slots):
    me = side[0]

    @pl.when(me == 0)
    def _():
        for half in range(2):
            upward = gotten[half * GH : (half + 1) * GH, :]
            below = fold(upward)
            for l in range(LEV - 1, -1, -1):
                upward = trans[span(l, half), :] * upward + glow[span(l, half), :]
                above = fold(upward)
                row = slice(8 * l, 8 * l + 8)
                net[row, :] = (net if half else sums)[row, :] + (below - above)
                below = above

    @pl.when(me == 1)
    def _():
        for half in range(2):
            thermal = gotten[half * GH : (half + 1) * GH, :]
            direct = gotten[GALL + half * GH : GALL + (half + 1) * GH, :]
            above = fold(thermal + direct)
            for l in range(LEV):
                thermal = trans[span(l, half), :] * thermal + glow[span(l, half), :]
                direct = direct * passing[span(l, half), :]
                below = fold(thermal + direct)
                row = slice(8 * l, 8 * l + 8)
                net[row, :] = (net if half else sums)[row, :] + (above - below)
                above = below

    total = None
    for k in range(8):
        part = net[pl.ds(k, LEV, 8), :]
        total = part if total is None else total + part
    heat = jnp.concatenate([total / thick[0:LEV, :], jnp.zeros((ROW - LEV, RAD), F32)], axis=0)
    gap = jnp.zeros((16, RAD), F32)
    hi, lo = split(jnp.concatenate([heat, gap, heat, gap], axis=0))
    slots[...] = dot(spread[...], hi, NT) + dot(spread[...], lo, NT)
    lanes = lax.broadcasted_iota(jnp.int32, (PEERS, RAD), 1)
    for h in range(2):
        even, odd = slots[pl.ds(2 * h, PEERS, SLOTS), :], slots[pl.ds(2 * h + 1, PEERS, SLOTS), :]
        send[pl.ds(h, PEERS, 2), :] = jnp.where(lanes < 64, even, odd)


def unplace_kernel(returned, placing, heating):
    parts = []
    for h in range(2):
        turned = returned[pl.ds(h, PEERS, 2), :].T
        parts += [turned[0:ROW, :], turned[64 : 64 + ROW, :]]
    hi, lo = split(jnp.concatenate(parts, axis=1))
    heating[...] = (dot(hi, placing[...], NN) + dot(lo, placing[...], NN))[0:LEV, :]


def mix_kernel(tracers, adj, coef, from_left, from_right, mixed, high, low, band, stage):
    spare = LEV * SPECIES
    stage[spare:BODY, :] = jnp.zeros((BODY - spare, COLS), F32)
    for l in range(LEV):
        stage[SPECIES * l : SPECIES * (l + 1), :] = tracers[l]
    parts = (from_left[0:BODY, :], stage[...], from_right[0:BODY, :])
    for part, start in zip(parts, (0, REACH, REACH + COLS)):
        hi, lo = split(part)
        high[0, :, start : start + part.shape[1]] = hi
        low[0, :, start : start + part.shape[1]] = lo
    tables = jnp.concatenate([from_left[BODY:, :], mixing_table(adj, coef), from_right[BODY:, :]], axis=1)
    shifted = pltpu.roll(tables, WIDE - HALO, 1)
    rows = lax.broadcasted_iota(jnp.int32, (256, 128), 0).astype(F32)
    lanes = lax.broadcasted_iota(jnp.int32, (1, 128), 1).astype(F32)

    def build(source, k):
        part = source[:, k * 128 : (k + 1) * 128]
        blend = jnp.where(rows == lanes + HALO, 1.0 - jnp.sum(part[8:14, :], axis=0, keepdims=True), 0.0)
        for n in range(NEAR):
            blend = blend + jnp.where(rows == lanes + part[n : n + 1, :], part[8 + n : 9 + n, :], 0.0)
        return split(blend)

    for k in range(7):
        hi, lo = build(shifted, k)
        band[0, 0, k] = hi
        band[0, 1, k] = lo
    for k in range(6):
        hi, lo = build(tables, k + 1)
        band[1, 0, k] = hi
        band[1, 1, k] = lo
    for step in range(STEPS):
        now, later = step % 2, (step + 1) % 2
        tiles = 7 - step
        first = step // 2
        for k in range(tiles):
            window = slice(k * 128, k * 128 + 256)
            bh, bl = band[now, 0, k + first], band[now, 1, k + first]
            xh, xl = high[now, :, window], low[now, :, window]
            new = dot(xh, bh, NN) + (dot(xh, bl, NN) + dot(xl, bh, NN))
            if step < STEPS - 1:
                hi, lo = split(new)
                high[later, :, k * 128 : (k + 1) * 128] = hi
                low[later, :, k * 128 : (k + 1) * 128] = lo
            else:
                for l in range(LEV):
                    mixed[l, :, k * 128 : (k + 1) * 128] = new[SPECIES * l : SPECIES * (l + 1), :]


def shape(*dims):
    return jax.ShapeDtypeStruct(dims, F32)


LENGTH = {"pack": 27, "edges": 4, "join": 5, "weight": 30, "mix": 42, "first": 20, "second": 9, "unplace": 10}


def call(kernel, name, out_shape, scratch, vmem_limit_bytes=16 << 20, **specs):
    return pl.pallas_call(
        kernel,
        out_shape=out_shape,
        scratch_shapes=scratch,
        compiler_params=pltpu.CompilerParams(vmem_limit_bytes=vmem_limit_bytes),
        cost_estimate=pl.CostEstimate(flops=LENGTH[name] * 10**8, bytes_accessed=1 << 18, transcendentals=0),
        **specs,
    )


def per_device(
    stratum_warmth_anomaly,
    pressure_depth,
    absorber_amounts,
    ground_warmth_anomaly,
    sun_elevation_factor,
    daytime_mask,
    dispatch_position,
    arrival_membership,
    adjacency_table,
    blending_coefficient,
    opacity_table,
    emission_share,
    sunshine_share,
):
    n = lax.axis_size("grp")
    up = [(i, (i + 1) % n) for i in range(n)]
    down = [(j, i) for i, j in up]
    swap = [(0, 1), (1, 0)]
    halo_rows = BODY + 16
    tracers = jnp.transpose(absorber_amounts, (1, 0, 2))

    hbm = pl.BlockSpec(memory_space=pltpu.HBM)
    packed = shape(PEERS * CHUNK, 128)
    given = ((LEV, COLS), (LEV, COLS), (LEV, SPECIES, COLS), (1, COLS), (1, COLS))
    send = call(
        pack_kernel,
        "pack",
        packed,
        [pltpu.VMEM(dims, F32) for dims in given]
        + [pltpu.VMEM((1, COLS), jnp.int32)] * 2
        + [pltpu.VMEM(packed.shape, F32)]
        + [pltpu.VMEM((FEAT, COLS), F32), pltpu.SemaphoreType.DMA((7,)), pltpu.SemaphoreType.DMA((2,))],
        in_specs=[hbm] * 7,
        out_specs=hbm,
        vmem_limit_bytes=60 << 20,
    )(
        stratum_warmth_anomaly,
        pressure_depth,
        tracers,
        ground_warmth_anomaly[None],
        sun_elevation_factor[None],
        daytime_mask[None],
        dispatch_position,
    )
    right, left = call(edge_kernel, "edges", (shape(halo_rows, REACH), shape(halo_rows, REACH)), [])(
        tracers, adjacency_table, blending_coefficient
    )
    from_left = lax.ppermute(right, "grp", up)
    from_right = lax.ppermute(left, "grp", down)
    arrived = lax.all_to_all(send.reshape(PEERS * CHUNK, 1, 128), "grp", split_axis=0, concat_axis=0, tiled=True)
    side = lax.axis_index("sec").astype(jnp.int32)[None]
    opacity = call(join_kernel, "join", shape(SPECIES, GH, 128), [])(
        opacity_table, emission_share[None], sunshine_share[None]
    )
    whole = pl.BlockSpec(memory_space=pltpu.VMEM)
    scalar = pl.BlockSpec(memory_space=pltpu.SMEM)
    weights, emit, shine, spread, placing = call(
        weight_kernel,
        "weight",
        (
            jax.ShapeDtypeStruct((DEEP, 128), BF),
            shape(GALL, RAD),
            shape(GALL, RAD),
            jax.ShapeDtypeStruct((COLS, RAD), BF),
            jax.ShapeDtypeStruct((COLS, COLS), BF),
        ),
        [pltpu.VMEM((2, SPECIES, GH, 128), F32)],
        in_specs=[scalar] + [whole] * 4,
    )(side, opacity, lax.ppermute(opacity, "sec", swap), arrival_membership, dispatch_position)
    arrived, weights, emit, shine, spread, placing, side = lax.optimization_barrier(
        (arrived, weights, emit, shine, spread, placing, side)
    )
    trans, glow, passing, thick, sums, edge = call(
        first_kernel,
        "first",
        (
            shape(DEEP, RAD),
            shape(DEEP, RAD),
            shape(DEEP, RAD),
            shape(ROW, RAD),
            shape(8 * LEV, RAD),
            shape(2 * GALL, RAD),
        ),
        [
            pltpu.VMEM((3, COLS, 128), F32),
            pltpu.VMEM((FEAT, RAD), F32),
            pltpu.VMEM((ROW, RAD), F32),
            pltpu.VMEM((2, BLOCKS * 128, RAD), BF),
        ],
        in_specs=[scalar] + [whole] * 5,
    )(side, arrived.reshape(PEERS * CHUNK, 128), arrival_membership, weights, emit, shine)
    gotten = lax.ppermute(edge, "sec", swap)
    back = call(
        second_kernel,
        "second",
        shape(PEERS * 2, 128),
        [pltpu.VMEM((8 * LEV, RAD), F32), pltpu.VMEM((COLS, RAD), F32)],
        in_specs=[scalar] + [whole] * 7,
    )(side, gotten, trans, glow, passing, thick, sums, spread)
    returned = lax.all_to_all(
        back.reshape(PEERS * 2, 1, 128), "grp", split_axis=0, concat_axis=0, tiled=True
    ).reshape(PEERS * 2, 128)
    mixed = call(
        mix_kernel,
        "mix",
        shape(LEV, SPECIES, COLS),
        [
            pltpu.VMEM((2, BODY, WIDE), BF),
            pltpu.VMEM((2, BODY, WIDE), BF),
            pltpu.VMEM((2, 2, 7, 256, 128), BF),
            pltpu.VMEM((BODY, COLS), F32),
        ],
    )(tracers, adjacency_table, blending_coefficient, from_left, from_right)
    returned, mixed = lax.optimization_barrier((returned, mixed))
    heating = call(unplace_kernel, "unplace", shape(LEV, COLS), [])(returned, placing)
    return (heating, jnp.transpose(mixed, (1, 0, 2)))


def solution(mesh):
    in_specs = (
        P("sec", "grp"),
        P("sec", "grp"),
        P(None, "sec", "grp"),
        P("grp"),
        P("grp"),
        P("grp"),
        P("grp", None),
        P("grp", None),
        P(None, "grp"),
        P(None, "grp"),
        P(None, "sec", None),
        P("sec"),
        P("sec"),
    )
    out_specs = (P("sec", "grp"), P(None, "sec", "grp"))
    return jax.shard_map(
        per_device, mesh=mesh, in_specs=in_specs, out_specs=out_specs, check_vma=False
    )
```

```python
import math

import jax
import jax.numpy as jnp
from jax import lax
from jax.experimental import pallas as pl
from jax.experimental.pallas import tpu as pltpu
from jax.sharding import PartitionSpec as P


STEPS = 4
HALO = 64
DIFFUSE = 1.66
LOG2E = math.log2(math.e)
BF = jnp.bfloat16
F32 = jnp.float32

PEERS = 128
SLOTS = 4
COLS = 512
LEV = 45
ROW = 48
BASE = 2 * ROW
BODY = 192
FEAT = BASE + BODY
CHUNK = SLOTS * FEAT // 128
RAD = 128
GH = 56
REACH = STEPS * HALO
WIDE = COLS + 2 * REACH
SPECIES = 4
NEAR = 6
BLOCK = 9
BLOCKS = LEV // BLOCK
GALL = 2 * GH
TALL = 512
DEEP = 2 * BLOCKS * TALL
PART = 40
NT = (((1,), (1,)), ((), ()))
NN = (((1,), (0,)), ((), ()))


def split(x):
    hi = x.astype(BF)
    return hi, (x - hi.astype(F32)).astype(BF)


def dot(a, b, dims):
    return lax.dot_general(a, b, dims, preferred_element_type=F32)


def slot_matrix(position):
    rows = lax.broadcasted_iota(jnp.int32, (COLS, COLS), 0)
    slot = (rows & (PEERS - 1)) * SLOTS + (rows >> 7)
    return jnp.where(slot == position, 1.0, 0.0).astype(BF)


def mixing_table(adj, coef):
    column = lax.broadcasted_iota(jnp.int32, (NEAR, COLS), 1)
    pad = jnp.zeros((2, COLS), F32)
    return jnp.concatenate([(adj[...] - column).astype(F32), pad, coef[...], pad], axis=0)


def pack_kernel(*refs):
    sources, outs, scratch = refs[:9], refs[9:12], refs[12:]
    temp, thick, tracers, ground, sun, day, pos, adj, coef = scratch[:9]
    send, right, left, bundle, sems, done = scratch[9:]
    copies = [pltpu.make_async_copy(a, b, sems.at[i]) for i, (a, b) in enumerate(zip(sources, scratch))]
    for i in (6, 7, 8, 2, 0, 1, 3, 4, 5):
        copies[i].start()
    middle = PEERS * CHUNK // 2
    pairs = [(send.at[0:middle, :], outs[0].at[0:middle, :]), (right, outs[1]), (left, outs[2])]
    pairs.append((send.at[middle : 2 * middle, :], outs[0].at[middle : 2 * middle, :]))
    stores = [pltpu.make_async_copy(a, b, done.at[i]) for i, (a, b) in enumerate(pairs)]
    bundle[ROW + LEV : BASE, :] = jnp.zeros((ROW - LEV, COLS), F32)
    spare = BASE + LEV * SPECIES
    bundle[spare:FEAT, :] = jnp.zeros((FEAT - spare, COLS), F32)
    for i in (6, 7, 8):
        copies[i].wait()
    placing = slot_matrix(pos[...])
    both = mixing_table(adj, coef)
    right[BODY : BODY + 16, :] = both[:, COLS - REACH :]
    left[BODY : BODY + 16, :] = both[:, :REACH]
    copies[2].wait()
    for l in range(LEV):
        bundle[BASE + SPECIES * l : BASE + SPECIES * (l + 1), :] = tracers[l]
    right[0:BODY, :] = bundle[BASE:FEAT, COLS - REACH :]
    left[0:BODY, :] = bundle[BASE:FEAT, :REACH]
    for i in (1, 2):
        stores[i].start()
    for i in (0, 1, 3, 4, 5):
        copies[i].wait()
    bundle[0:LEV, :] = temp[...]
    bundle[ROW : ROW + LEV, :] = thick[...]
    sunny = sun[...]
    bundle[LEV : LEV + 1, :] = ground[...]
    bundle[LEV + 1 : LEV + 2, :] = sunny
    bundle[LEV + 2 : LEV + 3, :] = day[...].astype(F32) * sunny
    hi, lo = split(bundle[0:256, :])
    packed = dot(placing, hi, NT) + dot(placing, lo, NT)
    tail = bundle[256:288, :]
    hi = tail.astype(BF).astype(F32)
    tails = dot(placing, jnp.concatenate([hi] * SLOTS + [tail - hi] * SLOTS, axis=0).astype(BF), NT)
    tails = tails[:, 0:128] + tails[:, 128:256]
    lane = lax.broadcasted_iota(jnp.int32, (PEERS, 128), 1) >> 5
    last = jnp.zeros((PEERS, 128), F32)
    for m in range(SLOTS):
        block = packed[m * PEERS : (m + 1) * PEERS, :]
        send[pl.ds(2 * m, PEERS, CHUNK), :] = block[:, 0:128]
        send[pl.ds(2 * m + 1, PEERS, CHUNK), :] = block[:, 128:256]
        last = jnp.where(lane == m, tails[m * PEERS : (m + 1) * PEERS, :], last)
    send[pl.ds(CHUNK - 1, PEERS, CHUNK), :] = last
    stores[0].start()
    stores[3].start()
    for store in stores:
        store.wait()


def join_kernel(opacity, emission, sunshine, joined):
    rows = lax.broadcasted_iota(jnp.int32, (GH, GH), 0)
    lanes = lax.broadcasted_iota(jnp.int32, (GH, GH), 1)
    for s in range(SPECIES):
        joined[s] = jnp.zeros((GH, 128), F32)
        joined[s, :, 0 : 2 * LEV] = opacity[s]
    for k, share in enumerate((emission, sunshine)):
        square = jnp.where(rows == lanes, jnp.broadcast_to(share[...], (GH, GH)), 0.0)
        joined[0, :, 2 * LEV + k : 2 * LEV + k + 1] = jnp.sum(square, axis=1, keepdims=True)


def weight_kernel(side, own, other, member, pos, weights, emit, shine, spread, placing, full):
    placing[...] = slot_matrix(pos[...])
    ids = (member[...] >> 2).astype(F32)
    spots = lax.broadcasted_iota(jnp.int32, (128, RAD), 1).astype(F32)
    for k in range(SLOTS):
        part = slice(k * 128, (k + 1) * 128)
        column = jnp.broadcast_to(ids[:, part], (128, 128)).T
        spread[part, :] = jnp.where(column == spots, 1.0, 0.0).astype(BF)
    me = side[0]
    full[pl.ds(me, 1)] = own[...][None]
    full[pl.ds(1 - me, 1)] = other[...][None]
    shift = lax.rem(128 - LEV * me, 128)
    tables = [jnp.concatenate([full[0, s], full[1, s]], axis=0) for s in range(SPECIES)]
    emit[...] = jnp.broadcast_to(tables[0][:, 2 * LEV : 2 * LEV + 1], (GALL, RAD))
    shine[...] = jnp.broadcast_to(tables[0][:, 2 * LEV + 1 : 2 * LEV + 2], (GALL, RAD))
    tables = [pltpu.roll(table, shift, 1) for table in tables]
    rows = lax.broadcasted_iota(jnp.int32, (128, 128), 0)
    lanes = lax.broadcasted_iota(jnp.int32, (128, 128), 1)
    picks = []
    for s in range(SPECIES):
        lane = jnp.where(rows < BLOCK, SPECIES * rows + s, -1)
        picks.append((lanes == lane) | (lanes == jnp.where(lane < 0, -1, lane + 2 * PART)))
    for s in range(SPECIES):
        lane = jnp.where(rows < BLOCK, SPECIES * rows + s + PART, -1)
        picks.append(lanes == lane)
    picker = jnp.concatenate([jnp.where(p, 1.0, 0.0).astype(BF) for p in picks], axis=0)
    group = lax.broadcasted_iota(jnp.int32, (GH, 128), 1)
    group = jnp.where(group >= 2 * PART, group - 2 * PART, jnp.where(group >= PART, group - PART, group)) >> 2
    pad = jnp.zeros((TALL - BLOCK * GH, 128), F32)
    for b in range(BLOCKS):
        his, los = [], []
        for table in tables:
            hi, lo = split(pltpu.roll(table, 128 - b * BLOCK, 1) if b else table)
            his.append(hi)
            los.append(lo)
        wide = dot(jnp.concatenate(his + los, axis=1), picker, NN)
        for half in range(2):
            part = wide[half * GH : (half + 1) * GH, :]
            block = jnp.concatenate([jnp.where(group == i, part, 0.0) for i in range(BLOCK)] + [pad], axis=0)
            start = (half * BLOCKS + b) * TALL
            weights[start : start + TALL, :] = block.astype(BF)


def fold(x):
    return jnp.sum(x.reshape(GH // 8, 8, RAD), axis=0)


def span(level, half):
    start = (half * BLOCKS + level // BLOCK) * TALL + level % BLOCK * GH
    return slice(start, start + GH)


def first_kernel(side, arrived, member, weights, emit, shine, trans, glow, passing, thick, sums, edge, stage, pooled, warm, amounts):
    lane = lax.broadcasted_iota(jnp.int32, (PEERS, 128), 1) >> 5
    last = arrived[pl.ds(CHUNK - 1, PEERS, CHUNK), :]
    for m in range(SLOTS):
        part = pl.ds(m, PEERS, SLOTS)
        stage[0, part, :] = arrived[pl.ds(2 * m, PEERS, CHUNK), :]
        stage[1, part, :] = arrived[pl.ds(2 * m + 1, PEERS, CHUNK), :]
        stage[2, part, :] = jnp.where(lane == m, last, 0.0)
    rows = lax.broadcasted_iota(jnp.int32, (RAD, COLS), 0)
    selector = jnp.where(rows == member[...] >> 2, 0.25, 0.0).astype(BF)
    hi, lo = split(jnp.concatenate([stage[k] for k in range(3)], axis=1))
    total = dot(selector, hi, NN) + dot(selector, lo, NN)
    pooled[0:128, :] = total[:, 0:128].T
    pooled[128:256, :] = total[:, 128:256].T
    tail = total[:, 256:384].T
    pooled[256:288, :] = tail[0:32] + tail[32:64] + tail[64:96] + tail[96:128]
    surface = pooled[40:48, :]
    slant = 1.0 / (DIFFUSE * surface[6:7, :])
    warm[...] = jnp.square(jnp.square(pooled[0:ROW, :]))
    thick[...] = pooled[ROW:BASE, :]
    pooled[BASE:FEAT, :] = pooled[BASE:FEAT, :] * (-DIFFUSE * LOG2E)
    pad = jnp.zeros((128 - 3 * PART, RAD), F32)
    for b in range(BLOCKS):
        start = BASE + SPECIES * BLOCK * b
        part = pooled[start : start + PART, :]
        for k, values in enumerate((part, part * slant)):
            hi = values.astype(BF).astype(F32)
            mixture = jnp.concatenate([hi, hi, values - hi, pad], axis=0).astype(BF)
            amounts[k, b * 128 : (b + 1) * 128, :] = mixture

    def depths(half, b):
        rows = slice((half * BLOCKS + b) * TALL, (half * BLOCKS + b + 1) * TALL)
        for k, exponent in enumerate((trans, passing)):
            exponent[rows, :] = dot(weights[rows, :], amounts[k, b * 128 : (b + 1) * 128, :], NN)

    def ahead(order, place):
        if place == 0:
            depths(*order[0])
        if place + 1 < len(order):
            depths(*order[place + 1])

    me = side[0]

    def optics(l, half):
        kept = jnp.exp2(trans[span(l, half), :])
        source = emit[half * GH : (half + 1) * GH, :] * warm[l : l + 1, :]
        added = source - kept * source
        trans[span(l, half), :] = kept
        glow[span(l, half), :] = added
        return kept, added, jnp.exp2(passing[span(l, half), :])

    def note(l, half, change):
        row = slice(8 * l, 8 * l + 8)
        sums[row, :] = sums[row, :] + change if half else change

    @pl.when(me == 0)
    def _():
        order = [(half, b) for half in range(2) for b in range(BLOCKS)]
        for half in range(2):
            part = slice(half * GH, (half + 1) * GH)
            thermal = jnp.zeros((GH, RAD), F32)
            direct = shine[part, :] * surface[7:8, :]
            above = fold(direct)
            for l in range(LEV):
                if l % BLOCK == 0:
                    ahead(order, half * BLOCKS + l // BLOCK)
                kept, added, passed = optics(l, half)
                thermal = kept * thermal + added
                direct = direct * passed
                below = fold(thermal + direct)
                note(l, half, above - below)
                above = below
            edge[part, :] = thermal
            edge[GALL + half * GH : GALL + (half + 1) * GH, :] = direct

    @pl.when(me == 1)
    def _():
        ground = jnp.square(jnp.square(surface[5:6, :]))
        order = [(half, BLOCKS - 1 - b) for half in range(2) for b in range(BLOCKS)]
        for half in range(2):
            part = slice(half * GH, (half + 1) * GH)
            upward = emit[part, :] * ground
            below = fold(upward)
            for l in range(LEV - 1, -1, -1):
                if l % BLOCK == BLOCK - 1:
                    ahead(order, half * BLOCKS + BLOCKS - 1 - l // BLOCK)
                kept, added, passed = optics(l, half)
                passing[span(l, half), :] = passed
                upward = kept * upward + added
                above = fold(upward)
                note(l, half, below - above)
                below = above
            edge[part, :] = upward
        edge[GALL:, :] = jnp.zeros((GALL, RAD), F32)


def second_kernel(side, gotten, trans, glow, passing, thick, sums, spread, send, net, slots):
    me = side[0]

    @pl.when(me == 0)
    def _():
        for half in range(2):
            upward = gotten[half * GH : (half + 1) * GH, :]
            below = fold(upward)
            for l in range(LEV - 1, -1, -1):
                upward = trans[span(l, half), :] * upward + glow[span(l, half), :]
                above = fold(upward)
                row = slice(8 * l, 8 * l + 8)
                net[row, :] = (net if half else sums)[row, :] + (below - above)
                below = above

    @pl.when(me == 1)
    def _():
        for half in range(2):
            thermal = gotten[half * GH : (half + 1) * GH, :]
            direct = gotten[GALL + half * GH : GALL + (half + 1) * GH, :]
            above = fold(thermal + direct)
            for l in range(LEV):
                thermal = trans[span(l, half), :] * thermal + glow[span(l, half), :]
                direct = direct * passing[span(l, half), :]
                below = fold(thermal + direct)
                row = slice(8 * l, 8 * l + 8)
                net[row, :] = (net if half else sums)[row, :] + (above - below)
                above = below

    total = None
    for k in range(8):
        part = net[pl.ds(k, LEV, 8), :]
        total = part if total is None else total + part
    heat = jnp.concatenate([total / thick[0:LEV, :], jnp.zeros((ROW - LEV, RAD), F32)], axis=0)
    gap = jnp.zeros((16, RAD), F32)
    hi, lo = split(jnp.concatenate([heat, gap, heat, gap], axis=0))
    slots[...] = dot(spread[...], hi, NT) + dot(spread[...], lo, NT)
    lanes = lax.broadcasted_iota(jnp.int32, (PEERS, RAD), 1)
    for h in range(2):
        even, odd = slots[pl.ds(2 * h, PEERS, SLOTS), :], slots[pl.ds(2 * h + 1, PEERS, SLOTS), :]
        send[pl.ds(h, PEERS, 2), :] = jnp.where(lanes < 64, even, odd)


def unplace_kernel(returned, placing, heating):
    parts = []
    for h in range(2):
        turned = returned[pl.ds(h, PEERS, 2), :].T
        parts += [turned[0:ROW, :], turned[64 : 64 + ROW, :]]
    hi, lo = split(jnp.concatenate(parts, axis=1))
    heating[...] = (dot(hi, placing[...], NN) + dot(lo, placing[...], NN))[0:LEV, :]


def mix_kernel(tracers, adj, coef, from_left, from_right, mixed, high, low, band, stage):
    spare = LEV * SPECIES
    stage[spare:BODY, :] = jnp.zeros((BODY - spare, COLS), F32)
    for l in range(LEV):
        stage[SPECIES * l : SPECIES * (l + 1), :] = tracers[l]
    parts = (from_left[0:BODY, :], stage[...], from_right[0:BODY, :])
    for part, start in zip(parts, (0, REACH, REACH + COLS)):
        hi, lo = split(part)
        high[0, :, start : start + part.shape[1]] = hi
        low[0, :, start : start + part.shape[1]] = lo
    tables = jnp.concatenate([from_left[BODY:, :], mixing_table(adj, coef), from_right[BODY:, :]], axis=1)
    shifted = pltpu.roll(tables, WIDE - HALO, 1)
    rows = lax.broadcasted_iota(jnp.int32, (256, 128), 0).astype(F32)
    lanes = lax.broadcasted_iota(jnp.int32, (1, 128), 1).astype(F32)

    def build(source, k):
        part = source[:, k * 128 : (k + 1) * 128]
        blend = jnp.where(rows == lanes + HALO, 1.0 - jnp.sum(part[8:14, :], axis=0, keepdims=True), 0.0)
        for n in range(NEAR):
            blend = blend + jnp.where(rows == lanes + part[n : n + 1, :], part[8 + n : 9 + n, :], 0.0)
        return split(blend)

    for k in range(7):
        hi, lo = build(shifted, k)
        band[0, 0, k] = hi
        band[0, 1, k] = lo
    for k in range(6):
        hi, lo = build(tables, k + 1)
        band[1, 0, k] = hi
        band[1, 1, k] = lo
    for step in range(STEPS):
        now, later = step % 2, (step + 1) % 2
        tiles = 7 - step
        first = step // 2
        for k in range(tiles):
            window = slice(k * 128, k * 128 + 256)
            bh, bl = band[now, 0, k + first], band[now, 1, k + first]
            xh, xl = high[now, :, window], low[now, :, window]
            new = dot(xh, bh, NN) + (dot(xh, bl, NN) + dot(xl, bh, NN))
            if step < STEPS - 1:
                hi, lo = split(new)
                high[later, :, k * 128 : (k + 1) * 128] = hi
                low[later, :, k * 128 : (k + 1) * 128] = lo
            else:
                for l in range(LEV):
                    mixed[l, :, k * 128 : (k + 1) * 128] = new[SPECIES * l : SPECIES * (l + 1), :]


def shape(*dims):
    return jax.ShapeDtypeStruct(dims, F32)


LENGTH = {"pack": 27, "join": 5, "weight": 7, "mix": 42, "first": 20, "second": 9, "unplace": 10}


def call(kernel, name, out_shape, scratch, vmem_limit_bytes=16 << 20, **specs):
    return pl.pallas_call(
        kernel,
        out_shape=out_shape,
        scratch_shapes=scratch,
        compiler_params=pltpu.CompilerParams(vmem_limit_bytes=vmem_limit_bytes),
        cost_estimate=pl.CostEstimate(flops=LENGTH[name] * 10**8, bytes_accessed=1 << 18, transcendentals=0),
        **specs,
    )


def per_device(
    stratum_warmth_anomaly,
    pressure_depth,
    absorber_amounts,
    ground_warmth_anomaly,
    sun_elevation_factor,
    daytime_mask,
    dispatch_position,
    arrival_membership,
    adjacency_table,
    blending_coefficient,
    opacity_table,
    emission_share,
    sunshine_share,
):
    n = lax.axis_size("grp")
    up = [(i, (i + 1) % n) for i in range(n)]
    down = [(j, i) for i, j in up]
    swap = [(0, 1), (1, 0)]
    halo_rows = BODY + 16
    tracers = jnp.transpose(absorber_amounts, (1, 0, 2))

    hbm = pl.BlockSpec(memory_space=pltpu.HBM)
    packed = (shape(PEERS * CHUNK, 128), shape(halo_rows, REACH), shape(halo_rows, REACH))
    given = ((LEV, COLS), (LEV, COLS), (LEV, SPECIES, COLS), (1, COLS), (1, COLS))
    send, right, left = call(
        pack_kernel,
        "pack",
        packed,
        [pltpu.VMEM(dims, F32) for dims in given]
        + [pltpu.VMEM((rows, COLS), jnp.int32) for rows in (1, 1, NEAR)]
        + [pltpu.VMEM((NEAR, COLS), F32)]
        + [pltpu.VMEM(out.shape, F32) for out in packed]
        + [pltpu.VMEM((FEAT, COLS), F32), pltpu.SemaphoreType.DMA((9,)), pltpu.SemaphoreType.DMA((4,))],
        in_specs=[hbm] * 9,
        out_specs=[hbm] * 3,
        vmem_limit_bytes=60 << 20,
    )(
        stratum_warmth_anomaly,
        pressure_depth,
        tracers,
        ground_warmth_anomaly[None],
        sun_elevation_factor[None],
        daytime_mask[None],
        dispatch_position,
        adjacency_table,
        blending_coefficient,
    )
    from_left = lax.ppermute(right, "grp", up)
    from_right = lax.ppermute(left, "grp", down)
    arrived = lax.all_to_all(
        send.reshape(PEERS * CHUNK, 1, 128), "grp", split_axis=0, concat_axis=0, tiled=True
    )
    side = lax.axis_index("sec").astype(jnp.int32)[None]
    opacity = call(join_kernel, "join", shape(SPECIES, GH, 128), [])(
        opacity_table, emission_share[None], sunshine_share[None]
    )
    whole = pl.BlockSpec(memory_space=pltpu.VMEM)
    scalar = pl.BlockSpec(memory_space=pltpu.SMEM)
    weights, emit, shine, spread, placing = call(
        weight_kernel,
        "weight",
        (
            jax.ShapeDtypeStruct((DEEP, 128), BF),
            shape(GALL, RAD),
            shape(GALL, RAD),
            jax.ShapeDtypeStruct((COLS, RAD), BF),
            jax.ShapeDtypeStruct((COLS, COLS), BF),
        ),
        [pltpu.VMEM((2, SPECIES, GH, 128), F32)],
        in_specs=[scalar] + [whole] * 4,
    )(side, opacity, lax.ppermute(opacity, "sec", swap), arrival_membership, dispatch_position)
    arrived, weights, emit, shine, spread, placing, side = lax.optimization_barrier(
        (arrived, weights, emit, shine, spread, placing, side)
    )
    trans, glow, passing, thick, sums, edge = call(
        first_kernel,
        "first",
        (
            shape(DEEP, RAD),
            shape(DEEP, RAD),
            shape(DEEP, RAD),
            shape(ROW, RAD),
            shape(8 * LEV, RAD),
            shape(2 * GALL, RAD),
        ),
        [
            pltpu.VMEM((3, COLS, 128), F32),
            pltpu.VMEM((FEAT, RAD), F32),
            pltpu.VMEM((ROW, RAD), F32),
            pltpu.VMEM((2, BLOCKS * 128, RAD), BF),
        ],
        in_specs=[scalar] + [whole] * 5,
    )(side, arrived.reshape(PEERS * CHUNK, 128), arrival_membership, weights, emit, shine)
    gotten = lax.ppermute(edge, "sec", swap)
    back = call(
        second_kernel,
        "second",
        shape(PEERS * 2, 128),
        [pltpu.VMEM((8 * LEV, RAD), F32), pltpu.VMEM((COLS, RAD), F32)],
        in_specs=[scalar] + [whole] * 7,
    )(side, gotten, trans, glow, passing, thick, sums, spread)
    returned = lax.all_to_all(
        back.reshape(PEERS * 2, 1, 128), "grp", split_axis=0, concat_axis=0, tiled=True
    ).reshape(PEERS * 2, 128)
    mixed = call(
        mix_kernel,
        "mix",
        shape(LEV, SPECIES, COLS),
        [
            pltpu.VMEM((2, BODY, WIDE), BF),
            pltpu.VMEM((2, BODY, WIDE), BF),
            pltpu.VMEM((2, 2, 7, 256, 128), BF),
            pltpu.VMEM((BODY, COLS), F32),
        ],
    )(tracers, adjacency_table, blending_coefficient, from_left, from_right)
    returned, mixed = lax.optimization_barrier((returned, mixed))
    heating = call(unplace_kernel, "unplace", shape(LEV, COLS), [])(returned, placing)
    return (heating, jnp.transpose(mixed, (1, 0, 2)))


def solution(mesh):
    in_specs = (
        P("sec", "grp"),
        P("sec", "grp"),
        P(None, "sec", "grp"),
        P("grp"),
        P("grp"),
        P("grp"),
        P("grp", None),
        P("grp", None),
        P(None, "grp"),
        P(None, "grp"),
        P(None, "sec", None),
        P("sec"),
        P("sec"),
    )
    out_specs = (P("sec", "grp"), P(None, "sec", "grp"))
    return jax.shard_map(
        per_device, mesh=mesh, in_specs=in_specs, out_specs=out_specs, check_vma=False
    )
```
